128 devices in a mesh: gx: 16 (over x, y), yz: 8 (over z, core).
Axes of the slice: x: 4, y: 4, z: 4, core: 2. Of those that a mesh axis runs over, the one named last changes fastest.
Arguments:
- populations: bfloat16 [19, 256, 256, 128], P(None, 'gx', 'yz'), may hold values from -0.29882812 to 0.29882812
- levels: int32 [2048], replicated, may hold values from 0 to 1
- refine_flags: int32 [2048], replicated, may hold values from 0 to 2, as said below
- new_owner: int32 [2048], replicated, may hold values from 0 to 127, as said below
Outputs:
- migrated: bfloat16 [3072, 19, 4096], P(('gx', 'yz'))
The draws below stay inside these ranges and needn't reach their ends.
Inputs may be any that keep to these rules, and one draw needn't show every extreme that they name: On every device exactly 8 of the blocks it holds have refine_flags 1 or 2; all other blocks have 0. `new_owner`: A block with refine_flags 0 keeps the device that holds it. No device receives more than one flagged block from any one device, itself included. After migration a quarter of the devices hold exactly 24 blocks, a quarter exactly 16, and the rest exactly 16 minus half of 8.
All inputs are finite; a program needn't handle non-finite values.
Results may differ from the reference program's by a relative error of at most 0.0049.
Values may be sent and summed in bfloat16 or wider, within the bound.
No kernel may reach another device: no remote copies, remote signals or barrier semaphores. Data moves between devices by JAX's collectives and lax.ppermute only.
A program may use at most 192 MiB of HBM per device.

```python
import jax
import jax.numpy as jnp
from jax import lax

BS = 16
HALF = 8
BX = 1
BY = 2
BZ = 8
MIG = 8
STEPS = 2
BLK = 16
CAP = 24
CX = 16
NX = 256
NY = 256
NZ = 128
NBLOCKS = 2048
N_GX = 16
N_YZ = 8
DEVICES = 128


def migration_plan(key):
    plan_key = jax.random.fold_in(key, 17)
    key_rank, key_kind, key_load, key_source = jax.random.split(plan_key, 4)
    scores = jax.random.randint(key_rank, (DEVICES, BLK), 0, 1 << 20) * BLK + jnp.arange(BLK, dtype=jnp.int32)[None, :]
    block_ranks = jnp.argsort(jnp.argsort(scores, axis=1), axis=1).astype(jnp.int32)
    flag_kinds = 1 + jax.random.randint(key_kind, (DEVICES, BLK), 0, 2)
    flagged = block_ranks < MIG
    labels = jax.random.permutation(key_load, DEVICES).astype(jnp.int32)
    arrival_loads = jnp.where(labels < DEVICES // 4, 2 * MIG, jnp.where(labels < DEVICES // 2, MIG, MIG // 2))
    starts = jnp.cumsum(arrival_loads) - arrival_loads
    residues = jax.random.permutation(key_source, DEVICES).astype(jnp.int32)
    positions = residues[:, None] + block_ranks * DEVICES
    targets = jnp.sum((starts[None, None, :] <= positions[:, :, None]).astype(jnp.int32), axis=2) - 1
    owners = jnp.where(flagged, targets, jnp.arange(DEVICES, dtype=jnp.int32)[:, None])
    kind_map = jnp.where(flagged, flag_kinds, 0)

    def global_order(per_device):
        arranged = per_device.reshape(N_GX, N_YZ, BX, BY, BZ)
        return jnp.transpose(arranged, (0, 2, 1, 3, 4)).reshape(-1).astype(jnp.int32)
    return (global_order(kind_map), global_order(owners))


def draw_refine_flags(key, part):
    return migration_plan(key)[0]


def draw_new_owner(key, part):
    return migration_plan(key)[1]


def set_ends(drawn, stream_key, low, top_value):
    longest = drawn.shape.index(max(drawn.shape))
    spots = []
    for shift in (0, 1):
        where = [jax.random.randint(jax.random.fold_in(stream_key, axis), (), 0, length) for axis, length in enumerate(drawn.shape)]
        where[longest] = (where[longest] + shift) % drawn.shape[longest]
        spots.append(tuple(where))
    return drawn.at[spots[0]].set(low).at[spots[1]].set(top_value)


def block_scale(rng, shape, shards, low, high):
    gain, own = 1.0, jax.random.fold_in(rng, 6)
    for position, blocks in shards:
        draws = jnp.exp(jax.random.uniform(jax.random.fold_in(own, position), (blocks,), jnp.float32, low / len(shards), high / len(shards)))
        gain = gain * jnp.repeat(draws, shape[position] // blocks).reshape([-1 if axis == position else 1 for axis in range(len(shape))])
    return gain


def setup_inputs(seed: int = 0) -> dict:
    seeds = jax.random.split(jax.random.key(seed), 5)
    populations = jnp.clip(jax.random.uniform(seeds[0], (19, NX, NY, NZ), jnp.float32, -0.29882812, 0.29882812) * block_scale(seeds[0], (19, NX, NY, NZ), ((1, 16), (2, 8)), -0.4, 0.0), -0.29882812, 0.29882812).astype(jnp.bfloat16)
    levels = set_ends(jax.random.randint(seeds[1], (NBLOCKS,), 0, 2), jax.random.fold_in(seeds[1], 1), 0, 1).astype(jnp.int32)
    refine_flags = draw_refine_flags(jax.random.fold_in(seeds[4], 71), 0)
    new_owner = draw_new_owner(jax.random.fold_in(seeds[4], 71), 0)
    return dict(populations=populations, levels=levels, refine_flags=refine_flags, new_owner=new_owner)


VELOCITY_LIST = [[0, 0, 0], [1, 0, 0], [-1, 0, 0], [0, 1, 0], [0, -1, 0], [0, 0, 1], [0, 0, -1],
                 [1, 1, 0], [-1, -1, 0], [1, -1, 0], [-1, 1, 0], [1, 0, 1], [-1, 0, -1],
                 [1, 0, -1], [-1, 0, 1], [0, 1, 1], [0, -1, -1], [0, 1, -1], [0, -1, 1]]
WEIGHT_LIST = [1.0 / 3.0] + [1.0 / 18.0] * 6 + [1.0 / 36.0] * 12
OPPOSITE_LIST = [0, 2, 1, 4, 3, 6, 5, 8, 7, 10, 9, 12, 11, 14, 13, 16, 15, 18, 17]


def relax_rates(levels):
    return 1.0 / (0.5 + jnp.power(0.5, levels.astype(jnp.float32)))


def collide(current, relax_field):
    values = current.astype(jnp.float32)
    weights = jnp.asarray(WEIGHT_LIST, jnp.float32).reshape((19,) + (1,) * (values.ndim - 1))
    speeds = jnp.asarray(VELOCITY_LIST, jnp.float32)
    weighted = values * weights
    density = 1.0 + jnp.sum(weighted, axis=0)
    momentum = jnp.einsum("ic,i...->c...", speeds, weighted, precision=lax.Precision.HIGHEST)
    velocity = momentum / density
    speed_square = jnp.sum(velocity * velocity, axis=0)
    project = jnp.einsum("ic,c...->i...", speeds, velocity, precision=lax.Precision.HIGHEST)
    balance = density * (1.0 + 3.0 * project + 4.5 * project * project - 1.5 * speed_square) - 1.0
    return values - relax_field * (values - balance)


def propagate(collided):
    cells_pipe = collided.shape[1] - 2
    cells_cross = collided.shape[2] - 2
    interior = collided[:, 1:-1, 1:-1, :]
    results = []
    for direction in range(19):
        delta_first, delta_second, delta_third = VELOCITY_LIST[direction]
        shifted = collided[direction, 1 - delta_first:1 - delta_first + cells_pipe,
                           1 - delta_second:1 - delta_second + cells_cross, :]
        mirror = interior[OPPOSITE_LIST[direction]]
        if delta_third == 1:
            shifted = jnp.concatenate([mirror[:, :, :1], shifted[:, :, :-1]], axis=2)
        elif delta_third == -1:
            shifted = jnp.concatenate([shifted[:, :, 1:], mirror[:, :, -1:]], axis=2)
        results.append(shifted)
    return jnp.stack(results).astype(jnp.bfloat16)


def restrict(blocks):
    count = blocks.shape[0]
    values = blocks.astype(jnp.float32).reshape(count, 19, HALF, 2, HALF, 2, HALF, 2)
    return (jnp.sum(values, axis=(3, 5, 7)) * 0.125).reshape(count, 19, HALF * HALF * HALF).astype(jnp.bfloat16)


def prolong(coarse, flag_kinds):
    count = coarse.shape[0]
    fine_index = jnp.arange(BS, dtype=jnp.int32)
    parent = fine_index // 2
    neighbor_index = jnp.clip(jnp.where(fine_index % 2 == 0, parent - 1, parent + 1), 0, HALF - 1)
    coarse_index = jnp.arange(HALF, dtype=jnp.int32)
    inject = (parent[:, None] == coarse_index[None, :]).astype(jnp.float32)
    linear = 0.75 * inject + 0.25 * (neighbor_index[:, None] == coarse_index[None, :]).astype(jnp.float32)
    matrices = jnp.where((flag_kinds == 2)[:, None, None], linear[None], inject[None])
    values = coarse.astype(jnp.float32).reshape(count, 19, HALF, HALF, HALF)
    values = jnp.einsum("nah,nphij->npaij", matrices, values, precision=lax.Precision.HIGHEST)
    values = jnp.einsum("nbi,npaij->npabj", matrices, values, precision=lax.Precision.HIGHEST)
    values = jnp.einsum("ncj,npabj->npabc", matrices, values, precision=lax.Precision.HIGHEST)
    return values.reshape(count, 19, BS * BS * BS).astype(jnp.bfloat16)


def reference(populations, levels, refine_flags, new_owner):
    block_rates = relax_rates(levels).reshape(NX // BS, NY // BS, NZ // BS)
    relax_field = jnp.repeat(jnp.repeat(jnp.repeat(block_rates, BS, 0), BS, 1), BS, 2)
    padded_rates = jnp.pad(relax_field, ((1, 1), (1, 1), (0, 0)), mode="wrap")
    current = populations
    for sweep_number in range(STEPS):
        padded = jnp.pad(current, ((0, 0), (1, 1), (1, 1), (0, 0)), mode="wrap")

        def slab_step(offset):
            slab_piece = lax.dynamic_slice_in_dim(padded, offset, CX + 2, 1)
            rates_piece = lax.dynamic_slice_in_dim(padded_rates, offset, CX + 2, 0)
            return propagate(collide(slab_piece, rates_piece))

        slab_results = lax.map(slab_step, jnp.arange(N_GX, dtype=jnp.int32) * CX)
        current = jnp.transpose(slab_results, (1, 0, 2, 3, 4)).reshape(19, NX, NY, NZ)
    blocks = current.reshape(19, NX // BS, BS, NY // BS, BS, NZ // BS, BS)
    blocks = jnp.transpose(blocks, (1, 3, 5, 0, 2, 4, 6)).reshape(NBLOCKS, 19, BS * BS * BS)
    flagged_ids = jnp.nonzero(refine_flags != 0, size=MIG * DEVICES, fill_value=0)[0].astype(jnp.int32)

    def refine_group(block_ids):
        chosen = jnp.take(blocks, block_ids, axis=0)
        return prolong(restrict(chosen), jnp.take(refine_flags, block_ids))

    refined = lax.map(refine_group, flagged_ids.reshape(DEVICES, MIG)).reshape(DEVICES * MIG, 19, BS * BS * BS)
    blocks = blocks.at[flagged_ids].set(refined)
    block_pool = jnp.concatenate([blocks, jnp.zeros((1, 19, BS * BS * BS), jnp.bfloat16)], axis=0)

    def gather_owned(device):
        owned_ids = jnp.nonzero(new_owner == device, size=CAP, fill_value=NBLOCKS)[0].astype(jnp.int32)
        return jnp.take(block_pool, owned_ids, axis=0)

    migrated = lax.map(gather_owned, jnp.arange(DEVICES, dtype=jnp.int32))
    return migrated.reshape(DEVICES * CAP, 19, BS * BS * BS)
```

```python
import functools

import jax
import jax.numpy as jnp
import numpy as np
from jax import lax
from jax.experimental import pallas as pl
from jax.experimental.pallas import tpu as pltpu
from jax.sharding import PartitionSpec as P

BS = 16
BZ = 8
CAP = 24
BLK = 16
ROWS = 48
MAXIN = 16
F32 = jnp.float32
BF16 = jnp.bfloat16

VEL = [
    (0, 0, 0),
    (1, 0, 0), (-1, 0, 0), (0, 1, 0), (0, -1, 0), (0, 0, 1), (0, 0, -1),
    (1, 1, 0), (-1, -1, 0), (1, -1, 0), (-1, 1, 0),
    (1, 0, 1), (-1, 0, -1), (1, 0, -1), (-1, 0, 1),
    (0, 1, 1), (0, -1, -1), (0, 1, -1), (0, -1, 1),
]
OPP = [0, 2, 1, 4, 3, 6, 5, 8, 7, 10, 9, 12, 11, 14, 13, 16, 15, 18, 17]
PLUS = [i for i in range(19) if VEL[i][0] == 1]
MINUS = [i for i in range(19) if VEL[i][0] == -1]
FLAT = [i for i in range(19) if VEL[i][0] == 0]
RIGHTWARD = [(i, 2) for i in PLUS] + [(i, 1) for i in PLUS + FLAT + [12, 14]]
LEFTWARD = [(i, 2) for i in MINUS] + [(i, 1) for i in MINUS + FLAT + [11, 13]]
FACES = len(RIGHTWARD)
FROWS = 40
HALO_Y = ((0, 32), (1, 33), (6, -2), (7, -1))


def collide(h, r):
    p = {}
    d = {}
    for a in range(1, 19, 2):
        p[a] = h[a] + h[a + 1]
        d[a] = h[a] - h[a + 1]
    axis = p[1] + p[3] + p[5]
    diag = (p[7] + p[9]) + (p[11] + p[13]) + (p[15] + p[17])
    rho = 1.0 + (h[0] * (1.0 / 3.0) + axis * (1.0 / 18.0) + diag * (1.0 / 36.0))
    mx = (2.0 * d[1] + (d[7] + d[9]) + (d[11] + d[13])) * (1.0 / 36.0)
    my = (2.0 * d[3] + (d[7] - d[9]) + (d[15] + d[17])) * (1.0 / 36.0)
    mz = (2.0 * d[5] + (d[11] - d[13]) + (d[15] - d[17])) * (1.0 / 36.0)
    inv = 1.0 / rho
    ux, uy, uz = mx * inv, my * inv, mz * inv
    square = ux * ux + uy * uy + uz * uz
    keep = 1.0 - r
    base = r * (rho * (1.0 - 1.5 * square) - 1.0)
    quad = (4.5 * r) * rho
    lin = (3.0 * r) * rho
    proj = {
        1: ux, 3: uy, 5: uz, 7: ux + uy, 9: ux - uy, 11: ux + uz, 13: ux - uz, 15: uy + uz, 17: uy - uz,
    }
    out = [keep * h[0] + base] + [None] * 18
    for a in range(1, 19, 2):
        even = base + quad * (proj[a] * proj[a])
        odd = lin * proj[a]
        out[a] = keep * h[a] + (even + odd)
        out[a + 1] = keep * h[a + 1] + (even - odd)
    return out


def plan_kernel(owner_ref, owned_ref, part):
    me = lax.axis_index("gx") * lax.axis_size("yz") + lax.axis_index("yz")
    rows = owner_ref.shape[0]
    mine = owner_ref[...] == me
    mask = jnp.where(mine, 1.0, 0.0)
    upper = lax.broadcasted_iota(jnp.int32, (128, 128), 0) <= lax.broadcasted_iota(jnp.int32, (128, 128), 1)
    before = lax.broadcasted_iota(jnp.int32, (rows, rows), 1) < lax.broadcasted_iota(jnp.int32, (rows, rows), 0)
    prefix = jnp.dot(mask.astype(BF16), jnp.where(upper, 1.0, 0.0).astype(BF16), preferred_element_type=F32)
    total = jnp.sum(mask, axis=1, keepdims=True)
    total = jnp.broadcast_to(total, (rows, 128))
    offset = jnp.dot(jnp.where(before, 1.0, 0.0).astype(BF16), total.astype(BF16), preferred_element_type=F32)
    rank = prefix + offset
    ids = lax.broadcasted_iota(jnp.int32, (rows, 128), 0) * 128 + lax.broadcasted_iota(jnp.int32, (rows, 128), 1)
    marked = jnp.where(mine, ids.astype(F32) + 1.0, 0.0)
    part[...] = jnp.zeros_like(part)
    for slot in range(CAP):
        hit = jnp.where(rank == float(slot + 1), marked, 0.0)
        part[slot : slot + 1, :] = jnp.sum(hit, axis=0, keepdims=True)
    found = jnp.sum(part[...], axis=1, keepdims=True) - 1.0
    owned_ref[...] = jnp.broadcast_to(found, part.shape).astype(jnp.int32)


def collide_kernel(pop_ref, low_ref, high_ref, rate_ref, c1_ref, cy_ref, right_ref, left_ref, edge):
    @pl.loop(0, 16)
    def _(x):
        for t in range(4):
            rows = slice(8 * t, 8 * t + 8)
            h = [pop_ref[i, x, rows, :].astype(F32) for i in range(19)]
            out = collide(h, rate_ref[1, 8 + 8 * t : 16 + 8 * t, :])
            for i in range(19):
                c1_ref[i, x, rows, :] = out[i].astype(BF16)

    for slot, y in HALO_Y:
        source = low_ref if y < 0 else high_ref
        row = y + 2 if y < 0 else y - 32
        rate = jnp.broadcast_to(rate_ref[1, y + 8 : y + 9, :], (8, 128))

        @pl.loop(0, 2)
        def _(half):
            start = pl.multiple_of(half * 8, 8)
            h = [source[i, row, pl.ds(start, 8), :].astype(F32) for i in range(19)]
            out = collide(h, rate)
            for i in range(19):
                edge[pl.ds(pl.multiple_of((i * 8 + slot) * 16 + start, 8), 8), :] = out[i]
                cy_ref[i, slot, pl.ds(start, 8), :] = out[i].astype(BF16)

    for ref, faces, planes in ((right_ref, RIGHTWARD, (None, 15, 14)), (left_ref, LEFTWARD, (None, 0, 1))):
        for n, (i, depth) in enumerate(faces):
            plane = planes[depth]
            ref[n, 0:32, :] = c1_ref[i, plane, :, :]
            ref[n, 32:40, :] = edge[pl.ds(i * 128 + plane, 8, stride=16), :].astype(BF16)


def shifted(ref, at, lane):
    out = []
    for i in range(19):
        dx, dy, dz = VEL[i]
        v = ref[i, pl.ds(at(-dx, -dy), 8), :]
        if dz == 1:
            v = jnp.where(lane == 0, ref[OPP[i], pl.ds(at(0, 0), 8), :], pltpu.roll(v, 1, axis=1))
        elif dz == -1:
            v = jnp.where(lane == 127, ref[OPP[i], pl.ds(at(0, 0), 8), :], pltpu.roll(v, 127, axis=1))
        out.append(v)
    return out


def step_kernel(
    flags_ref, owner_ref, owned_ref, c1_ref, cy_ref, gl_ref, gr_ref, rate_ref, reduce_ref,
    out_ref, send_ref,
    first, second, mix, blk, padded, coarse, pack, stage, zero, out_sem, send_sem,
):
    me = lax.axis_index("gx") * lax.axis_size("yz") + lax.axis_index("yz")
    lane = lax.broadcasted_iota(jnp.int32, (8, 128), 1)

    zero[...] = jnp.zeros_like(zero)

    @pl.loop(0, CAP)
    def _(s):
        @pl.when(owned_ref[s, 0] < 0)
        def _():
            pltpu.make_async_copy(zero, out_ref.at[s], out_sem.at[s]).start()

    @pl.loop(0, 16)
    def _(x):
        for i in range(19):
            start = pl.multiple_of((x + 2) * ROWS + 8, 8)
            first[i, pl.ds(start, 32), :] = c1_ref[i, x, :, :].astype(F32)

    for slot, y in HALO_Y:
        for i in range(19):
            for half in range(2):
                first[i, pl.ds((8 * half + 2) * ROWS + y + 8, 8, stride=ROWS), :] = cy_ref[
                    i, slot, 8 * half : 8 * half + 8, :
                ].astype(F32)
    for ref, faces, planes in ((gl_ref, RIGHTWARD, (None, -1, -2)), (gr_ref, LEFTWARD, (None, 16, 17))):
        for n, (i, depth) in enumerate(faces):
            base = (planes[depth] + 2) * ROWS
            first[i, base + 8 : base + 40, :] = ref[n, 0:32, :].astype(F32)
            edge = ref[n, 32:40, :].astype(F32)
            first[i, base + 40 : base + 48, :] = edge
            first[i, base : base + 8, :] = edge

    @pl.loop(0, 18)
    def _(p):
        which = (p + 15) // 16
        for t in range(5):
            def at(dx, dy, t=t):
                return pl.multiple_of(p * ROWS, 8) + ((dx + 1) * ROWS + 7 + 8 * t + dy)

            h = shifted(first, at, lane)
            out = collide([v.astype(BF16).astype(F32) for v in h], rate_ref[which, 7 + 8 * t : 15 + 8 * t, :])
            for i in range(19):
                second[i, pl.ds(pl.multiple_of(p * ROWS, 8) + (7 + 8 * t), 8), :] = out[i].astype(BF16).astype(F32)

    @pl.loop(0, 16)
    def _(x):
        for yh in range(4):
            def at(dx, dy, yh=yh):
                return pl.multiple_of(x * ROWS, 8) + ((dx + 1) * ROWS + 8 + 8 * yh + dy)

            h = shifted(second, at, lane)
            for i in range(19):
                mix[yh, 8 * i : 8 * i + 8, :] = h[i]
            groups = []
            for g in range(3):
                a = [mix[yh, pl.ds(64 * g + y, 8, stride=8), :] for y in range(8)]
                for bit in range(3):
                    width = 16 << bit
                    low = (lane & width) == 0
                    b = list(a)
                    for j in range(8):
                        if j & (1 << bit):
                            continue
                        k = j | (1 << bit)
                        b[j] = jnp.where(low, a[j], pltpu.roll(a[k], width, axis=1))
                        b[k] = jnp.where(low, pltpu.roll(a[j], 128 - width, axis=1), a[k])
                    a = b
                groups.append(a)
            lanes = pl.ds(pl.multiple_of(x * 256 + (yh % 2) * 128, 128), 128)
            for z in range(8):
                k = (yh // 2) * 8 + z
                head = jnp.concatenate([groups[0][z], groups[1][z]], axis=0).astype(BF16)
                tail = groups[2][z].astype(BF16)
                padded[k, 0:16, lanes] = head
                padded[k, 16:24, lanes] = tail
                blk[k, 0:16, lanes] = head
                blk[k, 16:19, lanes] = tail[0:3, :]

    @pl.loop(0, CAP)
    def _(s):
        b = owned_ref[s, 0]

        @pl.when((b >= 0) & (flags_ref[jnp.maximum(b, 0)] == 0))
        def _():
            pltpu.make_async_copy(blk.at[b - me * BLK], out_ref.at[s], out_sem.at[s]).start()

    for q in range(4):
        part = padded[:, :, q * 1024 : (q + 1) * 1024].reshape(BLK * 24, 1024)
        mean = jnp.dot(part, reduce_ref[...], preferred_element_type=F32)
        coarse[:, q, :, :] = mean.reshape(BLK, 24, 128)

    @pl.loop(0, BLK)
    def _(k):
        @pl.when(flags_ref[me * BLK + k] != 0)
        def _():
            for q in range(4):
                pack[20 * q : 20 * q + 24, :] = coarse[k, q, :, :]
            stage[k, :, :] = pack[0:80, :].astype(BF16)
            pltpu.make_async_copy(stage.at[k], send_ref.at[owner_ref[me * BLK + k]], send_sem.at[k]).start()

    @pl.loop(0, BLK)
    def _(k):
        @pl.when(flags_ref[me * BLK + k] != 0)
        def _():
            pltpu.make_async_copy(stage.at[k], send_ref.at[0], send_sem.at[k]).wait()

    @pl.loop(0, CAP)
    def _(s):
        b = owned_ref[s, 0]

        @pl.when((b < 0) | (flags_ref[jnp.maximum(b, 0)] == 0))
        def _():
            pltpu.make_async_copy(zero, out_ref.at[s], out_sem.at[s]).wait()


def refine_kernel(
    flags_ref, owned_ref, recv_ref, expand_ref, base_ref, out_ref,
    taken, fine, wide, product, result, slots, in_sem, out_sem,
):
    del base_ref

    def fetch(s, count):
        b = owned_ref[s, 0]
        arrives = (b >= 0) & (flags_ref[jnp.maximum(b, 0)] != 0)

        @pl.when(arrives)
        def _():
            slots[0, count] = s
            slots[1, count] = flags_ref[jnp.maximum(b, 0)]
            pltpu.make_async_copy(recv_ref.at[b // BLK], taken.at[count], in_sem.at[count]).start()

        return count + jnp.where(arrives, 1, 0)

    count = lax.fori_loop(0, CAP, fetch, jnp.int32(0))

    @pl.loop(0, count)
    def _(n):
        pltpu.make_async_copy(recv_ref.at[0], taken.at[n], in_sem.at[n]).wait()

    @pl.loop(0, (count + 3) // 4)
    def _(group):
        for m in range(4):
            fine[0:80, :] = taken[group * 4 + m, :, :].astype(F32)
            for q in range(4):
                wide[m * 96 + q * 24 : m * 96 + q * 24 + 24, :] = fine[20 * q : 20 * q + 24, :].astype(BF16)
        product[...] = jnp.dot(wide[...], expand_ref[...], preferred_element_type=F32)
        for m in range(4):
            n = group * 4 + m

            @pl.when(n < count)
            def _():
                kind = slots[1, n]
                linear = kind == 2
                near = jnp.where(linear, 0.75, 1.0)
                far = jnp.where(linear, 0.25, 0.0)
                offset = pl.multiple_of(jnp.where(linear, 512, 0), 512)

                def plane(c):
                    return product[
                        m * 96 + (c // 2) * 24 : m * 96 + (c // 2) * 24 + 24,
                        pl.ds(pl.multiple_of(offset + (c % 2) * 256, 256), 256),
                    ]

                for c in range(8):
                    mid = plane(c) * near
                    for odd in range(2):
                        other = max(c - 1, 0) if odd == 0 else min(c + 1, 7)
                        x = 2 * c + odd
                        value = (mid + plane(other) * far).astype(BF16)
                        result[n, 0:16, x * 256 : x * 256 + 256] = value[0:16, :]
                        result[n, 16:19, x * 256 : x * 256 + 256] = value[16:19, :]
                pltpu.make_async_copy(result.at[n], out_ref.at[slots[0, n]], out_sem.at[n]).start()

    @pl.loop(0, count)
    def _(n):
        pltpu.make_async_copy(result.at[n], out_ref.at[0], out_sem.at[n]).wait()


def mean_matrix():
    half = np.zeros((16, 8), np.float32)
    half[np.arange(16), np.arange(16) // 2] = 0.5
    pair = np.zeros((4, 2), np.float32)
    pair[np.arange(4), np.arange(4) // 2] = 0.5
    return np.kron(pair, np.kron(half, half))


def expand_matrix():
    inject = np.zeros((8, 16), np.float32)
    linear = np.zeros((8, 16), np.float32)
    for k in range(8):
        for odd, other in ((0, max(k - 1, 0)), (1, min(k + 1, 7))):
            inject[k, 2 * k + odd] = 1.0
            linear[k, 2 * k + odd] += 0.75
            linear[other, 2 * k + odd] += 0.25
    eye = np.eye(2, dtype=np.float32)
    return np.concatenate([np.kron(eye, np.kron(m, m)) for m in (inject, linear)], axis=1)


def ring(count, step):
    return [(i, (i + step) % count) for i in range(count)]


VM = pl.BlockSpec(memory_space=pltpu.VMEM)
SM = pl.BlockSpec(memory_space=pltpu.SMEM)
ANY = pl.BlockSpec(memory_space=pl.ANY)


def struct(shape, dtype):
    return jax.ShapeDtypeStruct(shape, dtype)


def body(populations, levels, refine_flags, new_owner):
    columns = lax.axis_size("yz")
    slabs = lax.axis_size("gx")
    slab = lax.axis_index("gx")
    column = lax.axis_index("yz")
    total = new_owner.shape[0]

    top = jnp.transpose(populations[:, :, 30:32, :], (0, 2, 1, 3))
    bottom = jnp.transpose(populations[:, :, 0:2, :], (0, 2, 1, 3))
    low = lax.ppermute(top, "yz", ring(columns, 1))
    high = lax.ppermute(bottom, "yz", ring(columns, -1))

    grid = levels.reshape(slabs, 2 * columns, BZ)
    grid = jnp.concatenate([grid[-1:], grid, grid[:1]], axis=0)
    grid = jnp.concatenate([grid[:, -1:], grid, grid[:, :1]], axis=1)
    near = lax.dynamic_slice(grid, (slab, 2 * column, 0), (3, 4, BZ)).astype(F32)
    near = 1.0 / (0.5 + jnp.power(0.5, near))
    rate = jnp.repeat(jnp.repeat(near, BS, axis=2), BS, axis=1)[:, 8:56, :]

    owned = pl.pallas_call(
        plan_kernel,
        out_shape=struct((32, 128), jnp.int32),
        in_specs=[VM],
        out_specs=VM,
        scratch_shapes=[pltpu.VMEM((32, 128), F32)],
    )(new_owner.reshape(total // 128, 128))

    c1, cy, right, left = pl.pallas_call(
        collide_kernel,
        out_shape=(
            struct((19, 16, 32, 128), BF16),
            struct((19, 8, 16, 128), BF16),
            struct((FACES, FROWS, 128), BF16),
            struct((FACES, FROWS, 128), BF16),
        ),
        in_specs=[VM] * 4,
        out_specs=(VM,) * 4,
        scratch_shapes=[pltpu.VMEM((19 * 128 + 128, 128), F32)],
    )(populations, low, high, rate)

    from_left = lax.ppermute(right, "gx", ring(slabs, 1))
    from_right = lax.ppermute(left, "gx", ring(slabs, -1))

    half, send = pl.pallas_call(
        step_kernel,
        out_shape=(struct((CAP, 19, 4096), BF16), struct((slabs * columns, 80, 128), BF16)),
        in_specs=[SM, SM, SM] + [VM] * 6,
        out_specs=(ANY, ANY),
        scratch_shapes=[
            pltpu.VMEM((19, 20 * ROWS, 128), F32),
            pltpu.VMEM((19, 18 * ROWS, 128), F32),
            pltpu.VMEM((4, 192, 128), F32),
            pltpu.VMEM((BLK, 19, 4096), BF16),
            pltpu.VMEM((BLK, 24, 4096), BF16),
            pltpu.VMEM((BLK, 4, 24, 128), F32),
            pltpu.VMEM((88, 128), F32),
            pltpu.VMEM((BLK, 80, 128), BF16),
            pltpu.VMEM((19, 4096), BF16),
            pltpu.SemaphoreType.DMA((CAP,)),
            pltpu.SemaphoreType.DMA((BLK,)),
        ],
    )(
        refine_flags, new_owner, owned, c1, cy, from_left, from_right, rate,
        jnp.asarray(mean_matrix(), BF16),
    )

    recv = lax.all_to_all(send, ("gx", "yz"), split_axis=0, concat_axis=0, tiled=True)

    return pl.pallas_call(
        refine_kernel,
        out_shape=struct((CAP, 19, 4096), BF16),
        in_specs=[SM, SM, ANY, VM, ANY],
        out_specs=ANY,
        input_output_aliases={4: 0},
        scratch_shapes=[
            pltpu.VMEM((MAXIN, 80, 128), BF16),
            pltpu.VMEM((88, 128), F32),
            pltpu.VMEM((384, 128), BF16),
            pltpu.VMEM((384, 1024), F32),
            pltpu.VMEM((MAXIN, 19, 4096), BF16),
            pltpu.SMEM((2, MAXIN), jnp.int32),
            pltpu.SemaphoreType.DMA((MAXIN,)),
            pltpu.SemaphoreType.DMA((MAXIN,)),
        ],
    )(refine_flags, owned, recv, jnp.asarray(expand_matrix(), BF16), half)


def solution(mesh):
    placed = (P(None, "gx", "yz", None), P(), P(), P())
    return jax.shard_map(
        body, mesh=mesh, in_specs=placed, out_specs=P(("gx", "yz"), None, None), check_vma=False
    )
```

```python
import jax
import jax.numpy as jnp
import numpy as np
from jax import lax
from jax.experimental import pallas as pl
from jax.experimental.pallas import tpu as pltpu
from jax.sharding import PartitionSpec as P

BS = 16
BZ = 8
CAP = 24
BLK = 16
ROWS = 48
F32 = jnp.float32
BF16 = jnp.bfloat16

VEL = [
    (0, 0, 0),
    (1, 0, 0), (-1, 0, 0), (0, 1, 0), (0, -1, 0), (0, 0, 1), (0, 0, -1),
    (1, 1, 0), (-1, -1, 0), (1, -1, 0), (-1, 1, 0),
    (1, 0, 1), (-1, 0, -1), (1, 0, -1), (-1, 0, 1),
    (0, 1, 1), (0, -1, -1), (0, 1, -1), (0, -1, 1),
]
OPP = [0, 2, 1, 4, 3, 6, 5, 8, 7, 10, 9, 12, 11, 14, 13, 16, 15, 18, 17]
PLUS = [i for i in range(19) if VEL[i][0] == 1]
MINUS = [i for i in range(19) if VEL[i][0] == -1]
FLAT = [i for i in range(19) if VEL[i][0] == 0]
RIGHTWARD = [(i, 2) for i in PLUS] + [(i, 1) for i in PLUS + FLAT + [12, 14]]
LEFTWARD = [(i, 2) for i in MINUS] + [(i, 1) for i in MINUS + FLAT + [11, 13]]
FACES = len(RIGHTWARD)
FROWS = 40
HALO_Y = ((0, 32), (1, 33), (6, -2), (7, -1))


def collide(h, r):
    p = {}
    d = {}
    for a in range(1, 19, 2):
        p[a] = h[a] + h[a + 1]
        d[a] = h[a] - h[a + 1]
    axis = p[1] + p[3] + p[5]
    diag = (p[7] + p[9]) + (p[11] + p[13]) + (p[15] + p[17])
    rho = 1.0 + (h[0] * (1.0 / 3.0) + axis * (1.0 / 18.0) + diag * (1.0 / 36.0))
    mx = (2.0 * d[1] + (d[7] + d[9]) + (d[11] + d[13])) * (1.0 / 36.0)
    my = (2.0 * d[3] + (d[7] - d[9]) + (d[15] + d[17])) * (1.0 / 36.0)
    mz = (2.0 * d[5] + (d[11] - d[13]) + (d[15] - d[17])) * (1.0 / 36.0)
    inv = 1.0 / rho
    ux, uy, uz = mx * inv, my * inv, mz * inv
    square = ux * ux + uy * uy + uz * uz
    keep = 1.0 - r
    base = r * (rho * (1.0 - 1.5 * square) - 1.0)
    quad = (4.5 * r) * rho
    lin = (3.0 * r) * rho
    proj = {
        1: ux, 3: uy, 5: uz, 7: ux + uy, 9: ux - uy, 11: ux + uz, 13: ux - uz, 15: uy + uz, 17: uy - uz,
    }
    out = [keep * h[0] + base] + [None] * 18
    for a in range(1, 19, 2):
        even = base + quad * (proj[a] * proj[a])
        odd = lin * proj[a]
        out[a] = keep * h[a] + (even + odd)
        out[a + 1] = keep * h[a + 1] + (even - odd)
    return out


def plan_kernel(levels_ref, flags_ref, owner_ref, rate_ref, owned_ref, kind_ref, part, kinds):
    slab, column = lax.axis_index("gx"), lax.axis_index("yz")
    slabs, columns = lax.axis_size("gx"), lax.axis_size("yz")
    me = slab * columns + column

    group = lax.broadcasted_iota(jnp.int32, (8, 128), 1) // BS
    for plane in range(3):
        row = lax.rem(slab + (plane + slabs - 1), slabs) * (2 * columns)
        for band, (first, last) in enumerate(((0, 8), (8, 24), (24, 40), (40, 48))):
            start = (row + lax.rem(2 * column + (band + 2 * columns - 1), 2 * columns)) * BZ
            level = jnp.zeros((8, 128), F32)
            for z in range(BZ):
                level = jnp.where(group == z, levels_ref[start + z].astype(F32), level)
            rate = 1.0 / (0.5 + jnp.exp2(-level))
            for at in range(first, last, 8):
                rate_ref[plane, at : at + 8, :] = rate

    rows = owner_ref.shape[0]
    mine = owner_ref[...] == me
    mask = jnp.where(mine, 1.0, 0.0)
    upper = lax.broadcasted_iota(jnp.int32, (128, 128), 0) <= lax.broadcasted_iota(jnp.int32, (128, 128), 1)
    before = lax.broadcasted_iota(jnp.int32, (rows, rows), 1) < lax.broadcasted_iota(jnp.int32, (rows, rows), 0)
    prefix = jnp.dot(mask.astype(BF16), jnp.where(upper, 1.0, 0.0).astype(BF16), preferred_element_type=F32)
    total = jnp.broadcast_to(jnp.sum(mask, axis=1, keepdims=True), (rows, 128))
    offset = jnp.dot(jnp.where(before, 1.0, 0.0).astype(BF16), total.astype(BF16), preferred_element_type=F32)
    rank = prefix + offset
    ids = lax.broadcasted_iota(jnp.int32, (rows, 128), 0) * 128 + lax.broadcasted_iota(jnp.int32, (rows, 128), 1)
    marked = jnp.where(mine, ids.astype(F32) + 1.0, 0.0)
    flagged = jnp.where(mine, flags_ref[...].astype(F32), 0.0)
    part[...] = jnp.zeros_like(part)
    kinds[...] = jnp.zeros_like(kinds)
    for slot in range(CAP):
        hit = rank == float(slot + 1)
        part[slot : slot + 1, :] = jnp.sum(jnp.where(hit, marked, 0.0), axis=0, keepdims=True)
        kinds[slot : slot + 1, :] = jnp.sum(jnp.where(hit, flagged, 0.0), axis=0, keepdims=True)
    found = jnp.sum(part[...], axis=1, keepdims=True) - 1.0
    owned_ref[...] = jnp.broadcast_to(found, part.shape).astype(jnp.int32)
    kind_ref[...] = jnp.broadcast_to(jnp.sum(kinds[...], axis=1, keepdims=True), kinds.shape)


def collide_kernel(pop_ref, rate_ref, c1_ref):
    @pl.loop(0, 16)
    def _(x):
        for t in range(4):
            rows = slice(8 * t, 8 * t + 8)
            h = [pop_ref[i, x, rows, :].astype(F32) for i in range(19)]
            out = collide(h, rate_ref[1, 8 + 8 * t : 16 + 8 * t, :])
            for i in range(19):
                c1_ref[i, x, rows, :] = out[i].astype(BF16)


def face_kernel(c1_ref, low_ref, high_ref, rate_ref, cy_ref, rim_ref, right_ref, left_ref, planes, edge, sem):
    copies = [
        pltpu.make_async_copy(c1_ref.at[:, a : a + 2], planes.at[:, b : b + 2], sem.at[n])
        for n, (a, b) in enumerate(((0, 0), (14, 2)))
    ]
    for copy in copies:
        copy.start()

    for slot, y in HALO_Y:
        source = low_ref if y < 0 else high_ref
        row = y + 2 if y < 0 else y - 32
        rate = jnp.broadcast_to(rate_ref[1, y + 8 : y + 9, :], (8, 128))

        @pl.loop(0, 2)
        def _(half):
            start = pl.multiple_of(half * 8, 8)
            h = [source[i, row, pl.ds(start, 8), :].astype(F32) for i in range(19)]
            out = collide(h, rate)
            for i in range(19):
                edge[pl.ds(pl.multiple_of((i * 8 + slot) * 16 + start, 8), 8), :] = out[i]
                cy_ref[i, slot, pl.ds(start, 8), :] = out[i].astype(BF16)

    for copy in copies:
        copy.wait()
    for i in range(19):
        for n, plane in enumerate((0, 1, 14, 15)):
            body_rows = planes[i, n, :, :]
            ends = edge[pl.ds(i * 128 + plane, 8, stride=16), :].astype(BF16)
            rim_ref[i, n, 0:32, :] = body_rows
            rim_ref[i, n, 32:40, :] = ends
            for ref, faces, depth in ((right_ref, RIGHTWARD, 16 - plane), (left_ref, LEFTWARD, plane + 1)):
                if (i, depth) in faces:
                    at = faces.index((i, depth))
                    ref[at, 0:32, :] = body_rows
                    ref[at, 32:40, :] = ends


def shifted(ref, at, lane):
    out = []
    for i in range(19):
        dx, dy, dz = VEL[i]
        v = ref[i, pl.ds(at(-dx, -dy), 8), :]
        if dz == 1:
            v = jnp.where(lane == 0, ref[OPP[i], pl.ds(at(0, 0), 8), :], pltpu.roll(v, 1, axis=1))
        elif dz == -1:
            v = jnp.where(lane == 127, ref[OPP[i], pl.ds(at(0, 0), 8), :], pltpu.roll(v, 127, axis=1))
        out.append(v)
    return out


def advance(source, at, rate, target, row, lane):
    h = shifted(source, at, lane)
    out = collide([v.astype(BF16).astype(F32) for v in h], rate)
    for i in range(19):
        target[i, pl.ds(row, 8), :] = out[i].astype(BF16).astype(F32)


def inner_kernel(c1_ref, cy_ref, rate_ref, c2_ref, first, second, sem):
    lane = lax.broadcasted_iota(jnp.int32, (8, 128), 1)

    @pl.loop(0, 16)
    def _(x):
        for i in range(19):
            first[i, pl.ds(pl.multiple_of(x * ROWS + 8, 8), 32), :] = c1_ref[i, x, :, :].astype(F32)

    for slot, y in HALO_Y:
        for i in range(19):
            for half in range(2):
                first[i, pl.ds(8 * half * ROWS + y + 8, 8, stride=ROWS), :] = cy_ref[
                    i, slot, 8 * half : 8 * half + 8, :
                ].astype(F32)

    @pl.loop(0, 14)
    def _(p):
        base = pl.multiple_of(p * ROWS, 8)
        for t in range(5):
            def at(dx, dy, t=t):
                return base + ((dx + 1) * ROWS + 7 + 8 * t + dy)

            advance(first, at, rate_ref[1, 7 + 8 * t : 15 + 8 * t, :], second, base + (7 + 8 * t), lane)
        pltpu.make_async_copy(second.at[:, pl.ds(base, ROWS)], c2_ref.at[:, pl.ds(base, ROWS)], sem.at[p]).start()

    @pl.loop(0, 14)
    def _(p):
        base = pl.multiple_of(p * ROWS, 8)
        pltpu.make_async_copy(second.at[:, pl.ds(base, ROWS)], c2_ref.at[:, pl.ds(base, ROWS)], sem.at[p]).wait()


def butterfly(a, lane, unit):
    for bit in range(3):
        width = unit << bit
        low = (lane & width) == 0
        b = list(a)
        for j in range(8):
            if j & (1 << bit):
                continue
            k = j | (1 << bit)
            b[j] = jnp.where(low, a[j], pltpu.roll(a[k], width, axis=1))
            b[k] = jnp.where(low, pltpu.roll(a[j], 128 - width, axis=1), a[k])
        a = b
    return a


def step_kernel(
    flags_ref, owner_ref, c2_ref, rim_ref, gl_ref, gr_ref, rate_ref, reduce_ref,
    state_ref, send_ref,
    first, second, state, mean, pack, stage, in_sem, out_sem, send_sem,
):
    me = lax.axis_index("gx") * lax.axis_size("yz") + lax.axis_index("yz")
    lane = lax.broadcasted_iota(jnp.int32, (8, 128), 1)
    inner = pltpu.make_async_copy(c2_ref, second.at[:, 2 * ROWS : 16 * ROWS], in_sem)
    inner.start()

    def place(i, at, rows):
        first[i, at * ROWS + 8 : at * ROWS + 40, :] = rows[0:32, :]
        first[i, at * ROWS + 40 : at * ROWS + 48, :] = rows[32:40, :]
        first[i, at * ROWS : at * ROWS + 8, :] = rows[32:40, :]

    for i in range(19):
        for n, at in enumerate((2, 3, 4, 5)):
            place(i, at, rim_ref[i, n, :, :].astype(F32))
    for ref, faces, places in ((gl_ref, RIGHTWARD, (None, 1, 0)), (gr_ref, LEFTWARD, (None, 6, 7))):
        for n, (i, depth) in enumerate(faces):
            place(i, places[depth], ref[n, :, :].astype(F32))

    @pl.loop(0, 4)
    def _(e):
        above = e // 2
        base = pl.multiple_of((e + 2 * above) * ROWS, 8)
        row = pl.multiple_of((e + 14 * above) * ROWS, 8)
        for t in range(5):
            def at(dx, dy, t=t):
                return base + ((dx + 1) * ROWS + 7 + 8 * t + dy)

            advance(first, at, rate_ref[(e + 1) // 2, 7 + 8 * t : 15 + 8 * t, :], second, row + (7 + 8 * t), lane)

    inner.wait()

    for q in range(4):
        @pl.loop(0, 4)
        def _(part):
            base = pl.multiple_of((4 * q + part) * ROWS, 8)
            for yh in range(4):
                def at(dx, dy, yh=yh):
                    return base + ((dx + 1) * ROWS + 8 + 8 * yh + dy)

                h = shifted(second, at, lane)
                for i in range(19):
                    state[q, 32 * i + 8 * yh : 32 * i + 8 * yh + 8, pl.ds(pl.multiple_of(part * 128, 128), 128)] = h[
                        i
                    ].astype(BF16)

        pltpu.make_async_copy(state.at[q], state_ref.at[q], out_sem.at[q]).start()
        mean[0:608, :] = jnp.dot(state[q, :, :], reduce_ref[...], preferred_element_type=F32)
        for by in range(2):
            for g in range(3):
                rows = [256 * g + 16 * by + 2 * y for y in range(8)]
                a = [mean[pl.ds(r, 8, stride=32), :] + mean[pl.ds(r + 1, 8, stride=32), :] for r in rows]
                a = butterfly(a, lane, 8)
                for z in range(8):
                    pack[8 * by + z, 20 * q + 8 * g : 20 * q + 8 * g + 8, :] = a[z]

    @pl.loop(0, BLK)
    def _(k):
        @pl.when(flags_ref[me * BLK + k] != 0)
        def _():
            stage[k, :, :] = pack[k, 0:80, :].astype(BF16)
            pltpu.make_async_copy(stage.at[k], send_ref.at[owner_ref[me * BLK + k]], send_sem.at[k]).start()

    @pl.loop(0, BLK)
    def _(k):
        @pl.when(flags_ref[me * BLK + k] != 0)
        def _():
            pltpu.make_async_copy(stage.at[k], send_ref.at[0], send_sem.at[k]).wait()

    for q in range(4):
        pltpu.make_async_copy(state.at[q], state_ref.at[q], out_sem.at[q]).wait()


def keep_kernel(flags_ref, owned_ref, state_ref, half_ref, mix, slots, place):
    me = lax.axis_index("gx") * lax.axis_size("yz") + lax.axis_index("yz")
    lane = lax.broadcasted_iota(jnp.int32, (8, 128), 1)

    @pl.loop(0, BLK)
    def _(k):
        place[k] = CAP

    @pl.loop(0, CAP)
    def _(s):
        b = owned_ref[s, 0]

        @pl.when((b >= 0) & (flags_ref[jnp.maximum(b, 0)] == 0))
        def _():
            place[b - me * BLK] = s

    @pl.loop(0, 32)
    def _(c):
        for r in range(CAP * 3):
            slots[c, 8 * r : 8 * r + 8, :] = jnp.zeros((8, 128), F32)

    @pl.loop(0, 16)
    def _(x):
        lanes = pl.ds(pl.multiple_of((x % 4) * 128, 128), 128)
        for yh in range(4):
            for i in range(19):
                mix[yh, 8 * i : 8 * i + 8, :] = state_ref[x // 4, 32 * i + 8 * yh : 32 * i + 8 * yh + 8, lanes].astype(
                    F32
                )
            for g in range(3):
                a = [mix[yh, pl.ds(64 * g + y, 8, stride=8), :] for y in range(8)]
                a = butterfly(a, lane, 16)
                for z in range(8):
                    row = pl.multiple_of(place[(yh // 2) * 8 + z] * 24 + 8 * g, 8)
                    slots[2 * x + yh % 2, pl.ds(row, 8), :] = a[z]

    @pl.loop(0, 32)
    def _(c):
        lanes = pl.ds(pl.multiple_of(c * 128, 128), 128)
        for i in range(19):
            parts = [slots[c, pl.ds(192 * g + i, 8, stride=24), :] for g in range(3)]
            half_ref[i, 0:16, lanes] = jnp.concatenate(parts[:2], axis=0).astype(BF16)
            half_ref[i, 16:24, lanes] = parts[2].astype(BF16)


def refine_kernel(
    flags_ref, owned_ref, recv_ref, kind_ref, expand_ref, half_ref, out_ref,
    taken, rows, wide, product, half, result, in_sem, half_sem, out_sem,
):
    def each_arrival(act):
        @pl.loop(0, CAP)
        def _(s):
            b = owned_ref[s, 0]

            @pl.when((b >= 0) & (flags_ref[jnp.maximum(b, 0)] != 0))
            def _():
                act(s, b // BLK)

    def fetch(s, device):
        pltpu.make_async_copy(recv_ref.at[device], taken.at[s], in_sem.at[s]).start()

    def widen(s, device):
        pltpu.make_async_copy(recv_ref.at[device], taken.at[s], in_sem.at[s]).wait()
        rows[pl.ds(pl.multiple_of(s * 80, 8), 80), :] = taken[s, :, :].astype(F32)

    each_arrival(fetch)

    @pl.loop(0, 19)
    def _(i):
        pltpu.make_async_copy(half_ref.at[i], half.at[i], half_sem.at[i]).start()

    each_arrival(widen)

    kinds = [kind_ref[8 * g : 8 * g + 8, :] for g in range(3)]
    for q in range(4):
        for i in range(19):
            ones, twos = [], []
            for g in range(3):
                v = rows[pl.ds(640 * g + 20 * q + i, 8, stride=80), :]
                ones.append(jnp.where(kinds[g] == 1.0, v, 0.0))
                twos.append(jnp.where(kinds[g] == 2.0, v, 0.0))
            for start, v in ((0, ones), (128, twos)):
                wide[q, 24 * i : 24 * i + 16, start : start + 128] = jnp.concatenate(v[:2], axis=0).astype(BF16)
                wide[q, 24 * i + 16 : 24 * i + 24, start : start + 128] = v[2].astype(BF16)
        product[q, :, :] = jnp.dot(wide[q, :, :], expand_ref[...], preferred_element_type=F32)

    linear = jnp.concatenate([jnp.concatenate([k, k], axis=1) for k in kinds], axis=0) == 2.0
    near = jnp.where(linear, 0.75, 1.0)
    far = jnp.where(linear, 0.25, 0.0)

    @pl.loop(0, 19)
    def _(i):
        pltpu.make_async_copy(half_ref.at[i], half.at[i], half_sem.at[i]).wait()
        start = pl.multiple_of(i * 24, 8)

        def plane(c):
            return product[c // 2, pl.ds(start, 24), (c % 2) * 256 : (c % 2) * 256 + 256]

        for c in range(8):
            mid = plane(c) * near
            for odd in range(2):
                other = max(c - 1, 0) if odd == 0 else min(c + 1, 7)
                x = slice((2 * c + odd) * 256, (2 * c + odd) * 256 + 256)
                value = (mid + plane(other) * far) + half[i, :, x].astype(F32)
                result[i, :, x] = value.astype(BF16)
        pltpu.make_async_copy(result.at[i], out_ref.at[i], out_sem.at[i]).start()

    @pl.loop(0, 19)
    def _(i):
        pltpu.make_async_copy(result.at[i], out_ref.at[i], out_sem.at[i]).wait()


def mean_matrix():
    half = np.zeros((128, 64), np.float32)
    half[np.arange(128), np.arange(128) // 2] = 0.125
    pair = np.zeros((4, 2), np.float32)
    pair[np.arange(4), np.arange(4) // 2] = 1.0
    return np.kron(pair, half)


def expand_matrix():
    inject = np.zeros((8, 16), np.float32)
    linear = np.zeros((8, 16), np.float32)
    for k in range(8):
        for odd, other in ((0, max(k - 1, 0)), (1, min(k + 1, 7))):
            inject[k, 2 * k + odd] = 1.0
            linear[k, 2 * k + odd] += 0.75
            linear[other, 2 * k + odd] += 0.25
    eye = np.eye(2, dtype=np.float32)
    return np.concatenate([np.kron(eye, np.kron(m, m)) for m in (inject, linear)], axis=0)


def ring(count, step):
    return [(i, (i + step) % count) for i in range(count)]


VM = pl.BlockSpec(memory_space=pltpu.VMEM)
SM = pl.BlockSpec(memory_space=pltpu.SMEM)
ANY = pl.BlockSpec(memory_space=pl.ANY)


def struct(shape, dtype):
    return jax.ShapeDtypeStruct(shape, dtype)


def cost(microseconds):
    return pl.CostEstimate(flops=0, bytes_accessed=int(microseconds * 3.0e6), transcendentals=0)


def body(populations, levels, refine_flags, new_owner):
    columns = lax.axis_size("yz")
    slabs = lax.axis_size("gx")
    total = new_owner.shape[0]
    devices = slabs * columns

    top = jnp.transpose(populations[:, :, 30:32, :], (0, 2, 1, 3))
    bottom = jnp.transpose(populations[:, :, 0:2, :], (0, 2, 1, 3))
    low = lax.ppermute(top, "yz", ring(columns, 1))
    high = lax.ppermute(bottom, "yz", ring(columns, -1))

    rate, owned, kind = pl.pallas_call(
        plan_kernel,
        out_shape=(struct((3, ROWS, 128), F32), struct((32, 128), jnp.int32), struct((32, 128), F32)),
        in_specs=[SM, VM, VM],
        out_specs=(VM, VM, VM),
        scratch_shapes=[pltpu.VMEM((32, 128), F32), pltpu.VMEM((32, 128), F32)],
        cost_estimate=cost(2),
        name="plan",
    )(levels, refine_flags.reshape(total // 128, 128), new_owner.reshape(total // 128, 128))

    c1 = pl.pallas_call(
        collide_kernel,
        out_shape=struct((19, 16, 32, 128), BF16),
        in_specs=[VM, VM],
        out_specs=VM,
        cost_estimate=cost(5),
        name="collide",
    )(populations, rate)

    cy, rim, right, left = pl.pallas_call(
        face_kernel,
        out_shape=(
            struct((19, 8, 16, 128), BF16),
            struct((19, 4, FROWS, 128), BF16),
            struct((FACES, FROWS, 128), BF16),
            struct((FACES, FROWS, 128), BF16),
        ),
        in_specs=[ANY, VM, VM, VM],
        out_specs=(VM,) * 4,
        scratch_shapes=[
            pltpu.VMEM((19, 4, 32, 128), BF16),
            pltpu.VMEM((19 * 128 + 128, 128), F32),
            pltpu.SemaphoreType.DMA((2,)),
        ],
        cost_estimate=cost(2),
        name="faces",
    )(c1, low, high, rate)

    from_left = lax.ppermute(right, "gx", ring(slabs, 1))
    from_right = lax.ppermute(left, "gx", ring(slabs, -1))

    c2 = pl.pallas_call(
        inner_kernel,
        out_shape=struct((19, 14 * ROWS, 128), F32),
        in_specs=[VM, VM, VM],
        out_specs=ANY,
        scratch_shapes=[
            pltpu.VMEM((19, 16 * ROWS, 128), F32),
            pltpu.VMEM((19, 14 * ROWS, 128), F32),
            pltpu.SemaphoreType.DMA((14,)),
        ],
        cost_estimate=cost(6),
        name="inner",
    )(c1, cy, rate)

    state, send = pl.pallas_call(
        step_kernel,
        out_shape=(struct((4, 608, 512), BF16), struct((devices, 80, 128), BF16)),
        in_specs=[SM, SM, ANY] + [VM] * 5,
        out_specs=(ANY, ANY),
        scratch_shapes=[
            pltpu.VMEM((19, 8 * ROWS, 128), F32),
            pltpu.VMEM((19, 18 * ROWS, 128), F32),
            pltpu.VMEM((4, 608, 512), BF16),
            pltpu.VMEM((768, 128), F32),
            pltpu.VMEM((BLK, 88, 128), F32),
            pltpu.VMEM((BLK, 80, 128), BF16),
            pltpu.SemaphoreType.DMA,
            pltpu.SemaphoreType.DMA((4,)),
            pltpu.SemaphoreType.DMA((BLK,)),
        ],
        cost_estimate=cost(6),
        name="step",
    )(
        refine_flags, new_owner, c2, rim, from_left, from_right, rate,
        jnp.asarray(mean_matrix(), BF16),
    )

    recv = lax.all_to_all(send, ("gx", "yz"), split_axis=0, concat_axis=0, tiled=True)

    half = pl.pallas_call(
        keep_kernel,
        out_shape=struct((19, CAP, 4096), BF16),
        in_specs=[SM, SM, VM],
        out_specs=VM,
        scratch_shapes=[
            pltpu.VMEM((4, 192, 128), F32),
            pltpu.VMEM((32, (CAP + 1) * 24, 128), F32),
            pltpu.SMEM((BLK,), jnp.int32),
        ],
        cost_estimate=cost(10),
        name="keep",
    )(refine_flags, owned, state)

    migrated = pl.pallas_call(
        refine_kernel,
        out_shape=struct((19, CAP, 4096), BF16),
        in_specs=[SM, SM, ANY, VM, VM, ANY],
        out_specs=ANY,
        scratch_shapes=[
            pltpu.VMEM((CAP, 80, 128), BF16),
            pltpu.VMEM((CAP * 80, 128), F32),
            pltpu.VMEM((4, 456, 256), BF16),
            pltpu.VMEM((4, 456, 512), F32),
            pltpu.VMEM((19, CAP, 4096), BF16),
            pltpu.VMEM((19, CAP, 4096), BF16),
            pltpu.SemaphoreType.DMA((CAP,)),
            pltpu.SemaphoreType.DMA((19,)),
            pltpu.SemaphoreType.DMA((19,)),
        ],
        cost_estimate=cost(5),
        name="refine",
    )(refine_flags, owned, recv, kind, jnp.asarray(expand_matrix(), BF16), half)
    return jnp.transpose(migrated, (1, 0, 2))


def solution(mesh):
    placed = (P(None, "gx", "yz", None), P(), P(), P())
    return jax.shard_map(
        body, mesh=mesh, in_specs=placed, out_specs=P(("gx", "yz"), None, None), check_vma=False
    )
```

```python
import jax
import jax.numpy as jnp
import numpy as np
from jax import lax
from jax.experimental import pallas as pl
from jax.experimental.pallas import tpu as pltpu
from jax.sharding import PartitionSpec as P

BS = 16
BZ = 8
CAP = 24
BLK = 16
ROWS = 48
F32 = jnp.float32
BF16 = jnp.bfloat16

VEL = [
    (0, 0, 0),
    (1, 0, 0), (-1, 0, 0), (0, 1, 0), (0, -1, 0), (0, 0, 1), (0, 0, -1),
    (1, 1, 0), (-1, -1, 0), (1, -1, 0), (-1, 1, 0),
    (1, 0, 1), (-1, 0, -1), (1, 0, -1), (-1, 0, 1),
    (0, 1, 1), (0, -1, -1), (0, 1, -1), (0, -1, 1),
]
OPP = [0, 2, 1, 4, 3, 6, 5, 8, 7, 10, 9, 12, 11, 14, 13, 16, 15, 18, 17]
PLUS = [i for i in range(19) if VEL[i][0] == 1]
MINUS = [i for i in range(19) if VEL[i][0] == -1]
FLAT = [i for i in range(19) if VEL[i][0] == 0]
RIGHTWARD = [(i, 2) for i in PLUS] + [(i, 1) for i in PLUS + FLAT + [12, 14]]
LEFTWARD = [(i, 2) for i in MINUS] + [(i, 1) for i in MINUS + FLAT + [11, 13]]
FACES = len(RIGHTWARD)
FROWS = 40
HALO_Y = ((0, 32), (1, 33), (6, -2), (7, -1))


def collide(h, r):
    p = {}
    d = {}
    for a in range(1, 19, 2):
        p[a] = h[a] + h[a + 1]
        d[a] = h[a] - h[a + 1]
    axis = p[1] + p[3] + p[5]
    diag = (p[7] + p[9]) + (p[11] + p[13]) + (p[15] + p[17])
    rho = 1.0 + (h[0] * (1.0 / 3.0) + axis * (1.0 / 18.0) + diag * (1.0 / 36.0))
    mx = (2.0 * d[1] + (d[7] + d[9]) + (d[11] + d[13])) * (1.0 / 36.0)
    my = (2.0 * d[3] + (d[7] - d[9]) + (d[15] + d[17])) * (1.0 / 36.0)
    mz = (2.0 * d[5] + (d[11] - d[13]) + (d[15] - d[17])) * (1.0 / 36.0)
    inv = 1.0 / rho
    ux, uy, uz = mx * inv, my * inv, mz * inv
    square = ux * ux + uy * uy + uz * uz
    keep = 1.0 - r
    base = r * (rho * (1.0 - 1.5 * square) - 1.0)
    quad = (4.5 * r) * rho
    lin = (3.0 * r) * rho
    proj = {
        1: ux, 3: uy, 5: uz, 7: ux + uy, 9: ux - uy, 11: ux + uz, 13: ux - uz, 15: uy + uz, 17: uy - uz,
    }
    out = [keep * h[0] + base] + [None] * 18
    for a in range(1, 19, 2):
        even = base + quad * (proj[a] * proj[a])
        odd = lin * proj[a]
        out[a] = keep * h[a] + (even + odd)
        out[a + 1] = keep * h[a + 1] + (even - odd)
    return out


def rate_kernel(levels_ref, rate_ref):
    slab, column = lax.axis_index("gx"), lax.axis_index("yz")
    slabs, columns = lax.axis_size("gx"), lax.axis_size("yz")
    group = lax.broadcasted_iota(jnp.int32, (8, 128), 1) // BS
    for plane in range(3):
        row = lax.rem(slab + (plane + slabs - 1), slabs) * (2 * columns)
        for band, (first, last) in enumerate(((0, 8), (8, 24), (24, 40), (40, 48))):
            start = (row + lax.rem(2 * column + (band + 2 * columns - 1), 2 * columns)) * BZ
            level = jnp.zeros((8, 128), F32)
            for z in range(BZ):
                level = jnp.where(group == z, levels_ref[start + z].astype(F32), level)
            rate = 1.0 / (0.5 + jnp.exp2(-level))
            for at in range(first, last, 8):
                rate_ref[plane, at : at + 8, :] = rate


def plan_kernel(flags_ref, owner_ref, after_ref, owned_ref, kind_ref, part, kinds):
    del after_ref
    me = lax.axis_index("gx") * lax.axis_size("yz") + lax.axis_index("yz")
    rows = owner_ref.shape[0]
    mine = owner_ref[...] == me
    mask = jnp.where(mine, 1.0, 0.0)
    upper = lax.broadcasted_iota(jnp.int32, (128, 128), 0) <= lax.broadcasted_iota(jnp.int32, (128, 128), 1)
    before = lax.broadcasted_iota(jnp.int32, (rows, rows), 1) < lax.broadcasted_iota(jnp.int32, (rows, rows), 0)
    prefix = jnp.dot(mask.astype(BF16), jnp.where(upper, 1.0, 0.0).astype(BF16), preferred_element_type=F32)
    total = jnp.broadcast_to(jnp.sum(mask, axis=1, keepdims=True), (rows, 128))
    offset = jnp.dot(jnp.where(before, 1.0, 0.0).astype(BF16), total.astype(BF16), preferred_element_type=F32)
    rank = prefix + offset
    ids = lax.broadcasted_iota(jnp.int32, (rows, 128), 0) * 128 + lax.broadcasted_iota(jnp.int32, (rows, 128), 1)
    marked = jnp.where(mine, ids.astype(F32) + 1.0, 0.0)
    flagged = jnp.where(mine, flags_ref[...].astype(F32), 0.0)
    part[...] = jnp.zeros_like(part)
    kinds[...] = jnp.zeros_like(kinds)
    for slot in range(CAP):
        hit = rank == float(slot + 1)
        part[slot : slot + 1, :] = jnp.sum(jnp.where(hit, marked, 0.0), axis=0, keepdims=True)
        kinds[slot : slot + 1, :] = jnp.sum(jnp.where(hit, flagged, 0.0), axis=0, keepdims=True)
    found = jnp.sum(part[...], axis=1, keepdims=True) - 1.0
    owned_ref[...] = jnp.broadcast_to(found, part.shape).astype(jnp.int32)
    kind_ref[...] = jnp.broadcast_to(jnp.sum(kinds[...], axis=1, keepdims=True), kinds.shape)


def collide_kernel(pop_ref, rate_ref, c1_ref, planes, sem):
    def fetch(part):
        at = pl.ds(part * 4, 4)
        return pltpu.make_async_copy(pop_ref.at[:, at], planes.at[:, at], sem.at[part])

    for part in range(4):
        fetch(part).start()

    @pl.loop(0, 4)
    def _(part):
        fetch(part).wait()

        @pl.loop(0, 4)
        def _(step):
            x = part * 4 + step
            for t in range(4):
                rows = slice(8 * t, 8 * t + 8)
                h = [planes[i, x, rows, :].astype(F32) for i in range(19)]
                out = collide(h, rate_ref[1, 8 + 8 * t : 16 + 8 * t, :])
                for i in range(19):
                    c1_ref[i, x, rows, :] = out[i].astype(BF16)


def face_kernel(c1_ref, low_ref, high_ref, rate_ref, cy_ref, rim_ref, right_ref, left_ref, planes, edge, sem):
    copies = [
        pltpu.make_async_copy(c1_ref.at[:, a : a + 2], planes.at[:, b : b + 2], sem.at[n])
        for n, (a, b) in enumerate(((0, 0), (14, 2)))
    ]
    for copy in copies:
        copy.start()

    for slot, y in HALO_Y:
        source = low_ref if y < 0 else high_ref
        row = y + 2 if y < 0 else y - 32
        rate = jnp.broadcast_to(rate_ref[1, y + 8 : y + 9, :], (8, 128))

        @pl.loop(0, 2)
        def _(half):
            start = pl.multiple_of(half * 8, 8)
            h = [source[i, row, pl.ds(start, 8), :].astype(F32) for i in range(19)]
            out = collide(h, rate)
            for i in range(19):
                edge[pl.ds(pl.multiple_of((i * 8 + slot) * 16 + start, 8), 8), :] = out[i]
                cy_ref[i, slot, pl.ds(start, 8), :] = out[i].astype(BF16)

    for copy in copies:
        copy.wait()
    for i in range(19):
        for n, plane in enumerate((0, 1, 14, 15)):
            body_rows = planes[i, n, :, :]
            ends = edge[pl.ds(i * 128 + plane, 8, stride=16), :].astype(BF16)
            rim_ref[i, n, 0:32, :] = body_rows
            rim_ref[i, n, 32:40, :] = ends
            for ref, faces, depth in ((right_ref, RIGHTWARD, 16 - plane), (left_ref, LEFTWARD, plane + 1)):
                if (i, depth) in faces:
                    at = faces.index((i, depth))
                    ref[at, 0:32, :] = body_rows
                    ref[at, 32:40, :] = ends


def shifted(ref, at, lane):
    out = []
    for i in range(19):
        dx, dy, dz = VEL[i]
        v = ref[i, pl.ds(at(-dx, -dy), 8), :]
        if dz == 1:
            v = jnp.where(lane == 0, ref[OPP[i], pl.ds(at(0, 0), 8), :], pltpu.roll(v, 1, axis=1))
        elif dz == -1:
            v = jnp.where(lane == 127, ref[OPP[i], pl.ds(at(0, 0), 8), :], pltpu.roll(v, 127, axis=1))
        out.append(v)
    return out


def advance(source, at, rate, target, row, lane):
    out = collide(shifted(source, at, lane), rate)
    for i in range(19):
        target[i, pl.ds(row, 8), :] = out[i]


def settle(source, base, target, part, lanes, lane):
    for yh in range(4):
        def at(dx, dy, yh=yh):
            return base + ((dx + 1) * ROWS + 8 + 8 * yh + dy)

        h = shifted(source, at, lane)
        for i in range(19):
            target[part, 32 * i + 8 * yh : 32 * i + 8 * yh + 8, lanes] = h[i].astype(BF16)


def inner_kernel(c1_ref, cy_ref, rate_ref, rest_ref, state_ref, first, second, sem):
    lane = lax.broadcasted_iota(jnp.int32, (8, 128), 1)

    @pl.loop(0, 16)
    def _(x):
        for i in range(19):
            first[i, pl.ds(pl.multiple_of(x * ROWS + 8, 8), 32), :] = c1_ref[i, x, :, :].astype(F32)

    for slot, y in HALO_Y:
        for i in range(19):
            for half in range(2):
                first[i, pl.ds(8 * half * ROWS + y + 8, 8, stride=ROWS), :] = cy_ref[
                    i, slot, 8 * half : 8 * half + 8, :
                ].astype(F32)

    @pl.loop(0, 14)
    def _(p):
        base = pl.multiple_of(p * ROWS, 8)
        for t in range(5):
            def at(dx, dy, t=t):
                return base + ((dx + 1) * ROWS + 7 + 8 * t + dy)

            advance(first, at, rate_ref[1, 7 + 8 * t : 15 + 8 * t, :], second, base + (7 + 8 * t), lane)

    copies = [
        pltpu.make_async_copy(
            second.at[:, a * ROWS : (a + 2) * ROWS], rest_ref.at[:, b * ROWS : (b + 2) * ROWS], sem.at[n]
        )
        for n, (a, b) in enumerate(((0, 0), (12, 2)))
    ]
    for copy in copies:
        copy.start()

    @pl.loop(0, 12)
    def _(p):
        lanes = pl.ds(pl.multiple_of((p % 2) * 128, 128), 128)
        settle(second, pl.multiple_of(p * ROWS, 8), state_ref, p // 2, lanes, lane)

    for copy in copies:
        copy.wait()


def butterfly(a, lane, unit):
    for bit in range(3):
        width = unit << bit
        low = (lane & width) == 0
        b = list(a)
        for j in range(8):
            if j & (1 << bit):
                continue
            k = j | (1 << bit)
            b[j] = jnp.where(low, a[j], pltpu.roll(a[k], width, axis=1))
            b[k] = jnp.where(low, pltpu.roll(a[j], 128 - width, axis=1), a[k])
        a = b
    return a


def step_kernel(
    flags_ref, owner_ref, rest_ref, rim_ref, gl_ref, gr_ref, rate_ref, reduce_ref, inner_ref,
    outer_ref, send_ref,
    first, second, mean, mix, pack, stage, in_sem, send_sem,
):
    me = lax.axis_index("gx") * lax.axis_size("yz") + lax.axis_index("yz")
    lane = lax.broadcasted_iota(jnp.int32, (8, 128), 1)
    rest = pltpu.make_async_copy(rest_ref, second.at[:, 2 * ROWS : 6 * ROWS], in_sem)
    rest.start()

    def place(i, at, rows):
        first[i, at * ROWS + 8 : at * ROWS + 40, :] = rows[0:32, :]
        first[i, at * ROWS + 40 : at * ROWS + 48, :] = rows[32:40, :]
        first[i, at * ROWS : at * ROWS + 8, :] = rows[32:40, :]

    for i in range(19):
        for n, at in enumerate((2, 3, 4, 5)):
            place(i, at, rim_ref[i, n, :, :].astype(F32))
    for ref, faces, places in ((gl_ref, RIGHTWARD, (None, 1, 0)), (gr_ref, LEFTWARD, (None, 6, 7))):
        for n, (i, depth) in enumerate(faces):
            place(i, places[depth], ref[n, :, :].astype(F32))

    @pl.loop(0, 4)
    def _(e):
        above = e // 2
        base = pl.multiple_of((e + 2 * above) * ROWS, 8)
        row = pl.multiple_of((e + 4 * above) * ROWS, 8)
        for t in range(5):
            def at(dx, dy, t=t):
                return base + ((dx + 1) * ROWS + 7 + 8 * t + dy)

            advance(first, at, rate_ref[(e + 1) // 2, 7 + 8 * t : 15 + 8 * t, :], second, row + (7 + 8 * t), lane)

    rest.wait()

    @pl.loop(0, 4)
    def _(e):
        above = e // 2
        lanes = pl.ds(pl.multiple_of((e % 2) * 128, 128), 128)
        settle(second, pl.multiple_of((e + 2 * above) * ROWS, 8), outer_ref, above, lanes, lane)

    for q in range(4):
        total = None
        for par in range(2):
            c = 2 * q + par
            pair = outer_ref[c // 7, :, :] if c in (0, 7) else inner_ref[c - 1, :, :]
            term = jnp.dot(pair, reduce_ref[par, :, :], preferred_element_type=F32)
            total = term if total is None else total + term
        mean[q, :, :] = total
        for i in range(19):
            for by in range(2):
                at = 32 * i + 16 * by
                mix[q, by, 8 * i : 8 * i + 8, :] = (
                    mean[q, pl.ds(at, 8, stride=2), :] + mean[q, pl.ds(at + 1, 8, stride=2), :]
                )
        for by in range(2):
            for g in range(3):
                a = [mix[q, by, pl.ds(64 * g + y, 8, stride=8), :] for y in range(8)]
                a = butterfly(a, lane, 8)
                for z in range(8):
                    pack[8 * by + z, 20 * q + 8 * g : 20 * q + 8 * g + 8, :] = a[z]

    @pl.loop(0, BLK)
    def _(k):
        @pl.when(flags_ref[me * BLK + k] != 0)
        def _():
            stage[k, :, :] = pack[k, 0:80, :].astype(BF16)
            pltpu.make_async_copy(stage.at[k], send_ref.at[owner_ref[me * BLK + k]], send_sem.at[k]).start()

    @pl.loop(0, BLK)
    def _(k):
        @pl.when(flags_ref[me * BLK + k] != 0)
        def _():
            pltpu.make_async_copy(stage.at[k], send_ref.at[0], send_sem.at[k]).wait()


def keep_kernel(flags_ref, owned_ref, inner_ref, outer_ref, half_ref, mix, slots, place):
    me = lax.axis_index("gx") * lax.axis_size("yz") + lax.axis_index("yz")
    lane = lax.broadcasted_iota(jnp.int32, (8, 128), 1)

    @pl.loop(0, BLK)
    def _(k):
        place[k] = CAP

    @pl.loop(0, CAP)
    def _(s):
        b = owned_ref[s, 0]

        @pl.when((b >= 0) & (flags_ref[jnp.maximum(b, 0)] == 0))
        def _():
            place[b - me * BLK] = s

    @pl.loop(0, 32)
    def _(c):
        for r in range(CAP * 3):
            slots[c, 8 * r : 8 * r + 8, :] = jnp.zeros((8, 128), F32)

    def spread(state_ref, pair, x):
        lanes = pl.ds(pl.multiple_of((x % 2) * 128, 128), 128)
        for yh in range(4):
            for i in range(19):
                tile = state_ref[pair, 32 * i + 8 * yh : 32 * i + 8 * yh + 8, lanes]
                mix[yh, 8 * i : 8 * i + 8, :] = tile.astype(F32)
            for g in range(3):
                a = [mix[yh, pl.ds(64 * g + y, 8, stride=8), :] for y in range(8)]
                a = butterfly(a, lane, 16)
                for z in range(8):
                    row = pl.multiple_of(place[(yh // 2) * 8 + z] * 24 + 8 * g, 8)
                    slots[2 * x + yh % 2, pl.ds(row, 8), :] = a[z]

    @pl.loop(2, 14)
    def _(x):
        spread(inner_ref, x // 2 - 1, x)

    @pl.loop(0, 4)
    def _(e):
        spread(outer_ref, e // 2, e + 12 * (e // 2))

    @pl.loop(0, 32)
    def _(c):
        lanes = pl.ds(pl.multiple_of(c * 128, 128), 128)
        for i in range(19):
            parts = [slots[c, pl.ds(192 * g + i, 8, stride=24), :] for g in range(3)]
            half_ref[i, 0:16, lanes] = jnp.concatenate(parts[:2], axis=0).astype(BF16)
            half_ref[i, 16:24, lanes] = parts[2].astype(BF16)


def refine_kernel(
    flags_ref, owned_ref, recv_ref, kind_ref, expand_ref, half_ref, out_ref,
    taken, rows, wide, product, half, result, in_sem, half_sem, out_sem,
):
    def each_arrival(act):
        @pl.loop(0, CAP)
        def _(s):
            b = owned_ref[s, 0]

            @pl.when((b >= 0) & (flags_ref[jnp.maximum(b, 0)] != 0))
            def _():
                act(s, b // BLK)

    def fetch(s, device):
        pltpu.make_async_copy(recv_ref.at[device], taken.at[s], in_sem.at[s]).start()

    def widen(s, device):
        pltpu.make_async_copy(recv_ref.at[device], taken.at[s], in_sem.at[s]).wait()
        for r in range(10):
            rows[pl.ds(192 * r + s, 8, stride=24), :] = taken[s, 8 * r : 8 * r + 8, :].astype(F32)

    each_arrival(fetch)

    @pl.loop(0, 19)
    def _(i):
        pltpu.make_async_copy(half_ref.at[i], half.at[i], half_sem.at[i]).start()

    each_arrival(widen)

    kinds = [kind_ref[8 * g : 8 * g + 8, :] for g in range(3)]
    for q in range(4):
        for i in range(19):
            ones, twos = [], []
            for g in range(3):
                start = 24 * (20 * q + i) + 8 * g
                v = rows[start : start + 8, :]
                ones.append(jnp.where(kinds[g] == 1.0, v, 0.0))
                twos.append(jnp.where(kinds[g] == 2.0, v, 0.0))
            for start, v in ((0, ones), (128, twos)):
                wide[q, 24 * i : 24 * i + 16, start : start + 128] = jnp.concatenate(v[:2], axis=0).astype(BF16)
                wide[q, 24 * i + 16 : 24 * i + 24, start : start + 128] = v[2].astype(BF16)
        product[q, :, :] = jnp.dot(wide[q, :, :], expand_ref[...], preferred_element_type=F32)

    linear = jnp.concatenate([jnp.concatenate([k, k], axis=1) for k in kinds], axis=0) == 2.0
    near = jnp.where(linear, 0.75, 1.0)
    far = jnp.where(linear, 0.25, 0.0)

    @pl.loop(0, 19)
    def _(i):
        pltpu.make_async_copy(half_ref.at[i], half.at[i], half_sem.at[i]).wait()
        start = pl.multiple_of(i * 24, 8)

        def plane(c):
            return product[c // 2, pl.ds(start, 24), (c % 2) * 256 : (c % 2) * 256 + 256]

        for c in range(8):
            mid = plane(c) * near
            for odd in range(2):
                other = max(c - 1, 0) if odd == 0 else min(c + 1, 7)
                x = slice((2 * c + odd) * 256, (2 * c + odd) * 256 + 256)
                result[i, :, x] = (mid + plane(other) * far).astype(BF16) + half[i, :, x]
        pltpu.make_async_copy(result.at[i], out_ref.at[i], out_sem.at[i]).start()

    @pl.loop(0, 19)
    def _(i):
        pltpu.make_async_copy(result.at[i], out_ref.at[i], out_sem.at[i]).wait()


def mean_matrix():
    half = np.zeros((128, 64), np.float32)
    half[np.arange(128), np.arange(128) // 2] = 0.125
    both = np.concatenate([half, half], axis=0)
    none = np.zeros_like(both)
    return np.stack([np.concatenate([both, none], axis=1), np.concatenate([none, both], axis=1)])


def expand_matrix():
    inject = np.zeros((8, 16), np.float32)
    linear = np.zeros((8, 16), np.float32)
    for k in range(8):
        for odd, other in ((0, max(k - 1, 0)), (1, min(k + 1, 7))):
            inject[k, 2 * k + odd] = 1.0
            linear[k, 2 * k + odd] += 0.75
            linear[other, 2 * k + odd] += 0.25
    eye = np.eye(2, dtype=np.float32)
    return np.concatenate([np.kron(eye, np.kron(m, m)) for m in (inject, linear)], axis=0)


def ring(count, step):
    return [(i, (i + step) % count) for i in range(count)]


VM = pl.BlockSpec(memory_space=pltpu.VMEM)
SM = pl.BlockSpec(memory_space=pltpu.SMEM)
ANY = pl.BlockSpec(memory_space=pl.ANY)
HBM = pl.BlockSpec(memory_space=pltpu.HBM)


def struct(shape, dtype):
    return jax.ShapeDtypeStruct(shape, dtype)


def in_hbm(array):
    return pltpu.with_memory_space_constraint(array, pltpu.HBM)


def cost(microseconds):
    return pl.CostEstimate(flops=0, bytes_accessed=int(microseconds * 3.0e6), transcendentals=0)


def limit(mebibytes):
    return pltpu.CompilerParams(vmem_limit_bytes=mebibytes << 20)


def body(populations, levels, refine_flags, new_owner):
    columns = lax.axis_size("yz")
    slabs = lax.axis_size("gx")
    total = new_owner.shape[0]
    devices = slabs * columns

    top = jnp.transpose(populations[:, :, 30:32, :], (0, 2, 1, 3))
    bottom = jnp.transpose(populations[:, :, 0:2, :], (0, 2, 1, 3))
    low = lax.ppermute(top, "yz", ring(columns, 1))
    high = lax.ppermute(bottom, "yz", ring(columns, -1))

    rate = pl.pallas_call(
        rate_kernel,
        out_shape=struct((3, ROWS, 128), F32),
        in_specs=[SM],
        out_specs=VM,
        compiler_params=limit(4),
        cost_estimate=cost(1),
        name="rates",
    )(in_hbm(levels))

    c1 = pl.pallas_call(
        collide_kernel,
        out_shape=struct((19, 16, 32, 128), BF16),
        in_specs=[HBM, VM],
        out_specs=VM,
        scratch_shapes=[pltpu.VMEM((19, 16, 32, 128), BF16), pltpu.SemaphoreType.DMA((4,))],
        compiler_params=limit(8),
        cost_estimate=cost(5),
        name="collide",
    )(in_hbm(populations), rate)

    cy, rim, right, left = pl.pallas_call(
        face_kernel,
        out_shape=(
            struct((19, 8, 16, 128), BF16),
            struct((19, 4, FROWS, 128), BF16),
            struct((FACES, FROWS, 128), BF16),
            struct((FACES, FROWS, 128), BF16),
        ),
        in_specs=[ANY, VM, VM, VM],
        out_specs=(VM,) * 4,
        scratch_shapes=[
            pltpu.VMEM((19, 4, 32, 128), BF16),
            pltpu.VMEM((19 * 128 + 128, 128), F32),
            pltpu.SemaphoreType.DMA((2,)),
        ],
        compiler_params=limit(8),
        cost_estimate=cost(2),
        name="faces",
    )(c1, low, high, rate)

    from_left = lax.ppermute(right, "gx", ring(slabs, 1))
    from_right = lax.ppermute(left, "gx", ring(slabs, -1))

    rest, inner = pl.pallas_call(
        inner_kernel,
        out_shape=(struct((19, 4 * ROWS, 128), F32), struct((6, 608, 256), BF16)),
        in_specs=[VM, VM, VM],
        out_specs=(ANY, VM),
        scratch_shapes=[
            pltpu.VMEM((19, 16 * ROWS, 128), F32),
            pltpu.VMEM((19, 14 * ROWS, 128), F32),
            pltpu.SemaphoreType.DMA((2,)),
        ],
        compiler_params=limit(20),
        cost_estimate=cost(6),
        name="inner",
    )(c1, cy, rate)

    outer, send = pl.pallas_call(
        step_kernel,
        out_shape=(struct((2, 608, 256), BF16), pltpu.HBM((devices, 80, 128), BF16)),
        in_specs=[SM, SM, ANY] + [VM] * 6,
        out_specs=(VM, HBM),
        scratch_shapes=[
            pltpu.VMEM((19, 8 * ROWS, 128), F32),
            pltpu.VMEM((19, 8 * ROWS, 128), F32),
            pltpu.VMEM((4, 608, 128), F32),
            pltpu.VMEM((4, 2, 192, 128), F32),
            pltpu.VMEM((BLK, 88, 128), F32),
            pltpu.VMEM((BLK, 80, 128), BF16),
            pltpu.SemaphoreType.DMA,
            pltpu.SemaphoreType.DMA((BLK,)),
        ],
        compiler_params=limit(18),
        cost_estimate=cost(6),
        name="step",
    )(
        refine_flags, new_owner, rest, rim, from_left, from_right, rate,
        jnp.asarray(mean_matrix(), BF16), inner,
    )

    recv = lax.all_to_all(send, ("gx", "yz"), split_axis=0, concat_axis=0, tiled=True)

    owned, kind = pl.pallas_call(
        plan_kernel,
        out_shape=(struct((32, 128), jnp.int32), struct((32, 128), F32)),
        in_specs=[VM, VM, ANY],
        out_specs=(VM, VM),
        scratch_shapes=[pltpu.VMEM((32, 128), F32), pltpu.VMEM((32, 128), F32)],
        compiler_params=limit(4),
        cost_estimate=cost(2),
        name="plan",
    )(refine_flags.reshape(total // 128, 128), new_owner.reshape(total // 128, 128), outer)

    half = pl.pallas_call(
        keep_kernel,
        out_shape=pltpu.HBM((19, CAP, 4096), BF16),
        in_specs=[SM, SM, VM, VM],
        out_specs=VM,
        scratch_shapes=[
            pltpu.VMEM((4, 192, 128), F32),
            pltpu.VMEM((32, (CAP + 1) * 24, 128), F32),
            pltpu.SMEM((BLK,), jnp.int32),
        ],
        compiler_params=limit(20),
        cost_estimate=cost(10),
        name="keep",
    )(refine_flags, owned, inner, outer)

    migrated = pl.pallas_call(
        refine_kernel,
        out_shape=struct((19, CAP, 4096), BF16),
        in_specs=[SM, SM, ANY, VM, VM, HBM],
        out_specs=ANY,
        scratch_shapes=[
            pltpu.VMEM((CAP, 80, 128), BF16),
            pltpu.VMEM((CAP * 80, 128), F32),
            pltpu.VMEM((4, 456, 256), BF16),
            pltpu.VMEM((4, 456, 512), F32),
            pltpu.VMEM((19, CAP, 4096), BF16),
            pltpu.VMEM((19, CAP, 4096), BF16),
            pltpu.SemaphoreType.DMA((CAP,)),
            pltpu.SemaphoreType.DMA((19,)),
            pltpu.SemaphoreType.DMA((19,)),
        ],
        compiler_params=limit(18),
        cost_estimate=cost(5),
        name="refine",
    )(refine_flags, owned, recv, kind, jnp.asarray(expand_matrix(), BF16), in_hbm(half))
    return jnp.transpose(migrated, (1, 0, 2))


def solution(mesh):
    placed = (P(None, "gx", "yz", None), P(), P(), P())
    return jax.shard_map(
        body, mesh=mesh, in_specs=placed, out_specs=P(("gx", "yz"), None, None), check_vma=False
    )
```

```python
import jax
import jax.numpy as jnp
import numpy as np
from jax import lax
from jax.experimental import pallas as pl
from jax.experimental.pallas import tpu as pltpu
from jax.sharding import PartitionSpec as P

BS = 16
BZ = 8
CAP = 24
BLK = 16
ROWS = 48
F32 = jnp.float32
BF16 = jnp.bfloat16

VEL = [
    (0, 0, 0),
    (1, 0, 0), (-1, 0, 0), (0, 1, 0), (0, -1, 0), (0, 0, 1), (0, 0, -1),
    (1, 1, 0), (-1, -1, 0), (1, -1, 0), (-1, 1, 0),
    (1, 0, 1), (-1, 0, -1), (1, 0, -1), (-1, 0, 1),
    (0, 1, 1), (0, -1, -1), (0, 1, -1), (0, -1, 1),
]
OPP = [0, 2, 1, 4, 3, 6, 5, 8, 7, 10, 9, 12, 11, 14, 13, 16, 15, 18, 17]
PLUS = [i for i in range(19) if VEL[i][0] == 1]
MINUS = [i for i in range(19) if VEL[i][0] == -1]
FLAT = [i for i in range(19) if VEL[i][0] == 0]
RIGHTWARD = [(i, 2) for i in PLUS] + [(i, 1) for i in PLUS + FLAT + [12, 14]]
LEFTWARD = [(i, 2) for i in MINUS] + [(i, 1) for i in MINUS + FLAT + [11, 13]]
FACES = len(RIGHTWARD)
FROWS = 40
HALO_Y = ((0, 32), (1, 33), (6, -2), (7, -1))


def collide(h, r):
    p = {}
    d = {}
    for a in range(1, 19, 2):
        p[a] = h[a] + h[a + 1]
        d[a] = h[a] - h[a + 1]
    axis = p[1] + p[3] + p[5]
    diag = (p[7] + p[9]) + (p[11] + p[13]) + (p[15] + p[17])
    rho = 1.0 + (h[0] * (1.0 / 3.0) + axis * (1.0 / 18.0) + diag * (1.0 / 36.0))
    mx = (2.0 * d[1] + (d[7] + d[9]) + (d[11] + d[13])) * (1.0 / 36.0)
    my = (2.0 * d[3] + (d[7] - d[9]) + (d[15] + d[17])) * (1.0 / 36.0)
    mz = (2.0 * d[5] + (d[11] - d[13]) + (d[15] - d[17])) * (1.0 / 36.0)
    inv = 1.0 / rho
    ux, uy, uz = mx * inv, my * inv, mz * inv
    square = ux * ux + uy * uy + uz * uz
    keep = 1.0 - r
    base = r * (rho * (1.0 - 1.5 * square) - 1.0)
    quad = (4.5 * r) * rho
    lin = (3.0 * r) * rho
    proj = {
        1: ux, 3: uy, 5: uz, 7: ux + uy, 9: ux - uy, 11: ux + uz, 13: ux - uz, 15: uy + uz, 17: uy - uz,
    }
    out = [keep * h[0] + base] + [None] * 18
    for a in range(1, 19, 2):
        even = base + quad * (proj[a] * proj[a])
        odd = lin * proj[a]
        out[a] = keep * h[a] + (even + odd)
        out[a + 1] = keep * h[a + 1] + (even - odd)
    return out


def rate_kernel(levels_ref, rate_ref):
    slab, column = lax.axis_index("gx"), lax.axis_index("yz")
    slabs, columns = lax.axis_size("gx"), lax.axis_size("yz")
    group = lax.broadcasted_iota(jnp.int32, (8, 128), 1) // BS
    for plane in range(3):
        row = lax.rem(slab + (plane + slabs - 1), slabs) * (2 * columns)
        for band, (first, last) in enumerate(((0, 8), (8, 24), (24, 40), (40, 48))):
            start = (row + lax.rem(2 * column + (band + 2 * columns - 1), 2 * columns)) * BZ
            level = jnp.zeros((8, 128), F32)
            for z in range(BZ):
                level = jnp.where(group == z, levels_ref[start + z].astype(F32), level)
            rate = 1.0 / (0.5 + jnp.exp2(-level))
            for at in range(first, last, 8):
                rate_ref[plane, at : at + 8, :] = rate


def plan_kernel(flags_ref, owner_ref, after_ref, owned_ref, kind_ref, part, kinds):
    del after_ref
    me = lax.axis_index("gx") * lax.axis_size("yz") + lax.axis_index("yz")
    rows = owner_ref.shape[0]
    mine = owner_ref[...] == me
    mask = jnp.where(mine, 1.0, 0.0)
    upper = lax.broadcasted_iota(jnp.int32, (128, 128), 0) <= lax.broadcasted_iota(jnp.int32, (128, 128), 1)
    before = lax.broadcasted_iota(jnp.int32, (rows, rows), 1) < lax.broadcasted_iota(jnp.int32, (rows, rows), 0)
    prefix = jnp.dot(mask.astype(BF16), jnp.where(upper, 1.0, 0.0).astype(BF16), preferred_element_type=F32)
    total = jnp.broadcast_to(jnp.sum(mask, axis=1, keepdims=True), (rows, 128))
    offset = jnp.dot(jnp.where(before, 1.0, 0.0).astype(BF16), total.astype(BF16), preferred_element_type=F32)
    rank = prefix + offset
    ids = lax.broadcasted_iota(jnp.int32, (rows, 128), 0) * 128 + lax.broadcasted_iota(jnp.int32, (rows, 128), 1)
    marked = jnp.where(mine, ids.astype(F32) + 1.0, 0.0)
    flagged = jnp.where(mine, flags_ref[...].astype(F32), 0.0)
    part[...] = jnp.zeros_like(part)
    kinds[...] = jnp.zeros_like(kinds)
    for slot in range(CAP):
        hit = rank == float(slot + 1)
        part[slot : slot + 1, :] = jnp.sum(jnp.where(hit, marked, 0.0), axis=0, keepdims=True)
        kinds[slot : slot + 1, :] = jnp.sum(jnp.where(hit, flagged, 0.0), axis=0, keepdims=True)
    found = jnp.sum(part[...], axis=1, keepdims=True) - 1.0
    owned_ref[...] = jnp.broadcast_to(found, part.shape).astype(jnp.int32)
    kind_ref[...] = jnp.broadcast_to(jnp.sum(kinds[...], axis=1, keepdims=True), kinds.shape)


def collide_kernel(pop_ref, rate_ref, c1_ref, planes, sem):
    def fetch(part):
        at = pl.ds(part * 4, 4)
        return pltpu.make_async_copy(pop_ref.at[:, at], planes.at[:, at], sem.at[part])

    for part in range(4):
        fetch(part).start()

    @pl.loop(0, 4)
    def _(part):
        fetch(part).wait()

        @pl.loop(0, 4)
        def _(step):
            x = part * 4 + step
            for t in range(4):
                rows = slice(8 * t, 8 * t + 8)
                h = [planes[i, x, rows, :].astype(F32) for i in range(19)]
                out = collide(h, rate_ref[1, 8 + 8 * t : 16 + 8 * t, :])
                for i in range(19):
                    c1_ref[i, x, rows, :] = out[i].astype(BF16)


def face_kernel(c1_ref, low_ref, high_ref, rate_ref, cy_ref, rim_ref, right_ref, left_ref, planes, edge, sem):
    copies = [
        pltpu.make_async_copy(c1_ref.at[:, a : a + 2], planes.at[:, b : b + 2], sem.at[n])
        for n, (a, b) in enumerate(((0, 0), (14, 2)))
    ]
    for copy in copies:
        copy.start()

    for slot, y in HALO_Y:
        source = low_ref if y < 0 else high_ref
        row = y + 2 if y < 0 else y - 32
        rate = jnp.broadcast_to(rate_ref[1, y + 8 : y + 9, :], (8, 128))

        @pl.loop(0, 2)
        def _(half):
            start = pl.multiple_of(half * 8, 8)
            h = [source[i, row, pl.ds(start, 8), :].astype(F32) for i in range(19)]
            out = collide(h, rate)
            for i in range(19):
                edge[pl.ds(pl.multiple_of((i * 8 + slot) * 16 + start, 8), 8), :] = out[i]
                cy_ref[i, slot, pl.ds(start, 8), :] = out[i].astype(BF16)

    for copy in copies:
        copy.wait()
    for i in range(19):
        for n, plane in enumerate((0, 1, 14, 15)):
            body_rows = planes[i, n, :, :]
            ends = edge[pl.ds(i * 128 + plane, 8, stride=16), :].astype(BF16)
            rim_ref[i, n, 0:32, :] = body_rows
            rim_ref[i, n, 32:40, :] = ends
            for ref, faces, depth in ((right_ref, RIGHTWARD, 16 - plane), (left_ref, LEFTWARD, plane + 1)):
                if (i, depth) in faces:
                    at = faces.index((i, depth))
                    ref[at, 0:32, :] = body_rows
                    ref[at, 32:40, :] = ends


def shifted(ref, at, lane):
    out = []
    for i in range(19):
        dx, dy, dz = VEL[i]
        v = ref[i, pl.ds(at(-dx, -dy), 8), :]
        if dz == 1:
            v = jnp.where(lane == 0, ref[OPP[i], pl.ds(at(0, 0), 8), :], pltpu.roll(v, 1, axis=1))
        elif dz == -1:
            v = jnp.where(lane == 127, ref[OPP[i], pl.ds(at(0, 0), 8), :], pltpu.roll(v, 127, axis=1))
        out.append(v)
    return out


def advance(source, at, rate, target, row, lane):
    out = collide(shifted(source, at, lane), rate)
    for i in range(19):
        target[i, pl.ds(row, 8), :] = out[i]


def settle(source, base, target, part, lanes, lane):
    for yh in range(4):
        def at(dx, dy, yh=yh):
            return base + ((dx + 1) * ROWS + 8 + 8 * yh + dy)

        h = shifted(source, at, lane)
        for i in range(19):
            target[part, 32 * i + 8 * yh : 32 * i + 8 * yh + 8, lanes] = h[i].astype(BF16)


def inner_kernel(
    c1_ref, cy_ref, rate_ref, reduce_ref, rest_ref, state_ref, middle_ref, first, second, mean, mix, sem
):
    lane = lax.broadcasted_iota(jnp.int32, (8, 128), 1)

    @pl.loop(0, 16)
    def _(x):
        for i in range(19):
            first[i, pl.ds(pl.multiple_of(x * ROWS + 8, 8), 32), :] = c1_ref[i, x, :, :].astype(F32)

    for slot, y in HALO_Y:
        for i in range(19):
            for half in range(2):
                first[i, pl.ds(8 * half * ROWS + y + 8, 8, stride=ROWS), :] = cy_ref[
                    i, slot, 8 * half : 8 * half + 8, :
                ].astype(F32)

    @pl.loop(0, 14)
    def _(p):
        base = pl.multiple_of(p * ROWS, 8)
        for t in range(5):
            def at(dx, dy, t=t):
                return base + ((dx + 1) * ROWS + 7 + 8 * t + dy)

            advance(first, at, rate_ref[1, 7 + 8 * t : 15 + 8 * t, :], second, base + (7 + 8 * t), lane)

    copies = [
        pltpu.make_async_copy(
            second.at[:, a * ROWS : (a + 2) * ROWS], rest_ref.at[:, b * ROWS : (b + 2) * ROWS], sem.at[n]
        )
        for n, (a, b) in enumerate(((0, 0), (12, 2)))
    ]
    for copy in copies:
        copy.start()

    @pl.loop(0, 12)
    def _(p):
        lanes = pl.ds(pl.multiple_of((p % 2) * 128, 128), 128)
        settle(second, pl.multiple_of(p * ROWS, 8), state_ref, p // 2, lanes, lane)

    means(
        [(q, state_ref.at[2 * q - 1], state_ref.at[2 * q]) for q in (1, 2)], reduce_ref, mean, mix, middle_ref, lane
    )
    for copy in copies:
        copy.wait()


def butterfly(a, lane, unit):
    for bit in range(3):
        width = unit << bit
        low = (lane & width) == 0
        b = list(a)
        for j in range(8):
            if j & (1 << bit):
                continue
            k = j | (1 << bit)
            b[j] = jnp.where(low, a[j], pltpu.roll(a[k], width, axis=1))
            b[k] = jnp.where(low, pltpu.roll(a[j], 128 - width, axis=1), a[k])
        a = b
    return a


def means(quarters, reduce_ref, mean, mix, pack, lane):
    for n, (q, left, right) in enumerate(quarters):
        mean[n, :, :] = jnp.dot(left[...], reduce_ref[0, :, :], preferred_element_type=F32) + jnp.dot(
            right[...], reduce_ref[1, :, :], preferred_element_type=F32
        )
        for i in range(19):
            for by in range(2):
                at = 32 * i + 16 * by
                mix[n, by, 8 * i : 8 * i + 8, :] = (
                    mean[n, pl.ds(at, 8, stride=2), :] + mean[n, pl.ds(at + 1, 8, stride=2), :]
                )
        for by in range(2):
            for g in range(3):
                a = [mix[n, by, pl.ds(64 * g + y, 8, stride=8), :] for y in range(8)]
                a = butterfly(a, lane, 8)
                for z in range(8):
                    pack[8 * by + z, pl.ds(32 * g + q, 8, stride=4), :] = a[z]


def step_kernel(
    flags_ref, owner_ref, rest_ref, rim_ref, gl_ref, gr_ref, rate_ref, reduce_ref, inner_ref, middle_ref,
    outer_ref, send_ref,
    first, second, mean, mix, pack, stage, in_sem, send_sem,
):
    me = lax.axis_index("gx") * lax.axis_size("yz") + lax.axis_index("yz")
    lane = lax.broadcasted_iota(jnp.int32, (8, 128), 1)
    rest = pltpu.make_async_copy(rest_ref, second.at[:, 2 * ROWS : 6 * ROWS], in_sem)
    rest.start()

    def place(i, at, rows):
        first[i, at * ROWS + 8 : at * ROWS + 40, :] = rows[0:32, :]
        first[i, at * ROWS + 40 : at * ROWS + 48, :] = rows[32:40, :]
        first[i, at * ROWS : at * ROWS + 8, :] = rows[32:40, :]

    for i in range(19):
        for n, at in enumerate((2, 3, 4, 5)):
            place(i, at, rim_ref[i, n, :, :].astype(F32))
    for ref, faces, places in ((gl_ref, RIGHTWARD, (None, 1, 0)), (gr_ref, LEFTWARD, (None, 6, 7))):
        for n, (i, depth) in enumerate(faces):
            place(i, places[depth], ref[n, :, :].astype(F32))

    @pl.loop(0, 4)
    def _(e):
        above = e // 2
        base = pl.multiple_of((e + 2 * above) * ROWS, 8)
        row = pl.multiple_of((e + 4 * above) * ROWS, 8)
        for t in range(5):
            def at(dx, dy, t=t):
                return base + ((dx + 1) * ROWS + 7 + 8 * t + dy)

            advance(first, at, rate_ref[(e + 1) // 2, 7 + 8 * t : 15 + 8 * t, :], second, row + (7 + 8 * t), lane)

    rest.wait()

    @pl.loop(0, 4)
    def _(e):
        above = e // 2
        lanes = pl.ds(pl.multiple_of((e % 2) * 128, 128), 128)
        settle(second, pl.multiple_of((e + 2 * above) * ROWS, 8), outer_ref, above, lanes, lane)

    means(
        [(0, outer_ref.at[0], inner_ref.at[0]), (3, inner_ref.at[5], outer_ref.at[1])],
        reduce_ref, mean, mix, pack, lane,
    )

    quarter = lax.broadcasted_iota(jnp.int32, (4, 128), 0)
    middle = (quarter == 1) | (quarter == 2)

    @pl.loop(0, BLK)
    def _(k):
        @pl.when(flags_ref[me * BLK + k] != 0)
        def _():
            for i in range(19):
                rows = slice(4 * i, 4 * i + 4)
                stage[k, i, :, :] = jnp.where(middle, middle_ref[k, rows, :], pack[k, rows, :]).astype(BF16)
            pltpu.make_async_copy(stage.at[k], send_ref.at[owner_ref[me * BLK + k]], send_sem.at[k]).start()

    @pl.loop(0, BLK)
    def _(k):
        @pl.when(flags_ref[me * BLK + k] != 0)
        def _():
            pltpu.make_async_copy(stage.at[k], send_ref.at[0], send_sem.at[k]).wait()


def keep_kernel(flags_ref, owned_ref, inner_ref, outer_ref, half_ref, mix, slots, place):
    me = lax.axis_index("gx") * lax.axis_size("yz") + lax.axis_index("yz")
    lane = lax.broadcasted_iota(jnp.int32, (8, 128), 1)

    @pl.loop(0, BLK)
    def _(k):
        place[k] = CAP

    @pl.loop(0, CAP)
    def _(s):
        b = owned_ref[s, 0]

        @pl.when((b >= 0) & (flags_ref[jnp.maximum(b, 0)] == 0))
        def _():
            place[b - me * BLK] = s

    @pl.loop(0, 32)
    def _(c):
        for r in range(CAP * 3):
            slots[c, 8 * r : 8 * r + 8, :] = jnp.zeros((8, 128), F32)

    def spread(state_ref, pair, x):
        lanes = pl.ds(pl.multiple_of((x % 2) * 128, 128), 128)
        for yh in range(4):
            for i in range(19):
                tile = state_ref[pair, 32 * i + 8 * yh : 32 * i + 8 * yh + 8, lanes]
                mix[yh, 8 * i : 8 * i + 8, :] = tile.astype(F32)
            for g in range(3):
                a = [mix[yh, pl.ds(64 * g + y, 8, stride=8), :] for y in range(8)]
                a = butterfly(a, lane, 16)
                for z in range(8):
                    row = pl.multiple_of(place[(yh // 2) * 8 + z] * 24 + 8 * g, 8)
                    slots[2 * x + yh % 2, pl.ds(row, 8), :] = a[z]

    @pl.loop(2, 14)
    def _(x):
        spread(inner_ref, x // 2 - 1, x)

    @pl.loop(0, 4)
    def _(e):
        spread(outer_ref, e // 2, e + 12 * (e // 2))

    @pl.loop(0, 32)
    def _(c):
        lanes = pl.ds(pl.multiple_of(c * 128, 128), 128)
        for i in range(19):
            parts = [slots[c, pl.ds(192 * g + i, 8, stride=24), :] for g in range(3)]
            half_ref[i, 0:16, lanes] = jnp.concatenate(parts[:2], axis=0).astype(BF16)
            half_ref[i, 16:24, lanes] = parts[2].astype(BF16)


def refine_kernel(
    flags_ref, owned_ref, recv_ref, kind_ref, expand_ref, half_ref, out_ref,
    taken, rows, wide, product, half, result, in_sem, half_sem, out_sem,
):
    def each_arrival(act):
        @pl.loop(0, CAP)
        def _(s):
            b = owned_ref[s, 0]

            @pl.when((b >= 0) & (flags_ref[jnp.maximum(b, 0)] != 0))
            def _():
                act(s, b // BLK)

    def fetch(s, device):
        pltpu.make_async_copy(recv_ref.at[device], taken.at[s], in_sem.at[s]).start()

    def widen(s, device):
        pltpu.make_async_copy(recv_ref.at[device], taken.at[s], in_sem.at[s]).wait()
        for i in range(19):
            rows[pl.ds(96 * i + s, 4, stride=24), :] = taken[s, i, :, :].astype(F32)

    each_arrival(fetch)

    @pl.loop(0, 19)
    def _(i):
        pltpu.make_async_copy(half_ref.at[i], half.at[i], half_sem.at[i]).start()

    each_arrival(widen)

    kinds = [kind_ref[8 * g : 8 * g + 8, :] for g in range(3)]
    for q in range(4):
        for i in range(19):
            ones, twos = [], []
            for g in range(3):
                start = 24 * (4 * i + q) + 8 * g
                v = rows[start : start + 8, :]
                ones.append(jnp.where(kinds[g] == 1.0, v, 0.0))
                twos.append(jnp.where(kinds[g] == 2.0, v, 0.0))
            for start, v in ((0, ones), (128, twos)):
                wide[q, 24 * i : 24 * i + 16, start : start + 128] = jnp.concatenate(v[:2], axis=0).astype(BF16)
                wide[q, 24 * i + 16 : 24 * i + 24, start : start + 128] = v[2].astype(BF16)
        product[q, :, :] = jnp.dot(wide[q, :, :], expand_ref[...], preferred_element_type=F32)

    linear = jnp.concatenate([jnp.concatenate([k, k], axis=1) for k in kinds], axis=0) == 2.0
    near = jnp.where(linear, 0.75, 1.0)
    far = jnp.where(linear, 0.25, 0.0)

    @pl.loop(0, 19)
    def _(i):
        pltpu.make_async_copy(half_ref.at[i], half.at[i], half_sem.at[i]).wait()
        start = pl.multiple_of(i * 24, 8)

        def plane(c):
            return product[c // 2, pl.ds(start, 24), (c % 2) * 256 : (c % 2) * 256 + 256]

        for c in range(8):
            mid = plane(c) * near
            for odd in range(2):
                other = max(c - 1, 0) if odd == 0 else min(c + 1, 7)
                x = slice((2 * c + odd) * 256, (2 * c + odd) * 256 + 256)
                result[i, :, x] = (mid + plane(other) * far).astype(BF16) + half[i, :, x]
        pltpu.make_async_copy(result.at[i], out_ref.at[i], out_sem.at[i]).start()

    @pl.loop(0, 19)
    def _(i):
        pltpu.make_async_copy(result.at[i], out_ref.at[i], out_sem.at[i]).wait()


def mean_matrix():
    half = np.zeros((128, 64), np.float32)
    half[np.arange(128), np.arange(128) // 2] = 0.125
    both = np.concatenate([half, half], axis=0)
    none = np.zeros_like(both)
    return np.stack([np.concatenate([both, none], axis=1), np.concatenate([none, both], axis=1)])


def expand_matrix():
    inject = np.zeros((8, 16), np.float32)
    linear = np.zeros((8, 16), np.float32)
    for k in range(8):
        for odd, other in ((0, max(k - 1, 0)), (1, min(k + 1, 7))):
            inject[k, 2 * k + odd] = 1.0
            linear[k, 2 * k + odd] += 0.75
            linear[other, 2 * k + odd] += 0.25
    eye = np.eye(2, dtype=np.float32)
    return np.concatenate([np.kron(eye, np.kron(m, m)) for m in (inject, linear)], axis=0)


def ring(count, step):
    return [(i, (i + step) % count) for i in range(count)]


VM = pl.BlockSpec(memory_space=pltpu.VMEM)
SM = pl.BlockSpec(memory_space=pltpu.SMEM)
ANY = pl.BlockSpec(memory_space=pl.ANY)
HBM = pl.BlockSpec(memory_space=pltpu.HBM)


def struct(shape, dtype):
    return jax.ShapeDtypeStruct(shape, dtype)


def in_hbm(array):
    return pltpu.with_memory_space_constraint(array, pltpu.HBM)


def cost(microseconds):
    return pl.CostEstimate(flops=0, bytes_accessed=int(microseconds * 3.0e6), transcendentals=0)


def limit(mebibytes):
    return pltpu.CompilerParams(vmem_limit_bytes=mebibytes << 20)


def body(populations, levels, refine_flags, new_owner):
    columns = lax.axis_size("yz")
    slabs = lax.axis_size("gx")
    total = new_owner.shape[0]
    devices = slabs * columns

    top = jnp.transpose(populations[:, :, 30:32, :], (0, 2, 1, 3))
    bottom = jnp.transpose(populations[:, :, 0:2, :], (0, 2, 1, 3))
    low = lax.ppermute(top, "yz", ring(columns, 1))
    high = lax.ppermute(bottom, "yz", ring(columns, -1))

    rate = pl.pallas_call(
        rate_kernel,
        out_shape=struct((3, ROWS, 128), F32),
        in_specs=[SM],
        out_specs=VM,
        compiler_params=limit(4),
        cost_estimate=cost(1),
        name="rates",
    )(in_hbm(levels))

    c1 = pl.pallas_call(
        collide_kernel,
        out_shape=struct((19, 16, 32, 128), BF16),
        in_specs=[HBM, VM],
        out_specs=VM,
        scratch_shapes=[pltpu.VMEM((19, 16, 32, 128), BF16), pltpu.SemaphoreType.DMA((4,))],
        compiler_params=limit(8),
        cost_estimate=cost(5),
        name="collide",
    )(in_hbm(populations), rate)

    cy, rim, right, left = pl.pallas_call(
        face_kernel,
        out_shape=(
            struct((19, 8, 16, 128), BF16),
            struct((19, 4, FROWS, 128), BF16),
            struct((FACES, FROWS, 128), BF16),
            struct((FACES, FROWS, 128), BF16),
        ),
        in_specs=[ANY, VM, VM, VM],
        out_specs=(VM,) * 4,
        scratch_shapes=[
            pltpu.VMEM((19, 4, 32, 128), BF16),
            pltpu.VMEM((19 * 128 + 128, 128), F32),
            pltpu.SemaphoreType.DMA((2,)),
        ],
        compiler_params=limit(8),
        cost_estimate=cost(2),
        name="faces",
    )(c1, low, high, rate)

    from_left = lax.ppermute(right, "gx", ring(slabs, 1))
    from_right = lax.ppermute(left, "gx", ring(slabs, -1))

    reduce = jnp.asarray(mean_matrix(), BF16)
    rest, inner, middle = pl.pallas_call(
        inner_kernel,
        out_shape=(
            struct((19, 4 * ROWS, 128), F32),
            struct((6, 608, 256), BF16),
            struct((BLK, 96, 128), F32),
        ),
        in_specs=[VM] * 4,
        out_specs=(ANY, VM, VM),
        scratch_shapes=[
            pltpu.VMEM((19, 16 * ROWS, 128), F32),
            pltpu.VMEM((19, 14 * ROWS, 128), F32),
            pltpu.VMEM((2, 608, 128), F32),
            pltpu.VMEM((2, 2, 192, 128), F32),
            pltpu.SemaphoreType.DMA((2,)),
        ],
        compiler_params=limit(22),
        cost_estimate=cost(6),
        name="inner",
    )(c1, cy, rate, reduce)

    outer, send = pl.pallas_call(
        step_kernel,
        out_shape=(struct((2, 608, 256), BF16), pltpu.HBM((devices, 19, 4, 128), BF16)),
        in_specs=[SM, SM, ANY] + [VM] * 7,
        out_specs=(VM, HBM),
        scratch_shapes=[
            pltpu.VMEM((19, 8 * ROWS, 128), F32),
            pltpu.VMEM((19, 8 * ROWS, 128), F32),
            pltpu.VMEM((2, 608, 128), F32),
            pltpu.VMEM((2, 2, 192, 128), F32),
            pltpu.VMEM((BLK, 96, 128), F32),
            pltpu.VMEM((BLK, 19, 4, 128), BF16),
            pltpu.SemaphoreType.DMA,
            pltpu.SemaphoreType.DMA((BLK,)),
        ],
        compiler_params=limit(18),
        cost_estimate=cost(6),
        name="step",
    )(
        refine_flags, new_owner, rest, rim, from_left, from_right, rate, reduce, inner, middle,
    )

    recv = lax.all_to_all(send, ("gx", "yz"), split_axis=0, concat_axis=0, tiled=True)

    owned, kind = pl.pallas_call(
        plan_kernel,
        out_shape=(struct((32, 128), jnp.int32), struct((32, 128), F32)),
        in_specs=[VM, VM, ANY],
        out_specs=(VM, VM),
        scratch_shapes=[pltpu.VMEM((32, 128), F32), pltpu.VMEM((32, 128), F32)],
        compiler_params=limit(4),
        cost_estimate=cost(2),
        name="plan",
    )(refine_flags.reshape(total // 128, 128), new_owner.reshape(total // 128, 128), outer)

    half = pl.pallas_call(
        keep_kernel,
        out_shape=pltpu.HBM((19, CAP, 4096), BF16),
        in_specs=[SM, SM, VM, VM],
        out_specs=VM,
        scratch_shapes=[
            pltpu.VMEM((4, 192, 128), F32),
            pltpu.VMEM((32, (CAP + 1) * 24, 128), F32),
            pltpu.SMEM((BLK,), jnp.int32),
        ],
        compiler_params=limit(20),
        cost_estimate=cost(10),
        name="keep",
    )(refine_flags, owned, inner, outer)

    migrated = pl.pallas_call(
        refine_kernel,
        out_shape=struct((19, CAP, 4096), BF16),
        in_specs=[SM, SM, ANY, VM, VM, HBM],
        out_specs=ANY,
        scratch_shapes=[
            pltpu.VMEM((CAP, 19, 4, 128), BF16),
            pltpu.VMEM((CAP * 76, 128), F32),
            pltpu.VMEM((4, 456, 256), BF16),
            pltpu.VMEM((4, 456, 512), F32),
            pltpu.VMEM((19, CAP, 4096), BF16),
            pltpu.VMEM((19, CAP, 4096), BF16),
            pltpu.SemaphoreType.DMA((CAP,)),
            pltpu.SemaphoreType.DMA((19,)),
            pltpu.SemaphoreType.DMA((19,)),
        ],
        compiler_params=limit(18),
        cost_estimate=cost(5),
        name="refine",
    )(refine_flags, owned, in_hbm(recv), kind, jnp.asarray(expand_matrix(), BF16), in_hbm(half))
    return jnp.transpose(migrated, (1, 0, 2))


def solution(mesh):
    placed = (P(None, "gx", "yz", None), P(), P(), P())
    return jax.shard_map(
        body, mesh=mesh, in_specs=placed, out_specs=P(("gx", "yz"), None, None), check_vma=False
    )
```

```python
import jax
import jax.numpy as jnp
import numpy as np
from jax import lax
from jax.experimental import pallas as pl
from jax.experimental.pallas import tpu as pltpu
from jax.sharding import PartitionSpec as P

BS = 16
BZ = 8
CAP = 24
BLK = 16
ROWS = 48
F32 = jnp.float32
BF16 = jnp.bfloat16

VEL = [
    (0, 0, 0),
    (1, 0, 0), (-1, 0, 0), (0, 1, 0), (0, -1, 0), (0, 0, 1), (0, 0, -1),
    (1, 1, 0), (-1, -1, 0), (1, -1, 0), (-1, 1, 0),
    (1, 0, 1), (-1, 0, -1), (1, 0, -1), (-1, 0, 1),
    (0, 1, 1), (0, -1, -1), (0, 1, -1), (0, -1, 1),
]
OPP = [0, 2, 1, 4, 3, 6, 5, 8, 7, 10, 9, 12, 11, 14, 13, 16, 15, 18, 17]
PLUS = [i for i in range(19) if VEL[i][0] == 1]
MINUS = [i for i in range(19) if VEL[i][0] == -1]
FLAT = [i for i in range(19) if VEL[i][0] == 0]
RIGHTWARD = [(i, 2) for i in PLUS] + [(i, 1) for i in PLUS + FLAT]
LEFTWARD = [(i, 2) for i in MINUS] + [(i, 1) for i in MINUS + FLAT]
FACES = len(RIGHTWARD)
FROWS = 40
HALO_Y = ((0, 32), (1, 33), (6, -2), (7, -1))


def collide(h, r):
    p = {}
    d = {}
    for a in range(1, 19, 2):
        p[a] = h[a] + h[a + 1]
        d[a] = h[a] - h[a + 1]
    axis = p[1] + p[3] + p[5]
    diag = (p[7] + p[9]) + (p[11] + p[13]) + (p[15] + p[17])
    rho = 1.0 + (h[0] * (1.0 / 3.0) + axis * (1.0 / 18.0) + diag * (1.0 / 36.0))
    mx = (2.0 * d[1] + (d[7] + d[9]) + (d[11] + d[13])) * (1.0 / 36.0)
    my = (2.0 * d[3] + (d[7] - d[9]) + (d[15] + d[17])) * (1.0 / 36.0)
    mz = (2.0 * d[5] + (d[11] - d[13]) + (d[15] - d[17])) * (1.0 / 36.0)
    inv = 1.0 / rho
    ux, uy, uz = mx * inv, my * inv, mz * inv
    square = ux * ux + uy * uy + uz * uz
    keep = 1.0 - r
    base = r * (rho * (1.0 - 1.5 * square) - 1.0)
    quad = (4.5 * r) * rho
    lin = (3.0 * r) * rho
    proj = {
        1: ux, 3: uy, 5: uz, 7: ux + uy, 9: ux - uy, 11: ux + uz, 13: ux - uz, 15: uy + uz, 17: uy - uz,
    }
    out = [keep * h[0] + base] + [None] * 18
    for a in range(1, 19, 2):
        even = base + quad * (proj[a] * proj[a])
        odd = lin * proj[a]
        out[a] = keep * h[a] + (even + odd)
        out[a + 1] = keep * h[a + 1] + (even - odd)
    return out


def rate_kernel(levels_ref, rate_ref):
    slab, column = lax.axis_index("gx"), lax.axis_index("yz")
    slabs, columns = lax.axis_size("gx"), lax.axis_size("yz")
    group = lax.broadcasted_iota(jnp.int32, (8, 128), 1) // BS
    for plane in range(3):
        row = lax.rem(slab + (plane + slabs - 1), slabs) * (2 * columns)
        for band, (first, last) in enumerate(((0, 8), (8, 24), (24, 40), (40, 48))):
            start = (row + lax.rem(2 * column + (band + 2 * columns - 1), 2 * columns)) * BZ
            level = jnp.zeros((8, 128), F32)
            for z in range(BZ):
                level = jnp.where(group == z, levels_ref[start + z].astype(F32), level)
            rate = 1.0 / (0.5 + jnp.exp2(-level))
            for at in range(first, last, 8):
                rate_ref[plane, at : at + 8, :] = rate


def plan_kernel(flags_ref, owner_ref, after_ref, owned_ref, kind_ref, part, kinds):
    del after_ref
    me = lax.axis_index("gx") * lax.axis_size("yz") + lax.axis_index("yz")
    rows = owner_ref.shape[0]
    mine = owner_ref[...] == me
    mask = jnp.where(mine, 1.0, 0.0)
    upper = lax.broadcasted_iota(jnp.int32, (128, 128), 0) <= lax.broadcasted_iota(jnp.int32, (128, 128), 1)
    before = lax.broadcasted_iota(jnp.int32, (rows, rows), 1) < lax.broadcasted_iota(jnp.int32, (rows, rows), 0)
    prefix = jnp.dot(mask.astype(BF16), jnp.where(upper, 1.0, 0.0).astype(BF16), preferred_element_type=F32)
    total = jnp.broadcast_to(jnp.sum(mask, axis=1, keepdims=True), (rows, 128))
    offset = jnp.dot(jnp.where(before, 1.0, 0.0).astype(BF16), total.astype(BF16), preferred_element_type=F32)
    rank = prefix + offset
    ids = lax.broadcasted_iota(jnp.int32, (rows, 128), 0) * 128 + lax.broadcasted_iota(jnp.int32, (rows, 128), 1)
    marked = jnp.where(mine, ids.astype(F32) + 1.0, 0.0)
    flagged = jnp.where(mine, flags_ref[...].astype(F32), 0.0)
    part[...] = jnp.zeros_like(part)
    kinds[...] = jnp.zeros_like(kinds)
    for slot in range(CAP):
        hit = rank == float(slot + 1)
        part[slot : slot + 1, :] = jnp.sum(jnp.where(hit, marked, 0.0), axis=0, keepdims=True)
        kinds[slot : slot + 1, :] = jnp.sum(jnp.where(hit, flagged, 0.0), axis=0, keepdims=True)
    found = jnp.sum(part[...], axis=1, keepdims=True) - 1.0
    owned_ref[...] = jnp.broadcast_to(found, part.shape).astype(jnp.int32)
    kind_ref[...] = jnp.broadcast_to(jnp.sum(kinds[...], axis=1, keepdims=True), kinds.shape)


def collide_kernel(pop_ref, rate_ref, c1_ref, planes, sem):
    def fetch(part):
        at = pl.ds(part * 4, 4)
        return pltpu.make_async_copy(pop_ref.at[:, at], planes.at[:, at], sem.at[part])

    for part in range(4):
        fetch(part).start()

    @pl.loop(0, 4)
    def _(part):
        fetch(part).wait()

        @pl.loop(0, 4)
        def _(step):
            x = part * 4 + step
            for t in range(4):
                rows = slice(8 * t, 8 * t + 8)
                h = [planes[i, x, rows, :].astype(F32) for i in range(19)]
                out = collide(h, rate_ref[1, 8 + 8 * t : 16 + 8 * t, :])
                for i in range(19):
                    c1_ref[i, x, rows, :] = out[i].astype(BF16)


def turn(rows, turned, dz):
    lane = lax.broadcasted_iota(jnp.int32, rows.shape, 1)
    if dz == 1:
        rows = jnp.where(lane == 127, pltpu.roll(turned, 127, axis=1), rows)
    else:
        rows = jnp.where(lane == 0, pltpu.roll(turned, 1, axis=1), rows)
    return rows.astype(BF16)


def face_kernel(c1_ref, low_ref, high_ref, rate_ref, cy_ref, rim_ref, right_ref, left_ref, planes, edge, sem):
    copies = [
        pltpu.make_async_copy(c1_ref.at[:, a : a + 2], planes.at[:, b : b + 2], sem.at[n])
        for n, (a, b) in enumerate(((0, 0), (14, 2)))
    ]
    for copy in copies:
        copy.start()

    for slot, y in HALO_Y:
        source = low_ref if y < 0 else high_ref
        row = y + 2 if y < 0 else y - 32
        rate = jnp.broadcast_to(rate_ref[1, y + 8 : y + 9, :], (8, 128))

        @pl.loop(0, 2)
        def _(half):
            start = pl.multiple_of(half * 8, 8)
            h = [source[i, row, pl.ds(start, 8), :].astype(F32) for i in range(19)]
            out = collide(h, rate)
            for i in range(19):
                edge[pl.ds(pl.multiple_of((i * 8 + slot) * 16 + start, 8), 8), :] = out[i]
                cy_ref[i, slot, pl.ds(start, 8), :] = out[i].astype(BF16)

    for copy in copies:
        copy.wait()
    for i in range(19):
        for n, plane in enumerate((0, 1, 14, 15)):
            body_rows = planes[i, n, :, :]
            ends = edge[pl.ds(i * 128 + plane, 8, stride=16), :].astype(BF16)
            rim_ref[i, n, 0:32, :] = body_rows
            rim_ref[i, n, 32:40, :] = ends
            for ref, faces, depth, outermost in ((right_ref, RIGHTWARD, 16 - plane, 3), (left_ref, LEFTWARD, plane + 1, 0)):
                if (i, depth) not in faces:
                    continue
                at = faces.index((i, depth))
                dz = VEL[i][2]
                if depth == 1 or dz == 0:
                    ref[at, 0:32, :] = body_rows
                    ref[at, 32:40, :] = ends
                else:
                    last = (0, 1, 14, 15)[outermost]
                    turned = edge[pl.ds(OPP[i] * 128 + last, 8, stride=16), :]
                    ref[at, 0:32, :] = turn(body_rows.astype(F32), planes[OPP[i], outermost, :, :].astype(F32), dz)
                    ref[at, 32:40, :] = turn(ends.astype(F32), turned, dz)


def shifted(ref, at, lane):
    out = []
    for i in range(19):
        dx, dy, dz = VEL[i]
        v = ref[i, pl.ds(at(-dx, -dy), 8), :]
        if dz == 1:
            v = jnp.where(lane == 0, ref[OPP[i], pl.ds(at(0, 0), 8), :], pltpu.roll(v, 1, axis=1))
        elif dz == -1:
            v = jnp.where(lane == 127, ref[OPP[i], pl.ds(at(0, 0), 8), :], pltpu.roll(v, 127, axis=1))
        out.append(v)
    return out


def advance(source, at, rate, target, row, lane):
    out = collide(shifted(source, at, lane), rate)
    for i in range(19):
        target[i, pl.ds(row, 8), :] = out[i]


def settle(source, base, target, part, lanes, lane):
    for yh in range(4):
        def at(dx, dy, yh=yh):
            return base + ((dx + 1) * ROWS + 8 + 8 * yh + dy)

        h = shifted(source, at, lane)
        for i in range(19):
            target[part, 32 * i + 8 * yh : 32 * i + 8 * yh + 8, lanes] = h[i].astype(BF16)


def inner_kernel(
    c1_ref, cy_ref, rate_ref, reduce_ref, rest_ref, state_ref, middle_ref, first, second, mean, mix, sem
):
    lane = lax.broadcasted_iota(jnp.int32, (8, 128), 1)

    @pl.loop(0, 16)
    def _(x):
        for i in range(19):
            first[i, pl.ds(pl.multiple_of(x * ROWS + 8, 8), 32), :] = c1_ref[i, x, :, :].astype(F32)

    for slot, y in HALO_Y:
        for i in range(19):
            for half in range(2):
                first[i, pl.ds(8 * half * ROWS + y + 8, 8, stride=ROWS), :] = cy_ref[
                    i, slot, 8 * half : 8 * half + 8, :
                ].astype(F32)

    @pl.loop(0, 14)
    def _(p):
        base = pl.multiple_of(p * ROWS, 8)
        for t in range(5):
            def at(dx, dy, t=t):
                return base + ((dx + 1) * ROWS + 7 + 8 * t + dy)

            advance(first, at, rate_ref[1, 7 + 8 * t : 15 + 8 * t, :], second, base + (7 + 8 * t), lane)

    copies = [
        pltpu.make_async_copy(
            second.at[:, a * ROWS : (a + 2) * ROWS], rest_ref.at[:, b * ROWS : (b + 2) * ROWS], sem.at[n]
        )
        for n, (a, b) in enumerate(((0, 0), (12, 2)))
    ]
    for copy in copies:
        copy.start()

    @pl.loop(0, 12)
    def _(p):
        lanes = pl.ds(pl.multiple_of((p % 2) * 128, 128), 128)
        settle(second, pl.multiple_of(p * ROWS, 8), state_ref, p // 2, lanes, lane)

    means(
        [(q, state_ref.at[2 * q - 1], state_ref.at[2 * q]) for q in (1, 2)], reduce_ref, mean, mix, middle_ref, lane
    )
    for copy in copies:
        copy.wait()


def butterfly(a, lane, unit):
    for bit in range(3):
        width = unit << bit
        low = (lane & width) == 0
        b = list(a)
        for j in range(8):
            if j & (1 << bit):
                continue
            k = j | (1 << bit)
            b[j] = jnp.where(low, a[j], pltpu.roll(a[k], width, axis=1))
            b[k] = jnp.where(low, pltpu.roll(a[j], 128 - width, axis=1), a[k])
        a = b
    return a


def means(quarters, reduce_ref, mean, mix, pack, lane):
    for n, (q, left, right) in enumerate(quarters):
        mean[n, :, :] = jnp.dot(left[...], reduce_ref[0, :, :], preferred_element_type=F32) + jnp.dot(
            right[...], reduce_ref[1, :, :], preferred_element_type=F32
        )
        for i in range(19):
            for by in range(2):
                at = 32 * i + 16 * by
                mix[n, by, 8 * i : 8 * i + 8, :] = (
                    mean[n, pl.ds(at, 8, stride=2), :] + mean[n, pl.ds(at + 1, 8, stride=2), :]
                )
        for by in range(2):
            for g in range(3):
                a = [mix[n, by, pl.ds(64 * g + y, 8, stride=8), :] for y in range(8)]
                a = butterfly(a, lane, 8)
                for z in range(8):
                    pack[8 * by + z, pl.ds(32 * g + q, 8, stride=4), :] = a[z]


def step_kernel(
    flags_ref, owner_ref, rest_ref, rim_ref, gl_ref, gr_ref, rate_ref, reduce_ref, inner_ref, middle_ref,
    outer_ref, send_ref,
    first, second, mean, mix, pack, stage, in_sem, send_sem,
):
    me = lax.axis_index("gx") * lax.axis_size("yz") + lax.axis_index("yz")
    lane = lax.broadcasted_iota(jnp.int32, (8, 128), 1)
    rest = pltpu.make_async_copy(rest_ref, second.at[:, 2 * ROWS : 6 * ROWS], in_sem)
    rest.start()

    def place(i, at, rows):
        first[i, at * ROWS + 8 : at * ROWS + 40, :] = rows[0:32, :]
        first[i, at * ROWS + 40 : at * ROWS + 48, :] = rows[32:40, :]
        first[i, at * ROWS : at * ROWS + 8, :] = rows[32:40, :]

    for i in range(19):
        for n, at in enumerate((2, 3, 4, 5)):
            place(i, at, rim_ref[i, n, :, :].astype(F32))
    for ref, faces, places in ((gl_ref, RIGHTWARD, (None, 1, 0)), (gr_ref, LEFTWARD, (None, 6, 7))):
        for n, (i, depth) in enumerate(faces):
            rows = ref[n, :, :].astype(F32)
            place(i, places[depth], rows)
            if depth == 2 and VEL[i][2] != 0:
                place(OPP[i], places[1], pltpu.roll(rows, 1 if VEL[i][2] == 1 else 127, axis=1))

    @pl.loop(0, 4)
    def _(e):
        above = e // 2
        base = pl.multiple_of((e + 2 * above) * ROWS, 8)
        row = pl.multiple_of((e + 4 * above) * ROWS, 8)
        for t in range(5):
            def at(dx, dy, t=t):
                return base + ((dx + 1) * ROWS + 7 + 8 * t + dy)

            advance(first, at, rate_ref[(e + 1) // 2, 7 + 8 * t : 15 + 8 * t, :], second, row + (7 + 8 * t), lane)

    rest.wait()

    @pl.loop(0, 4)
    def _(e):
        above = e // 2
        lanes = pl.ds(pl.multiple_of((e % 2) * 128, 128), 128)
        settle(second, pl.multiple_of((e + 2 * above) * ROWS, 8), outer_ref, above, lanes, lane)

    means(
        [(0, outer_ref.at[0], inner_ref.at[0]), (3, inner_ref.at[5], outer_ref.at[1])],
        reduce_ref, mean, mix, pack, lane,
    )

    quarter = lax.broadcasted_iota(jnp.int32, (4, 128), 0)
    middle = (quarter == 1) | (quarter == 2)

    @pl.loop(0, BLK)
    def _(k):
        @pl.when(flags_ref[me * BLK + k] != 0)
        def _():
            for i in range(19):
                rows = slice(4 * i, 4 * i + 4)
                stage[k, i, :, :] = jnp.where(middle, middle_ref[k, rows, :], pack[k, rows, :]).astype(BF16)
            pltpu.make_async_copy(stage.at[k], send_ref.at[owner_ref[me * BLK + k]], send_sem.at[k]).start()

    @pl.loop(0, BLK)
    def _(k):
        @pl.when(flags_ref[me * BLK + k] != 0)
        def _():
            pltpu.make_async_copy(stage.at[k], send_ref.at[0], send_sem.at[k]).wait()


def keep_kernel(flags_ref, owned_ref, inner_ref, outer_ref, half_ref, mix, slots, place):
    me = lax.axis_index("gx") * lax.axis_size("yz") + lax.axis_index("yz")
    lane = lax.broadcasted_iota(jnp.int32, (8, 128), 1)

    @pl.loop(0, BLK)
    def _(k):
        place[k] = CAP

    @pl.loop(0, CAP)
    def _(s):
        b = owned_ref[s, 0]

        @pl.when((b >= 0) & (flags_ref[jnp.maximum(b, 0)] == 0))
        def _():
            place[b - me * BLK] = s

    @pl.loop(0, 32)
    def _(c):
        for r in range(CAP * 3):
            slots[c, 8 * r : 8 * r + 8, :] = jnp.zeros((8, 128), F32)

    def spread(state_ref, pair, x):
        lanes = pl.ds(pl.multiple_of((x % 2) * 128, 128), 128)
        for yh in range(4):
            for i in range(19):
                tile = state_ref[pair, 32 * i + 8 * yh : 32 * i + 8 * yh + 8, lanes]
                mix[yh, 8 * i : 8 * i + 8, :] = tile.astype(F32)
            for g in range(3):
                a = [mix[yh, pl.ds(64 * g + y, 8, stride=8), :] for y in range(8)]
                a = butterfly(a, lane, 16)
                for z in range(8):
                    row = pl.multiple_of(place[(yh // 2) * 8 + z] * 24 + 8 * g, 8)
                    slots[2 * x + yh % 2, pl.ds(row, 8), :] = a[z]

    @pl.loop(2, 14)
    def _(x):
        spread(inner_ref, x // 2 - 1, x)

    @pl.loop(0, 4)
    def _(e):
        spread(outer_ref, e // 2, e + 12 * (e // 2))

    @pl.loop(0, 32)
    def _(c):
        lanes = pl.ds(pl.multiple_of(c * 128, 128), 128)
        for i in range(19):
            parts = [slots[c, pl.ds(192 * g + i, 8, stride=24), :] for g in range(3)]
            half_ref[i, 0:16, lanes] = jnp.concatenate(parts[:2], axis=0).astype(BF16)
            half_ref[i, 16:24, lanes] = parts[2].astype(BF16)


def refine_kernel(
    flags_ref, owned_ref, recv_ref, kind_ref, expand_ref, half_ref, out_ref,
    rows, wide, product, half, result, half_sem, out_sem,
):
    @pl.loop(0, 19)
    def _(i):
        pltpu.make_async_copy(half_ref.at[i], half.at[i], half_sem.at[i]).start()

    @pl.loop(0, CAP)
    def _(s):
        b = owned_ref[s, 0]

        @pl.when((b >= 0) & (flags_ref[jnp.maximum(b, 0)] != 0))
        def _():
            for i in range(19):
                rows[pl.ds(96 * i + s, 4, stride=24), :] = recv_ref[b // BLK, i, :, :].astype(F32)

    kinds = [kind_ref[8 * g : 8 * g + 8, :] for g in range(3)]
    for q in range(4):
        for i in range(19):
            ones, twos = [], []
            for g in range(3):
                start = 24 * (4 * i + q) + 8 * g
                v = rows[start : start + 8, :]
                ones.append(jnp.where(kinds[g] == 1.0, v, 0.0))
                twos.append(jnp.where(kinds[g] == 2.0, v, 0.0))
            for start, v in ((0, ones), (128, twos)):
                wide[q, 24 * i : 24 * i + 16, start : start + 128] = jnp.concatenate(v[:2], axis=0).astype(BF16)
                wide[q, 24 * i + 16 : 24 * i + 24, start : start + 128] = v[2].astype(BF16)
        product[q, :, :] = jnp.dot(wide[q, :, :], expand_ref[...], preferred_element_type=F32)

    linear = jnp.concatenate([jnp.concatenate([k, k], axis=1) for k in kinds], axis=0) == 2.0
    near = jnp.where(linear, 0.75, 1.0)
    far = jnp.where(linear, 0.25, 0.0)

    @pl.loop(0, 19)
    def _(i):
        pltpu.make_async_copy(half_ref.at[i], half.at[i], half_sem.at[i]).wait()
        start = pl.multiple_of(i * 24, 8)

        def plane(c):
            return product[c // 2, pl.ds(start, 24), (c % 2) * 256 : (c % 2) * 256 + 256]

        for c in range(8):
            mid = plane(c) * near
            for odd in range(2):
                other = max(c - 1, 0) if odd == 0 else min(c + 1, 7)
                x = slice((2 * c + odd) * 256, (2 * c + odd) * 256 + 256)
                result[i, :, x] = (mid + plane(other) * far).astype(BF16) + half[i, :, x]
        pltpu.make_async_copy(result.at[i], out_ref.at[i], out_sem.at[i]).start()

    @pl.loop(0, 19)
    def _(i):
        pltpu.make_async_copy(result.at[i], out_ref.at[i], out_sem.at[i]).wait()


def mean_matrix():
    half = np.zeros((128, 64), np.float32)
    half[np.arange(128), np.arange(128) // 2] = 0.125
    both = np.concatenate([half, half], axis=0)
    none = np.zeros_like(both)
    return np.stack([np.concatenate([both, none], axis=1), np.concatenate([none, both], axis=1)])


def expand_matrix():
    inject = np.zeros((8, 16), np.float32)
    linear = np.zeros((8, 16), np.float32)
    for k in range(8):
        for odd, other in ((0, max(k - 1, 0)), (1, min(k + 1, 7))):
            inject[k, 2 * k + odd] = 1.0
            linear[k, 2 * k + odd] += 0.75
            linear[other, 2 * k + odd] += 0.25
    eye = np.eye(2, dtype=np.float32)
    return np.concatenate([np.kron(eye, np.kron(m, m)) for m in (inject, linear)], axis=0)


def ring(count, step):
    return [(i, (i + step) % count) for i in range(count)]


VM = pl.BlockSpec(memory_space=pltpu.VMEM)
SM = pl.BlockSpec(memory_space=pltpu.SMEM)
ANY = pl.BlockSpec(memory_space=pl.ANY)
HBM = pl.BlockSpec(memory_space=pltpu.HBM)


def struct(shape, dtype):
    return jax.ShapeDtypeStruct(shape, dtype)


def in_hbm(array):
    return pltpu.with_memory_space_constraint(array, pltpu.HBM)


def cost(microseconds):
    return pl.CostEstimate(flops=0, bytes_accessed=int(microseconds * 3.0e6), transcendentals=0)


def limit(mebibytes):
    return pltpu.CompilerParams(vmem_limit_bytes=mebibytes << 20)


def body(populations, levels, refine_flags, new_owner):
    columns = lax.axis_size("yz")
    slabs = lax.axis_size("gx")
    total = new_owner.shape[0]
    devices = slabs * columns

    top = jnp.transpose(populations[:, :, 30:32, :], (0, 2, 1, 3))
    bottom = jnp.transpose(populations[:, :, 0:2, :], (0, 2, 1, 3))
    low = lax.ppermute(top, "yz", ring(columns, 1))
    high = lax.ppermute(bottom, "yz", ring(columns, -1))

    rate = pl.pallas_call(
        rate_kernel,
        out_shape=struct((3, ROWS, 128), F32),
        in_specs=[SM],
        out_specs=VM,
        compiler_params=limit(4),
        cost_estimate=cost(1),
        name="rates",
    )(in_hbm(levels))

    c1 = pl.pallas_call(
        collide_kernel,
        out_shape=struct((19, 16, 32, 128), BF16),
        in_specs=[HBM, VM],
        out_specs=VM,
        scratch_shapes=[pltpu.VMEM((19, 16, 32, 128), BF16), pltpu.SemaphoreType.DMA((4,))],
        compiler_params=limit(8),
        cost_estimate=cost(5),
        name="collide",
    )(in_hbm(populations), rate)

    cy, rim, right, left = pl.pallas_call(
        face_kernel,
        out_shape=(
            struct((19, 8, 16, 128), BF16),
            struct((19, 4, FROWS, 128), BF16),
            struct((FACES, FROWS, 128), BF16),
            struct((FACES, FROWS, 128), BF16),
        ),
        in_specs=[ANY, VM, VM, VM],
        out_specs=(VM,) * 4,
        scratch_shapes=[
            pltpu.VMEM((19, 4, 32, 128), BF16),
            pltpu.VMEM((19 * 128 + 128, 128), F32),
            pltpu.SemaphoreType.DMA((2,)),
        ],
        compiler_params=limit(8),
        cost_estimate=cost(2),
        name="faces",
    )(c1, low, high, rate)

    from_left = lax.ppermute(right, "gx", ring(slabs, 1))
    from_right = lax.ppermute(left, "gx", ring(slabs, -1))

    reduce = jnp.asarray(mean_matrix(), BF16)
    rest, inner, middle = pl.pallas_call(
        inner_kernel,
        out_shape=(
            struct((19, 4 * ROWS, 128), F32),
            struct((6, 608, 256), BF16),
            struct((BLK, 96, 128), F32),
        ),
        in_specs=[VM] * 4,
        out_specs=(ANY, VM, VM),
        scratch_shapes=[
            pltpu.VMEM((19, 16 * ROWS, 128), F32),
            pltpu.VMEM((19, 14 * ROWS, 128), F32),
            pltpu.VMEM((2, 608, 128), F32),
            pltpu.VMEM((2, 2, 192, 128), F32),
            pltpu.SemaphoreType.DMA((2,)),
        ],
        compiler_params=limit(22),
        cost_estimate=cost(6),
        name="inner",
    )(c1, cy, rate, reduce)

    outer, send = pl.pallas_call(
        step_kernel,
        out_shape=(struct((2, 608, 256), BF16), pltpu.HBM((devices, 19, 4, 128), BF16)),
        in_specs=[SM, SM, ANY] + [VM] * 7,
        out_specs=(VM, HBM),
        scratch_shapes=[
            pltpu.VMEM((19, 8 * ROWS, 128), F32),
            pltpu.VMEM((19, 8 * ROWS, 128), F32),
            pltpu.VMEM((2, 608, 128), F32),
            pltpu.VMEM((2, 2, 192, 128), F32),
            pltpu.VMEM((BLK, 96, 128), F32),
            pltpu.VMEM((BLK, 19, 4, 128), BF16),
            pltpu.SemaphoreType.DMA,
            pltpu.SemaphoreType.DMA((BLK,)),
        ],
        compiler_params=limit(18),
        cost_estimate=cost(6),
        name="step",
    )(
        refine_flags, new_owner, rest, rim, from_left, from_right, rate, reduce, inner, middle,
    )

    recv = lax.all_to_all(send, ("gx", "yz"), split_axis=0, concat_axis=0, tiled=True)

    owned, kind = pl.pallas_call(
        plan_kernel,
        out_shape=(struct((32, 128), jnp.int32), struct((32, 128), F32)),
        in_specs=[VM, VM, ANY],
        out_specs=(VM, VM),
        scratch_shapes=[pltpu.VMEM((32, 128), F32), pltpu.VMEM((32, 128), F32)],
        compiler_params=limit(4),
        cost_estimate=cost(2),
        name="plan",
    )(refine_flags.reshape(total // 128, 128), new_owner.reshape(total // 128, 128), outer)

    half = pl.pallas_call(
        keep_kernel,
        out_shape=pltpu.HBM((19, CAP, 4096), BF16),
        in_specs=[SM, SM, VM, VM],
        out_specs=VM,
        scratch_shapes=[
            pltpu.VMEM((4, 192, 128), F32),
            pltpu.VMEM((32, (CAP + 1) * 24, 128), F32),
            pltpu.SMEM((BLK,), jnp.int32),
        ],
        compiler_params=limit(20),
        cost_estimate=cost(10),
        name="keep",
    )(refine_flags, owned, inner, outer)

    migrated = pl.pallas_call(
        refine_kernel,
        out_shape=struct((19, CAP, 4096), BF16),
        in_specs=[SM, SM, VM, VM, VM, HBM],
        out_specs=ANY,
        scratch_shapes=[
            pltpu.VMEM((CAP * 76, 128), F32),
            pltpu.VMEM((4, 456, 256), BF16),
            pltpu.VMEM((4, 456, 512), F32),
            pltpu.VMEM((19, CAP, 4096), BF16),
            pltpu.VMEM((19, CAP, 4096), BF16),
            pltpu.SemaphoreType.DMA((19,)),
            pltpu.SemaphoreType.DMA((19,)),
        ],
        compiler_params=limit(18),
        cost_estimate=cost(5),
        name="refine",
    )(refine_flags, owned, recv, kind, jnp.asarray(expand_matrix(), BF16), in_hbm(half))
    return jnp.transpose(migrated, (1, 0, 2))


def solution(mesh):
    placed = (P(None, "gx", "yz", None), P(), P(), P())
    return jax.shard_map(
        body, mesh=mesh, in_specs=placed, out_specs=P(("gx", "yz"), None, None), check_vma=False
    )
```

```python
import jax
import jax.numpy as jnp
import numpy as np
from jax import lax
from jax.experimental import pallas as pl
from jax.experimental.pallas import tpu as pltpu
from jax.sharding import PartitionSpec as P

BS = 16
BZ = 8
CAP = 24
BLK = 16
ROWS = 48
F32 = jnp.float32
BF16 = jnp.bfloat16

VEL = [
    (0, 0, 0),
    (1, 0, 0), (-1, 0, 0), (0, 1, 0), (0, -1, 0), (0, 0, 1), (0, 0, -1),
    (1, 1, 0), (-1, -1, 0), (1, -1, 0), (-1, 1, 0),
    (1, 0, 1), (-1, 0, -1), (1, 0, -1), (-1, 0, 1),
    (0, 1, 1), (0, -1, -1), (0, 1, -1), (0, -1, 1),
]
OPP = [0, 2, 1, 4, 3, 6, 5, 8, 7, 10, 9, 12, 11, 14, 13, 16, 15, 18, 17]
PLUS = [i for i in range(19) if VEL[i][0] == 1]
MINUS = [i for i in range(19) if VEL[i][0] == -1]
FLAT = [i for i in range(19) if VEL[i][0] == 0]
RIGHTWARD = [(i, 2) for i in PLUS] + [(i, 1) for i in PLUS + FLAT]
LEFTWARD = [(i, 2) for i in MINUS] + [(i, 1) for i in MINUS + FLAT]
FACES = len(RIGHTWARD)
FROWS = 40
HALO_Y = ((0, 32), (1, 33), (6, -2), (7, -1))


def collide(h, r):
    p = {}
    d = {}
    for a in range(1, 19, 2):
        p[a] = h[a] + h[a + 1]
        d[a] = h[a] - h[a + 1]
    axis = p[1] + p[3] + p[5]
    diag = (p[7] + p[9]) + (p[11] + p[13]) + (p[15] + p[17])
    rho = 1.0 + (h[0] * (1.0 / 3.0) + axis * (1.0 / 18.0) + diag * (1.0 / 36.0))
    mx = (2.0 * d[1] + (d[7] + d[9]) + (d[11] + d[13])) * (1.0 / 36.0)
    my = (2.0 * d[3] + (d[7] - d[9]) + (d[15] + d[17])) * (1.0 / 36.0)
    mz = (2.0 * d[5] + (d[11] - d[13]) + (d[15] - d[17])) * (1.0 / 36.0)
    inv = 1.0 / rho
    ux, uy, uz = mx * inv, my * inv, mz * inv
    square = ux * ux + uy * uy + uz * uz
    keep = 1.0 - r
    base = r * (rho * (1.0 - 1.5 * square) - 1.0)
    quad = (4.5 * r) * rho
    lin = (3.0 * r) * rho
    proj = {
        1: ux, 3: uy, 5: uz, 7: ux + uy, 9: ux - uy, 11: ux + uz, 13: ux - uz, 15: uy + uz, 17: uy - uz,
    }
    out = [keep * h[0] + base] + [None] * 18
    for a in range(1, 19, 2):
        even = base + quad * (proj[a] * proj[a])
        odd = lin * proj[a]
        out[a] = keep * h[a] + (even + odd)
        out[a + 1] = keep * h[a + 1] + (even - odd)
    return out


def rate_kernel(levels_ref, rate_ref):
    slab, column = lax.axis_index("gx"), lax.axis_index("yz")
    slabs, columns = lax.axis_size("gx"), lax.axis_size("yz")
    group = lax.broadcasted_iota(jnp.int32, (8, 128), 1) // BS
    for plane in range(3):
        row = lax.rem(slab + (plane + slabs - 1), slabs) * (2 * columns)
        for band, (first, last) in enumerate(((0, 8), (8, 24), (24, 40), (40, 48))):
            start = (row + lax.rem(2 * column + (band + 2 * columns - 1), 2 * columns)) * BZ
            level = jnp.zeros((8, 128), F32)
            for z in range(BZ):
                level = jnp.where(group == z, levels_ref[start + z].astype(F32), level)
            rate = 1.0 / (0.5 + jnp.exp2(-level))
            for at in range(first, last, 8):
                rate_ref[plane, at : at + 8, :] = rate


def plan_kernel(flags_ref, owner_ref, after_ref, owned_ref, kind_ref, part, kinds):
    del after_ref
    me = lax.axis_index("gx") * lax.axis_size("yz") + lax.axis_index("yz")
    rows = owner_ref.shape[0]
    mine = owner_ref[...] == me
    mask = jnp.where(mine, 1.0, 0.0)
    upper = lax.broadcasted_iota(jnp.int32, (128, 128), 0) <= lax.broadcasted_iota(jnp.int32, (128, 128), 1)
    before = lax.broadcasted_iota(jnp.int32, (rows, rows), 1) < lax.broadcasted_iota(jnp.int32, (rows, rows), 0)
    prefix = jnp.dot(mask.astype(BF16), jnp.where(upper, 1.0, 0.0).astype(BF16), preferred_element_type=F32)
    total = jnp.broadcast_to(jnp.sum(mask, axis=1, keepdims=True), (rows, 128))
    offset = jnp.dot(jnp.where(before, 1.0, 0.0).astype(BF16), total.astype(BF16), preferred_element_type=F32)
    rank = prefix + offset
    ids = lax.broadcasted_iota(jnp.int32, (rows, 128), 0) * 128 + lax.broadcasted_iota(jnp.int32, (rows, 128), 1)
    marked = jnp.where(mine, ids.astype(F32) + 1.0, 0.0)
    flagged = jnp.where(mine, flags_ref[...].astype(F32), 0.0)
    part[...] = jnp.zeros_like(part)
    kinds[...] = jnp.zeros_like(kinds)
    for slot in range(CAP):
        hit = rank == float(slot + 1)
        part[slot : slot + 1, :] = jnp.sum(jnp.where(hit, marked, 0.0), axis=0, keepdims=True)
        kinds[slot : slot + 1, :] = jnp.sum(jnp.where(hit, flagged, 0.0), axis=0, keepdims=True)
    found = jnp.broadcast_to(jnp.sum(part[...], axis=1, keepdims=True) - 1.0, part.shape)
    kind = jnp.broadcast_to(jnp.sum(kinds[...], axis=1, keepdims=True), kinds.shape)
    kind_ref[...] = kind

    own = lax.broadcasted_iota(jnp.int32, part.shape, 0) == lax.broadcasted_iota(jnp.int32, part.shape, 1)
    found = jnp.sum(jnp.where(own, found, 0.0), axis=0, keepdims=True)
    kind = jnp.sum(jnp.where(own, kind, 0.0), axis=0, keepdims=True)
    row = lax.broadcasted_iota(jnp.int32, owned_ref.shape, 0)
    owned_ref[...] = jnp.where(row == 0, found, kind).astype(jnp.int32)


def collide_kernel(pop_ref, rate_ref, c1_ref, planes, sem):
    def fetch(part):
        at = pl.ds(part * 4, 4)
        return pltpu.make_async_copy(pop_ref.at[:, at], planes.at[:, at], sem.at[part])

    for part in range(4):
        fetch(part).start()

    @pl.loop(0, 4)
    def _(part):
        fetch(part).wait()

        @pl.loop(0, 4)
        def _(step):
            x = part * 4 + step
            for t in range(4):
                rows = slice(8 * t, 8 * t + 8)
                h = [planes[i, x, rows, :].astype(F32) for i in range(19)]
                out = collide(h, rate_ref[1, 8 + 8 * t : 16 + 8 * t, :])
                for i in range(19):
                    c1_ref[i, x, rows, :] = out[i].astype(BF16)


def turn(rows, turned, dz):
    lane = lax.broadcasted_iota(jnp.int32, rows.shape, 1)
    if dz == 1:
        rows = jnp.where(lane == 127, pltpu.roll(turned, 127, axis=1), rows)
    else:
        rows = jnp.where(lane == 0, pltpu.roll(turned, 1, axis=1), rows)
    return rows.astype(BF16)


def face_kernel(c1_ref, low_ref, high_ref, rate_ref, cy_ref, rim_ref, right_ref, left_ref, planes, edge, sem):
    copies = [
        pltpu.make_async_copy(c1_ref.at[:, a : a + 2], planes.at[:, b : b + 2], sem.at[n])
        for n, (a, b) in enumerate(((0, 0), (14, 2)))
    ]
    for copy in copies:
        copy.start()

    for slot, y in HALO_Y:
        source = low_ref if y < 0 else high_ref
        row = y + 2 if y < 0 else y - 32
        rate = jnp.broadcast_to(rate_ref[1, y + 8 : y + 9, :], (8, 128))

        @pl.loop(0, 2)
        def _(half):
            start = pl.multiple_of(half * 8, 8)
            h = [source[i, row, pl.ds(start, 8), :].astype(F32) for i in range(19)]
            out = collide(h, rate)
            for i in range(19):
                edge[pl.ds(pl.multiple_of((i * 8 + slot) * 16 + start, 8), 8), :] = out[i]
                cy_ref[i, slot, pl.ds(start, 8), :] = out[i].astype(BF16)

    for copy in copies:
        copy.wait()
    for i in range(19):
        for n, plane in enumerate((0, 1, 14, 15)):
            body_rows = planes[i, n, :, :]
            ends = edge[pl.ds(i * 128 + plane, 8, stride=16), :].astype(BF16)
            rim_ref[i, n, 0:32, :] = body_rows
            rim_ref[i, n, 32:40, :] = ends
            for ref, faces, depth, outermost in ((right_ref, RIGHTWARD, 16 - plane, 3), (left_ref, LEFTWARD, plane + 1, 0)):
                if (i, depth) not in faces:
                    continue
                at = faces.index((i, depth))
                dz = VEL[i][2]
                if depth == 1 or dz == 0:
                    ref[at, 0:32, :] = body_rows
                    ref[at, 32:40, :] = ends
                else:
                    last = (0, 1, 14, 15)[outermost]
                    turned = edge[pl.ds(OPP[i] * 128 + last, 8, stride=16), :]
                    ref[at, 0:32, :] = turn(body_rows.astype(F32), planes[OPP[i], outermost, :, :].astype(F32), dz)
                    ref[at, 32:40, :] = turn(ends.astype(F32), turned, dz)


def shifted(ref, at, lane):
    out = []
    for i in range(19):
        dx, dy, dz = VEL[i]
        v = ref[i, pl.ds(at(-dx, -dy), 8), :]
        if dz == 1:
            v = jnp.where(lane == 0, ref[OPP[i], pl.ds(at(0, 0), 8), :], pltpu.roll(v, 1, axis=1))
        elif dz == -1:
            v = jnp.where(lane == 127, ref[OPP[i], pl.ds(at(0, 0), 8), :], pltpu.roll(v, 127, axis=1))
        out.append(v)
    return out


def advance(source, at, rate, target, row, lane):
    out = collide(shifted(source, at, lane), rate)
    for i in range(19):
        target[i, pl.ds(row, 8), :] = out[i]


def settle(source, base, target, part, lanes, lane):
    for yh in range(4):
        def at(dx, dy, yh=yh):
            return base + ((dx + 1) * ROWS + 8 + 8 * yh + dy)

        h = shifted(source, at, lane)
        for i in range(19):
            target[part, 32 * i + 8 * yh : 32 * i + 8 * yh + 8, lanes] = h[i].astype(BF16)


def inner_kernel(
    c1_ref, cy_ref, rate_ref, reduce_ref, rest_ref, state_ref, middle_ref, first, second, mean, mix, sem
):
    lane = lax.broadcasted_iota(jnp.int32, (8, 128), 1)

    @pl.loop(0, 16)
    def _(x):
        for i in range(19):
            first[i, pl.ds(pl.multiple_of(x * ROWS + 8, 8), 32), :] = c1_ref[i, x, :, :].astype(F32)

    for slot, y in HALO_Y:
        for i in range(19):
            for half in range(2):
                first[i, pl.ds(8 * half * ROWS + y + 8, 8, stride=ROWS), :] = cy_ref[
                    i, slot, 8 * half : 8 * half + 8, :
                ].astype(F32)

    @pl.loop(0, 7)
    def _(w):
        for v in range(2):
            base = pl.multiple_of((2 * w + v) * ROWS, 8)
            for t in range(5):
                def at(dx, dy, t=t, base=base):
                    return base + ((dx + 1) * ROWS + 7 + 8 * t + dy)

                advance(first, at, rate_ref[1, 7 + 8 * t : 15 + 8 * t, :], second, base + (7 + 8 * t), lane)

    copies = [
        pltpu.make_async_copy(
            second.at[:, a * ROWS : (a + 2) * ROWS], rest_ref.at[:, b * ROWS : (b + 2) * ROWS], sem.at[n]
        )
        for n, (a, b) in enumerate(((0, 0), (12, 2)))
    ]
    for copy in copies:
        copy.start()

    @pl.loop(0, 12)
    def _(p):
        lanes = pl.ds(pl.multiple_of((p % 2) * 128, 128), 128)
        settle(second, pl.multiple_of(p * ROWS, 8), state_ref, p // 2, lanes, lane)

    means(
        [(q, state_ref.at[2 * q - 1], state_ref.at[2 * q]) for q in (1, 2)], reduce_ref, mean, mix, middle_ref, lane
    )
    for copy in copies:
        copy.wait()


def butterfly(a, lane, unit):
    for bit in range(3):
        width = unit << bit
        low = (lane & width) == 0
        b = list(a)
        for j in range(8):
            if j & (1 << bit):
                continue
            k = j | (1 << bit)
            b[j] = jnp.where(low, a[j], pltpu.roll(a[k], width, axis=1))
            b[k] = jnp.where(low, pltpu.roll(a[j], 128 - width, axis=1), a[k])
        a = b
    return a


def means(quarters, reduce_ref, mean, mix, pack, lane):
    for n, (q, left, right) in enumerate(quarters):
        mean[n, :, :] = jnp.dot(left[...], reduce_ref[0, :, :], preferred_element_type=F32) + jnp.dot(
            right[...], reduce_ref[1, :, :], preferred_element_type=F32
        )
        for i in range(19):
            for by in range(2):
                at = 32 * i + 16 * by
                mix[n, by, 8 * i : 8 * i + 8, :] = (
                    mean[n, pl.ds(at, 8, stride=2), :] + mean[n, pl.ds(at + 1, 8, stride=2), :]
                )
        for by in range(2):
            for g in range(3):
                a = [mix[n, by, pl.ds(64 * g + y, 8, stride=8), :] for y in range(8)]
                a = butterfly(a, lane, 8)
                for z in range(8):
                    pack[8 * by + z, pl.ds(32 * g + q, 8, stride=4), :] = a[z]


def step_kernel(
    flags_ref, owner_ref, rest_ref, rim_ref, gl_ref, gr_ref, rate_ref, reduce_ref, inner_ref, middle_ref,
    outer_ref, send_ref,
    first, second, mean, mix, pack, stage, in_sem, send_sem,
):
    me = lax.axis_index("gx") * lax.axis_size("yz") + lax.axis_index("yz")
    lane = lax.broadcasted_iota(jnp.int32, (8, 128), 1)
    rest = pltpu.make_async_copy(rest_ref, second.at[:, 2 * ROWS : 6 * ROWS], in_sem)
    rest.start()

    def place(i, at, rows):
        first[i, at * ROWS + 8 : at * ROWS + 40, :] = rows[0:32, :]
        first[i, at * ROWS + 40 : at * ROWS + 48, :] = rows[32:40, :]
        first[i, at * ROWS : at * ROWS + 8, :] = rows[32:40, :]

    for i in range(19):
        for n, at in enumerate((2, 3, 4, 5)):
            place(i, at, rim_ref[i, n, :, :].astype(F32))
    for ref, faces, places in ((gl_ref, RIGHTWARD, (None, 1, 0)), (gr_ref, LEFTWARD, (None, 6, 7))):
        for n, (i, depth) in enumerate(faces):
            rows = ref[n, :, :].astype(F32)
            place(i, places[depth], rows)
            if depth == 2 and VEL[i][2] != 0:
                place(OPP[i], places[1], pltpu.roll(rows, 1 if VEL[i][2] == 1 else 127, axis=1))

    @pl.loop(0, 2)
    def _(above):
        for v in range(2):
            base = pl.multiple_of((v + 4 * above) * ROWS, 8)
            row = pl.multiple_of((v + 6 * above) * ROWS, 8)
            for t in range(5):
                def at(dx, dy, t=t, base=base):
                    return base + ((dx + 1) * ROWS + 7 + 8 * t + dy)

                rate = rate_ref[above + v, 7 + 8 * t : 15 + 8 * t, :]
                advance(first, at, rate, second, row + (7 + 8 * t), lane)

    rest.wait()

    @pl.loop(0, 4)
    def _(e):
        above = e // 2
        lanes = pl.ds(pl.multiple_of((e % 2) * 128, 128), 128)
        settle(second, pl.multiple_of((e + 2 * above) * ROWS, 8), outer_ref, above, lanes, lane)

    means(
        [(0, outer_ref.at[0], inner_ref.at[0]), (3, inner_ref.at[5], outer_ref.at[1])],
        reduce_ref, mean, mix, pack, lane,
    )

    quarter = lax.broadcasted_iota(jnp.int32, (4, 128), 0)
    middle = (quarter == 1) | (quarter == 2)

    @pl.loop(0, BLK)
    def _(k):
        @pl.when(flags_ref[me * BLK + k] != 0)
        def _():
            for i in range(19):
                rows = slice(4 * i, 4 * i + 4)
                stage[k, i, :, :] = jnp.where(middle, middle_ref[k, rows, :], pack[k, rows, :]).astype(BF16)
            pltpu.make_async_copy(stage.at[k], send_ref.at[owner_ref[me * BLK + k]], send_sem.at[k]).start()

    @pl.loop(0, BLK)
    def _(k):
        @pl.when(flags_ref[me * BLK + k] != 0)
        def _():
            pltpu.make_async_copy(stage.at[k], send_ref.at[0], send_sem.at[k]).wait()


def keep_kernel(owned_ref, inner_ref, outer_ref, half_ref, mix, slots, place):
    me = lax.axis_index("gx") * lax.axis_size("yz") + lax.axis_index("yz")
    lane = lax.broadcasted_iota(jnp.int32, (8, 128), 1)

    @pl.loop(0, BLK)
    def _(k):
        place[k] = CAP

    @pl.loop(0, CAP)
    def _(s):
        b = owned_ref[0, s]

        @pl.when((b >= 0) & (owned_ref[1, s] == 0))
        def _():
            place[b - me * BLK] = s

    @pl.loop(0, 32)
    def _(c):
        for r in range(CAP * 3):
            slots[c, 8 * r : 8 * r + 8, :] = jnp.zeros((8, 128), F32)

    def spread(state_ref, pair, x):
        lanes = pl.ds(pl.multiple_of((x % 2) * 128, 128), 128)
        for yh in range(4):
            for i in range(19):
                tile = state_ref[pair, 32 * i + 8 * yh : 32 * i + 8 * yh + 8, lanes]
                mix[yh, 8 * i : 8 * i + 8, :] = tile.astype(F32)
            for g in range(3):
                a = [mix[yh, pl.ds(64 * g + y, 8, stride=8), :] for y in range(8)]
                a = butterfly(a, lane, 16)
                for z in range(8):
                    row = pl.multiple_of(place[(yh // 2) * 8 + z] * 24 + 8 * g, 8)
                    slots[2 * x + yh % 2, pl.ds(row, 8), :] = a[z]

    @pl.loop(2, 14)
    def _(x):
        spread(inner_ref, x // 2 - 1, x)

    @pl.loop(0, 4)
    def _(e):
        spread(outer_ref, e // 2, e + 12 * (e // 2))

    @pl.loop(0, 32)
    def _(c):
        lanes = pl.ds(pl.multiple_of(c * 128, 128), 128)
        for i in range(19):
            parts = [slots[c, pl.ds(192 * g + i, 8, stride=24), :] for g in range(3)]
            half_ref[i, 0:16, lanes] = jnp.concatenate(parts[:2], axis=0).astype(BF16)
            half_ref[i, 16:24, lanes] = parts[2].astype(BF16)


def refine_kernel(
    owned_ref, recv_ref, kind_ref, expand_ref, half_ref, out_ref,
    rows, wide, product, half, result, half_sem, out_sem,
):
    @pl.loop(0, 19)
    def _(i):
        pltpu.make_async_copy(half_ref.at[i], half.at[i], half_sem.at[i]).start()

    @pl.loop(0, CAP)
    def _(s):
        b = owned_ref[0, s]

        @pl.when(owned_ref[1, s] != 0)
        def _():
            for i in range(19):
                rows[pl.ds(96 * i + s, 4, stride=24), :] = recv_ref[b // BLK, i, :, :].astype(F32)

    kinds = [kind_ref[8 * g : 8 * g + 8, :] for g in range(3)]
    for q in range(4):
        for i in range(19):
            ones, twos = [], []
            for g in range(3):
                start = 24 * (4 * i + q) + 8 * g
                v = rows[start : start + 8, :]
                ones.append(jnp.where(kinds[g] == 1.0, v, 0.0))
                twos.append(jnp.where(kinds[g] == 2.0, v, 0.0))
            for start, v in ((0, ones), (128, twos)):
                wide[q, 24 * i : 24 * i + 16, start : start + 128] = jnp.concatenate(v[:2], axis=0).astype(BF16)
                wide[q, 24 * i + 16 : 24 * i + 24, start : start + 128] = v[2].astype(BF16)
        product[q, :, :] = jnp.dot(wide[q, :, :], expand_ref[...], preferred_element_type=F32)

    linear = jnp.concatenate([jnp.concatenate([k, k], axis=1) for k in kinds], axis=0) == 2.0
    near = jnp.where(linear, 0.75, 1.0)
    far = jnp.where(linear, 0.25, 0.0)

    @pl.loop(0, 19)
    def _(i):
        pltpu.make_async_copy(half_ref.at[i], half.at[i], half_sem.at[i]).wait()
        start = pl.multiple_of(i * 24, 8)

        def plane(c):
            return product[c // 2, pl.ds(start, 24), (c % 2) * 256 : (c % 2) * 256 + 256]

        for c in range(8):
            mid = plane(c) * near
            for odd in range(2):
                other = max(c - 1, 0) if odd == 0 else min(c + 1, 7)
                x = slice((2 * c + odd) * 256, (2 * c + odd) * 256 + 256)
                result[i, :, x] = (mid + plane(other) * far).astype(BF16) + half[i, :, x]
        pltpu.make_async_copy(result.at[i], out_ref.at[i], out_sem.at[i]).start()

    @pl.loop(0, 19)
    def _(i):
        pltpu.make_async_copy(result.at[i], out_ref.at[i], out_sem.at[i]).wait()


def mean_matrix():
    half = np.zeros((128, 64), np.float32)
    half[np.arange(128), np.arange(128) // 2] = 0.125
    both = np.concatenate([half, half], axis=0)
    none = np.zeros_like(both)
    return np.stack([np.concatenate([both, none], axis=1), np.concatenate([none, both], axis=1)])


def expand_matrix():
    inject = np.zeros((8, 16), np.float32)
    linear = np.zeros((8, 16), np.float32)
    for k in range(8):
        for odd, other in ((0, max(k - 1, 0)), (1, min(k + 1, 7))):
            inject[k, 2 * k + odd] = 1.0
            linear[k, 2 * k + odd] += 0.75
            linear[other, 2 * k + odd] += 0.25
    eye = np.eye(2, dtype=np.float32)
    return np.concatenate([np.kron(eye, np.kron(m, m)) for m in (inject, linear)], axis=0)


def ring(count, step):
    return [(i, (i + step) % count) for i in range(count)]


VM = pl.BlockSpec(memory_space=pltpu.VMEM)
SM = pl.BlockSpec(memory_space=pltpu.SMEM)
ANY = pl.BlockSpec(memory_space=pl.ANY)
HBM = pl.BlockSpec(memory_space=pltpu.HBM)


def struct(shape, dtype):
    return jax.ShapeDtypeStruct(shape, dtype)


def in_hbm(array):
    return pltpu.with_memory_space_constraint(array, pltpu.HBM)


def cost(microseconds):
    return pl.CostEstimate(flops=0, bytes_accessed=int(microseconds * 3.0e6), transcendentals=0)


def limit(mebibytes):
    return pltpu.CompilerParams(vmem_limit_bytes=mebibytes << 20)


def body(populations, levels, refine_flags, new_owner):
    columns = lax.axis_size("yz")
    slabs = lax.axis_size("gx")
    total = new_owner.shape[0]
    devices = slabs * columns

    top = jnp.transpose(populations[:, :, 30:32, :], (0, 2, 1, 3))
    bottom = jnp.transpose(populations[:, :, 0:2, :], (0, 2, 1, 3))
    low = lax.ppermute(top, "yz", ring(columns, 1))
    high = lax.ppermute(bottom, "yz", ring(columns, -1))

    rate = pl.pallas_call(
        rate_kernel,
        out_shape=struct((3, ROWS, 128), F32),
        in_specs=[SM],
        out_specs=VM,
        compiler_params=limit(4),
        cost_estimate=cost(1),
        name="rates",
    )(in_hbm(levels))

    c1 = pl.pallas_call(
        collide_kernel,
        out_shape=struct((19, 16, 32, 128), BF16),
        in_specs=[HBM, VM],
        out_specs=VM,
        scratch_shapes=[pltpu.VMEM((19, 16, 32, 128), BF16), pltpu.SemaphoreType.DMA((4,))],
        compiler_params=limit(8),
        cost_estimate=cost(5),
        name="collide",
    )(in_hbm(populations), rate)

    cy, rim, right, left = pl.pallas_call(
        face_kernel,
        out_shape=(
            struct((19, 8, 16, 128), BF16),
            struct((19, 4, FROWS, 128), BF16),
            struct((FACES, FROWS, 128), BF16),
            struct((FACES, FROWS, 128), BF16),
        ),
        in_specs=[ANY, VM, VM, VM],
        out_specs=(VM,) * 4,
        scratch_shapes=[
            pltpu.VMEM((19, 4, 32, 128), BF16),
            pltpu.VMEM((19 * 128 + 128, 128), F32),
            pltpu.SemaphoreType.DMA((2,)),
        ],
        compiler_params=limit(8),
        cost_estimate=cost(2),
        name="faces",
    )(c1, low, high, rate)

    from_left = lax.ppermute(right, "gx", ring(slabs, 1))
    from_right = lax.ppermute(left, "gx", ring(slabs, -1))

    reduce = jnp.asarray(mean_matrix(), BF16)
    rest, inner, middle = pl.pallas_call(
        inner_kernel,
        out_shape=(
            struct((19, 4 * ROWS, 128), F32),
            struct((6, 608, 256), BF16),
            struct((BLK, 96, 128), F32),
        ),
        in_specs=[VM] * 4,
        out_specs=(ANY, VM, VM),
        scratch_shapes=[
            pltpu.VMEM((19, 16 * ROWS, 128), F32),
            pltpu.VMEM((19, 14 * ROWS, 128), F32),
            pltpu.VMEM((2, 608, 128), F32),
            pltpu.VMEM((2, 2, 192, 128), F32),
            pltpu.SemaphoreType.DMA((2,)),
        ],
        compiler_params=limit(22),
        cost_estimate=cost(6),
        name="inner",
    )(c1, cy, rate, reduce)

    outer, send = pl.pallas_call(
        step_kernel,
        out_shape=(struct((2, 608, 256), BF16), pltpu.HBM((devices, 19, 4, 128), BF16)),
        in_specs=[SM, SM, ANY] + [VM] * 7,
        out_specs=(VM, HBM),
        scratch_shapes=[
            pltpu.VMEM((19, 8 * ROWS, 128), F32),
            pltpu.VMEM((19, 8 * ROWS, 128), F32),
            pltpu.VMEM((2, 608, 128), F32),
            pltpu.VMEM((2, 2, 192, 128), F32),
            pltpu.VMEM((BLK, 96, 128), F32),
            pltpu.VMEM((BLK, 19, 4, 128), BF16),
            pltpu.SemaphoreType.DMA,
            pltpu.SemaphoreType.DMA((BLK,)),
        ],
        compiler_params=limit(18),
        cost_estimate=cost(6),
        name="step",
    )(
        refine_flags, new_owner, rest, rim, from_left, from_right, rate, reduce, inner, middle,
    )

    recv = lax.all_to_all(send, ("gx", "yz"), split_axis=0, concat_axis=0, tiled=True)

    owned, kind = pl.pallas_call(
        plan_kernel,
        out_shape=(struct((8, 128), jnp.int32), struct((32, 128), F32)),
        in_specs=[VM, VM, ANY],
        out_specs=(VM, VM),
        scratch_shapes=[pltpu.VMEM((32, 128), F32), pltpu.VMEM((32, 128), F32)],
        compiler_params=limit(4),
        cost_estimate=cost(2),
        name="plan",
    )(refine_flags.reshape(total // 128, 128), new_owner.reshape(total // 128, 128), outer)

    half = pl.pallas_call(
        keep_kernel,
        out_shape=pltpu.HBM((19, CAP, 4096), BF16),
        in_specs=[SM, VM, VM],
        out_specs=VM,
        scratch_shapes=[
            pltpu.VMEM((4, 192, 128), F32),
            pltpu.VMEM((32, (CAP + 1) * 24, 128), F32),
            pltpu.SMEM((BLK,), jnp.int32),
        ],
        compiler_params=limit(20),
        cost_estimate=cost(10),
        name="keep",
    )(owned, inner, outer)

    migrated = pl.pallas_call(
        refine_kernel,
        out_shape=struct((19, CAP, 4096), BF16),
        in_specs=[SM, VM, VM, VM, HBM],
        out_specs=ANY,
        scratch_shapes=[
            pltpu.VMEM((CAP * 76, 128), F32),
            pltpu.VMEM((4, 456, 256), BF16),
            pltpu.VMEM((4, 456, 512), F32),
            pltpu.VMEM((19, CAP, 4096), BF16),
            pltpu.VMEM((19, CAP, 4096), BF16),
            pltpu.SemaphoreType.DMA((19,)),
            pltpu.SemaphoreType.DMA((19,)),
        ],
        compiler_params=limit(18),
        cost_estimate=cost(5),
        name="refine",
    )(owned, recv, kind, jnp.asarray(expand_matrix(), BF16), in_hbm(half))
    return jnp.transpose(migrated, (1, 0, 2))


def solution(mesh):
    placed = (P(None, "gx", "yz", None), P(), P(), P())
    return jax.shard_map(
        body, mesh=mesh, in_specs=placed, out_specs=P(("gx", "yz"), None, None), check_vma=False
    )
```

```python
import jax
import jax.numpy as jnp
import numpy as np
from jax import lax
from jax.experimental import pallas as pl
from jax.experimental.pallas import tpu as pltpu
from jax.sharding import PartitionSpec as P

BS = 16
BZ = 8
CAP = 24
BLK = 16
ROWS = 48
F32 = jnp.float32
BF16 = jnp.bfloat16

VEL = [
    (0, 0, 0),
    (1, 0, 0), (-1, 0, 0), (0, 1, 0), (0, -1, 0), (0, 0, 1), (0, 0, -1),
    (1, 1, 0), (-1, -1, 0), (1, -1, 0), (-1, 1, 0),
    (1, 0, 1), (-1, 0, -1), (1, 0, -1), (-1, 0, 1),
    (0, 1, 1), (0, -1, -1), (0, 1, -1), (0, -1, 1),
]
OPP = [0, 2, 1, 4, 3, 6, 5, 8, 7, 10, 9, 12, 11, 14, 13, 16, 15, 18, 17]
PLUS = [i for i in range(19) if VEL[i][0] == 1]
MINUS = [i for i in range(19) if VEL[i][0] == -1]
FLAT = [i for i in range(19) if VEL[i][0] == 0]
RIGHTWARD = [(i, 2) for i in PLUS] + [(i, 1) for i in PLUS + FLAT]
LEFTWARD = [(i, 2) for i in MINUS] + [(i, 1) for i in MINUS + FLAT]
FACES = len(RIGHTWARD)
FROWS = 40
HALO_Y = ((0, 32), (1, 33), (6, -2), (7, -1))


def collide(h, r):
    p = {}
    d = {}
    for a in range(1, 19, 2):
        p[a] = h[a] + h[a + 1]
        d[a] = h[a] - h[a + 1]
    axis = p[1] + p[3] + p[5]
    diag = (p[7] + p[9]) + (p[11] + p[13]) + (p[15] + p[17])
    rho = 1.0 + (h[0] * (1.0 / 3.0) + axis * (1.0 / 18.0) + diag * (1.0 / 36.0))
    mx = (2.0 * d[1] + (d[7] + d[9]) + (d[11] + d[13])) * (1.0 / 36.0)
    my = (2.0 * d[3] + (d[7] - d[9]) + (d[15] + d[17])) * (1.0 / 36.0)
    mz = (2.0 * d[5] + (d[11] - d[13]) + (d[15] - d[17])) * (1.0 / 36.0)
    inv = 1.0 / rho
    ux, uy, uz = mx * inv, my * inv, mz * inv
    square = ux * ux + uy * uy + uz * uz
    keep = 1.0 - r
    base = r * (rho * (1.0 - 1.5 * square) - 1.0)
    quad = (4.5 * r) * rho
    lin = (3.0 * r) * rho
    proj = {
        1: ux, 3: uy, 5: uz, 7: ux + uy, 9: ux - uy, 11: ux + uz, 13: ux - uz, 15: uy + uz, 17: uy - uz,
    }
    out = [keep * h[0] + base] + [None] * 18
    for a in range(1, 19, 2):
        even = base + quad * (proj[a] * proj[a])
        odd = lin * proj[a]
        out[a] = keep * h[a] + (even + odd)
        out[a + 1] = keep * h[a + 1] + (even - odd)
    return out


def rate_kernel(levels_ref, rate_ref):
    slab, column = lax.axis_index("gx"), lax.axis_index("yz")
    slabs, columns = lax.axis_size("gx"), lax.axis_size("yz")
    group = lax.broadcasted_iota(jnp.int32, (8, 128), 1) // BS
    for plane in range(3):
        row = lax.rem(slab + (plane + slabs - 1), slabs) * (2 * columns)
        for band, (first, last) in enumerate(((0, 8), (8, 24), (24, 40), (40, 48))):
            start = (row + lax.rem(2 * column + (band + 2 * columns - 1), 2 * columns)) * BZ
            level = jnp.zeros((8, 128), F32)
            for z in range(BZ):
                level = jnp.where(group == z, levels_ref[start + z].astype(F32), level)
            rate = 1.0 / (0.5 + jnp.exp2(-level))
            for at in range(first, last, 8):
                rate_ref[plane, at : at + 8, :] = rate


def plan_kernel(flags_ref, owner_ref, after_ref, owned_ref, kind_ref, part, kinds):
    del after_ref
    me = lax.axis_index("gx") * lax.axis_size("yz") + lax.axis_index("yz")
    rows = owner_ref.shape[0]
    mine = owner_ref[...] == me
    mask = jnp.where(mine, 1.0, 0.0)
    upper = lax.broadcasted_iota(jnp.int32, (128, 128), 0) <= lax.broadcasted_iota(jnp.int32, (128, 128), 1)
    before = lax.broadcasted_iota(jnp.int32, (rows, rows), 1) < lax.broadcasted_iota(jnp.int32, (rows, rows), 0)
    prefix = jnp.dot(mask.astype(BF16), jnp.where(upper, 1.0, 0.0).astype(BF16), preferred_element_type=F32)
    total = jnp.broadcast_to(jnp.sum(mask, axis=1, keepdims=True), (rows, 128))
    offset = jnp.dot(jnp.where(before, 1.0, 0.0).astype(BF16), total.astype(BF16), preferred_element_type=F32)
    rank = prefix + offset
    ids = lax.broadcasted_iota(jnp.int32, (rows, 128), 0) * 128 + lax.broadcasted_iota(jnp.int32, (rows, 128), 1)
    marked = jnp.where(mine, ids.astype(F32) + 1.0, 0.0)
    flagged = jnp.where(mine, flags_ref[...].astype(F32), 0.0)
    part[...] = jnp.zeros_like(part)
    kinds[...] = jnp.zeros_like(kinds)
    for slot in range(CAP):
        hit = rank == float(slot + 1)
        part[slot : slot + 1, :] = jnp.sum(jnp.where(hit, marked, 0.0), axis=0, keepdims=True)
        kinds[slot : slot + 1, :] = jnp.sum(jnp.where(hit, flagged, 0.0), axis=0, keepdims=True)
    found = jnp.broadcast_to(jnp.sum(part[...], axis=1, keepdims=True) - 1.0, part.shape)
    kind = jnp.broadcast_to(jnp.sum(kinds[...], axis=1, keepdims=True), kinds.shape)
    kind_ref[...] = kind

    own = lax.broadcasted_iota(jnp.int32, part.shape, 0) == lax.broadcasted_iota(jnp.int32, part.shape, 1)
    found = jnp.sum(jnp.where(own, found, 0.0), axis=0, keepdims=True)
    kind = jnp.sum(jnp.where(own, kind, 0.0), axis=0, keepdims=True)
    row = lax.broadcasted_iota(jnp.int32, owned_ref.shape, 0)
    owned_ref[...] = jnp.where(row == 0, found, kind).astype(jnp.int32)


def collide_kernel(pop_ref, rate_ref, c1_ref, planes, sem):
    def fetch(part):
        at = pl.ds(part * 4, 4)
        return pltpu.make_async_copy(pop_ref.at[:, at], planes.at[:, at], sem.at[part])

    for part in range(4):
        fetch(part).start()

    @pl.loop(0, 4)
    def _(part):
        fetch(part).wait()

        @pl.loop(0, 4)
        def _(step):
            x = part * 4 + step
            for t in range(4):
                rows = slice(8 * t, 8 * t + 8)
                h = [planes[i, x, rows, :].astype(F32) for i in range(19)]
                out = collide(h, rate_ref[1, 8 + 8 * t : 16 + 8 * t, :])
                for i in range(19):
                    c1_ref[i, x, rows, :] = out[i].astype(BF16)


def turn(rows, turned, dz):
    lane = lax.broadcasted_iota(jnp.int32, rows.shape, 1)
    if dz == 1:
        rows = jnp.where(lane == 127, pltpu.roll(turned, 127, axis=1), rows)
    else:
        rows = jnp.where(lane == 0, pltpu.roll(turned, 1, axis=1), rows)
    return rows.astype(BF16)


def face_kernel(c1_ref, low_ref, high_ref, rate_ref, cy_ref, rim_ref, right_ref, left_ref, planes, edge, sem):
    copies = [
        pltpu.make_async_copy(c1_ref.at[:, a : a + 2], planes.at[:, b : b + 2], sem.at[n])
        for n, (a, b) in enumerate(((0, 0), (14, 2)))
    ]
    for copy in copies:
        copy.start()

    for slot, y in HALO_Y:
        source = low_ref if y < 0 else high_ref
        row = y + 2 if y < 0 else y - 32
        rate = jnp.broadcast_to(rate_ref[1, y + 8 : y + 9, :], (8, 128))

        @pl.loop(0, 2)
        def _(half):
            start = pl.multiple_of(half * 8, 8)
            h = [source[i, row, pl.ds(start, 8), :].astype(F32) for i in range(19)]
            out = collide(h, rate)
            for i in range(19):
                edge[pl.ds(pl.multiple_of((i * 8 + slot) * 16 + start, 8), 8), :] = out[i]
                cy_ref[i, slot, pl.ds(start, 8), :] = out[i].astype(BF16)

    for copy in copies:
        copy.wait()
    for i in range(19):
        for n, plane in enumerate((0, 1, 14, 15)):
            body_rows = planes[i, n, :, :]
            ends = edge[pl.ds(i * 128 + plane, 8, stride=16), :].astype(BF16)
            rim_ref[i, n, 0:32, :] = body_rows
            rim_ref[i, n, 32:40, :] = ends
            for ref, faces, depth, outermost in ((right_ref, RIGHTWARD, 16 - plane, 3), (left_ref, LEFTWARD, plane + 1, 0)):
                if (i, depth) not in faces:
                    continue
                at = faces.index((i, depth))
                dz = VEL[i][2]
                if depth == 1 or dz == 0:
                    ref[at, 0:32, :] = body_rows
                    ref[at, 32:40, :] = ends
                else:
                    last = (0, 1, 14, 15)[outermost]
                    turned = edge[pl.ds(OPP[i] * 128 + last, 8, stride=16), :]
                    ref[at, 0:32, :] = turn(body_rows.astype(F32), planes[OPP[i], outermost, :, :].astype(F32), dz)
                    ref[at, 32:40, :] = turn(ends.astype(F32), turned, dz)


def shifted(ref, at, lane):
    out = []
    for i in range(19):
        dx, dy, dz = VEL[i]
        v = ref[i, pl.ds(at(-dx, -dy), 8), :]
        if dz == 1:
            v = jnp.where(lane == 0, ref[OPP[i], pl.ds(at(0, 0), 8), :], pltpu.roll(v, 1, axis=1))
        elif dz == -1:
            v = jnp.where(lane == 127, ref[OPP[i], pl.ds(at(0, 0), 8), :], pltpu.roll(v, 127, axis=1))
        out.append(v)
    return out


def advance(source, at, rate, target, row, lane):
    out = collide(shifted(source, at, lane), rate)
    for i in range(19):
        target[i, pl.ds(row, 8), :] = out[i]


def settle(source, base, target, part, lanes, lane):
    for yh in range(4):
        def at(dx, dy, yh=yh):
            return base + ((dx + 1) * ROWS + 8 + 8 * yh + dy)

        h = shifted(source, at, lane)
        for i in range(19):
            target[part, 32 * i + 8 * yh : 32 * i + 8 * yh + 8, lanes] = h[i].astype(BF16)


def inner_kernel(
    c1_ref, cy_ref, rate_ref, reduce_ref, flags_ref, owner_ref, rest_ref, state_ref, middle_ref, target_ref,
    first, second, mean, mix, sem,
):
    lane = lax.broadcasted_iota(jnp.int32, (8, 128), 1)

    me = lax.axis_index("gx") * lax.axis_size("yz") + lax.axis_index("yz")
    mine = lax.broadcasted_iota(jnp.int32, owner_ref.shape, 0) == me // 8
    goes = jnp.where(flags_ref[...] != 0, owner_ref[...], -1).astype(F32)
    goes = jnp.broadcast_to(jnp.sum(jnp.where(mine, goes, 0.0), axis=0, keepdims=True), (8, 128))
    goes = pltpu.roll(goes, lax.rem(128 - lax.rem(me, 8) * BLK, 128), axis=1)
    target_ref[...] = goes.astype(jnp.int32)

    @pl.loop(0, 16)
    def _(x):
        for i in range(19):
            first[i, pl.ds(pl.multiple_of(x * ROWS + 8, 8), 32), :] = c1_ref[i, x, :, :].astype(F32)

    for slot, y in HALO_Y:
        for i in range(19):
            for half in range(2):
                first[i, pl.ds(8 * half * ROWS + y + 8, 8, stride=ROWS), :] = cy_ref[
                    i, slot, 8 * half : 8 * half + 8, :
                ].astype(F32)

    @pl.loop(0, 7)
    def _(w):
        for v in range(2):
            base = pl.multiple_of((2 * w + v) * ROWS, 8)
            for t in range(5):
                def at(dx, dy, t=t, base=base):
                    return base + ((dx + 1) * ROWS + 7 + 8 * t + dy)

                advance(first, at, rate_ref[1, 7 + 8 * t : 15 + 8 * t, :], second, base + (7 + 8 * t), lane)

    copies = [
        pltpu.make_async_copy(
            second.at[:, a * ROWS : (a + 2) * ROWS], rest_ref.at[:, b * ROWS : (b + 2) * ROWS], sem.at[n]
        )
        for n, (a, b) in enumerate(((0, 0), (12, 2)))
    ]
    for copy in copies:
        copy.start()

    @pl.loop(0, 12)
    def _(p):
        lanes = pl.ds(pl.multiple_of((p % 2) * 128, 128), 128)
        settle(second, pl.multiple_of(p * ROWS, 8), state_ref, p // 2, lanes, lane)

    means(
        [(q, state_ref.at[2 * q - 1], state_ref.at[2 * q]) for q in (1, 2)], reduce_ref, mean, mix, middle_ref, lane
    )
    for copy in copies:
        copy.wait()


def butterfly(a, lane, unit):
    for bit in range(3):
        width = unit << bit
        low = (lane & width) == 0
        b = list(a)
        for j in range(8):
            if j & (1 << bit):
                continue
            k = j | (1 << bit)
            b[j] = jnp.where(low, a[j], pltpu.roll(a[k], width, axis=1))
            b[k] = jnp.where(low, pltpu.roll(a[j], 128 - width, axis=1), a[k])
        a = b
    return a


def means(quarters, reduce_ref, mean, mix, pack, lane):
    for n, (q, left, right) in enumerate(quarters):
        mean[n, :, :] = jnp.dot(left[...], reduce_ref[0, :, :], preferred_element_type=F32) + jnp.dot(
            right[...], reduce_ref[1, :, :], preferred_element_type=F32
        )
        for i in range(19):
            for by in range(2):
                at = 32 * i + 16 * by
                mix[n, by, 8 * i : 8 * i + 8, :] = (
                    mean[n, pl.ds(at, 8, stride=2), :] + mean[n, pl.ds(at + 1, 8, stride=2), :]
                )
        for by in range(2):
            for g in range(3):
                a = [mix[n, by, pl.ds(64 * g + y, 8, stride=8), :] for y in range(8)]
                a = butterfly(a, lane, 8)
                for z in range(8):
                    pack[8 * by + z, pl.ds(32 * g + q, 8, stride=4), :] = a[z]


def step_kernel(
    target_ref, rest_ref, rim_ref, gl_ref, gr_ref, rate_ref, reduce_ref, inner_ref, middle_ref,
    outer_ref, send_ref,
    first, second, mean, mix, pack, stage, in_sem, send_sem,
):
    lane = lax.broadcasted_iota(jnp.int32, (8, 128), 1)
    rest = pltpu.make_async_copy(rest_ref, second.at[:, 2 * ROWS : 6 * ROWS], in_sem)
    rest.start()

    def place(i, at, rows):
        first[i, at * ROWS + 8 : at * ROWS + 40, :] = rows[0:32, :]
        first[i, at * ROWS + 40 : at * ROWS + 48, :] = rows[32:40, :]
        first[i, at * ROWS : at * ROWS + 8, :] = rows[32:40, :]

    for i in range(19):
        for n, at in enumerate((2, 3, 4, 5)):
            place(i, at, rim_ref[i, n, :, :].astype(F32))
    for ref, faces, places in ((gl_ref, RIGHTWARD, (None, 1, 0)), (gr_ref, LEFTWARD, (None, 6, 7))):
        for n, (i, depth) in enumerate(faces):
            rows = ref[n, :, :].astype(F32)
            place(i, places[depth], rows)
            if depth == 2 and VEL[i][2] != 0:
                place(OPP[i], places[1], pltpu.roll(rows, 1 if VEL[i][2] == 1 else 127, axis=1))

    @pl.loop(0, 2)
    def _(above):
        for v in range(2):
            base = pl.multiple_of((v + 4 * above) * ROWS, 8)
            row = pl.multiple_of((v + 6 * above) * ROWS, 8)
            for t in range(5):
                def at(dx, dy, t=t, base=base):
                    return base + ((dx + 1) * ROWS + 7 + 8 * t + dy)

                rate = rate_ref[above + v, 7 + 8 * t : 15 + 8 * t, :]
                advance(first, at, rate, second, row + (7 + 8 * t), lane)

    rest.wait()

    @pl.loop(0, 4)
    def _(e):
        above = e // 2
        lanes = pl.ds(pl.multiple_of((e % 2) * 128, 128), 128)
        settle(second, pl.multiple_of((e + 2 * above) * ROWS, 8), outer_ref, above, lanes, lane)

    means(
        [(0, outer_ref.at[0], inner_ref.at[0]), (3, inner_ref.at[5], outer_ref.at[1])],
        reduce_ref, mean, mix, pack, lane,
    )

    quarter = lax.broadcasted_iota(jnp.int32, (4, 128), 0)
    middle = (quarter == 1) | (quarter == 2)

    @pl.loop(0, BLK)
    def _(k):
        @pl.when(target_ref[0, k] >= 0)
        def _():
            for i in range(19):
                rows = slice(4 * i, 4 * i + 4)
                stage[k, i, :, :] = jnp.where(middle, middle_ref[k, rows, :], pack[k, rows, :]).astype(BF16)
            pltpu.make_async_copy(stage.at[k], send_ref.at[target_ref[0, k]], send_sem.at[k]).start()

    @pl.loop(0, BLK)
    def _(k):
        @pl.when(target_ref[0, k] >= 0)
        def _():
            pltpu.make_async_copy(stage.at[k], send_ref.at[0], send_sem.at[k]).wait()


def keep_kernel(owned_ref, inner_ref, outer_ref, half_ref, mix, slots, place):
    me = lax.axis_index("gx") * lax.axis_size("yz") + lax.axis_index("yz")
    lane = lax.broadcasted_iota(jnp.int32, (8, 128), 1)

    @pl.loop(0, BLK)
    def _(k):
        place[k] = CAP

    @pl.loop(0, CAP)
    def _(s):
        b = owned_ref[0, s]

        @pl.when((b >= 0) & (owned_ref[1, s] == 0))
        def _():
            place[b - me * BLK] = s

    @pl.loop(0, 32)
    def _(c):
        for r in range(CAP * 3):
            slots[c, 8 * r : 8 * r + 8, :] = jnp.zeros((8, 128), F32)

    def spread(state_ref, pair, x):
        lanes = pl.ds(pl.multiple_of((x % 2) * 128, 128), 128)
        for yh in range(4):
            for i in range(19):
                tile = state_ref[pair, 32 * i + 8 * yh : 32 * i + 8 * yh + 8, lanes]
                mix[yh, 8 * i : 8 * i + 8, :] = tile.astype(F32)
            for g in range(3):
                a = [mix[yh, pl.ds(64 * g + y, 8, stride=8), :] for y in range(8)]
                a = butterfly(a, lane, 16)
                for z in range(8):
                    row = pl.multiple_of(place[(yh // 2) * 8 + z] * 24 + 8 * g, 8)
                    slots[2 * x + yh % 2, pl.ds(row, 8), :] = a[z]

    @pl.loop(2, 14)
    def _(x):
        spread(inner_ref, x // 2 - 1, x)

    @pl.loop(0, 4)
    def _(e):
        spread(outer_ref, e // 2, e + 12 * (e // 2))

    @pl.loop(0, 32)
    def _(c):
        lanes = pl.ds(pl.multiple_of(c * 128, 128), 128)
        for i in range(19):
            parts = [slots[c, pl.ds(192 * g + i, 8, stride=24), :] for g in range(3)]
            half_ref[i, 0:16, lanes] = jnp.concatenate(parts[:2], axis=0).astype(BF16)
            half_ref[i, 16:24, lanes] = parts[2].astype(BF16)


def refine_kernel(
    owned_ref, recv_ref, kind_ref, expand_ref, half_ref, out_ref,
    rows, wide, product, half, result, half_sem, out_sem,
):
    @pl.loop(0, 19)
    def _(i):
        pltpu.make_async_copy(half_ref.at[i], half.at[i], half_sem.at[i]).start()

    @pl.loop(0, CAP)
    def _(s):
        b = owned_ref[0, s]

        @pl.when(owned_ref[1, s] != 0)
        def _():
            for i in range(19):
                rows[pl.ds(96 * i + s, 4, stride=24), :] = recv_ref[b // BLK, i, :, :].astype(F32)

    kinds = [kind_ref[8 * g : 8 * g + 8, :] for g in range(3)]
    for q in range(4):
        for i in range(19):
            ones, twos = [], []
            for g in range(3):
                start = 24 * (4 * i + q) + 8 * g
                v = rows[start : start + 8, :]
                ones.append(jnp.where(kinds[g] == 1.0, v, 0.0))
                twos.append(jnp.where(kinds[g] == 2.0, v, 0.0))
            for start, v in ((0, ones), (128, twos)):
                wide[q, 24 * i : 24 * i + 16, start : start + 128] = jnp.concatenate(v[:2], axis=0).astype(BF16)
                wide[q, 24 * i + 16 : 24 * i + 24, start : start + 128] = v[2].astype(BF16)
        product[q, :, :] = jnp.dot(wide[q, :, :], expand_ref[...], preferred_element_type=F32)

    linear = jnp.concatenate([jnp.concatenate([k, k], axis=1) for k in kinds], axis=0) == 2.0
    near = jnp.where(linear, 0.75, 1.0)
    far = jnp.where(linear, 0.25, 0.0)

    @pl.loop(0, 19)
    def _(i):
        pltpu.make_async_copy(half_ref.at[i], half.at[i], half_sem.at[i]).wait()
        start = pl.multiple_of(i * 24, 8)

        def plane(c):
            return product[c // 2, pl.ds(start, 24), (c % 2) * 256 : (c % 2) * 256 + 256]

        for c in range(8):
            mid = plane(c) * near
            for odd in range(2):
                other = max(c - 1, 0) if odd == 0 else min(c + 1, 7)
                x = slice((2 * c + odd) * 256, (2 * c + odd) * 256 + 256)
                result[i, :, x] = (mid + plane(other) * far).astype(BF16) + half[i, :, x]
        pltpu.make_async_copy(result.at[i], out_ref.at[i], out_sem.at[i]).start()

    @pl.loop(0, 19)
    def _(i):
        pltpu.make_async_copy(result.at[i], out_ref.at[i], out_sem.at[i]).wait()


def mean_matrix():
    half = np.zeros((128, 64), np.float32)
    half[np.arange(128), np.arange(128) // 2] = 0.125
    both = np.concatenate([half, half], axis=0)
    none = np.zeros_like(both)
    return np.stack([np.concatenate([both, none], axis=1), np.concatenate([none, both], axis=1)])


def expand_matrix():
    inject = np.zeros((8, 16), np.float32)
    linear = np.zeros((8, 16), np.float32)
    for k in range(8):
        for odd, other in ((0, max(k - 1, 0)), (1, min(k + 1, 7))):
            inject[k, 2 * k + odd] = 1.0
            linear[k, 2 * k + odd] += 0.75
            linear[other, 2 * k + odd] += 0.25
    eye = np.eye(2, dtype=np.float32)
    return np.concatenate([np.kron(eye, np.kron(m, m)) for m in (inject, linear)], axis=0)


def ring(count, step):
    return [(i, (i + step) % count) for i in range(count)]


VM = pl.BlockSpec(memory_space=pltpu.VMEM)
SM = pl.BlockSpec(memory_space=pltpu.SMEM)
ANY = pl.BlockSpec(memory_space=pl.ANY)
HBM = pl.BlockSpec(memory_space=pltpu.HBM)


def struct(shape, dtype):
    return jax.ShapeDtypeStruct(shape, dtype)


def in_hbm(array):
    return pltpu.with_memory_space_constraint(array, pltpu.HBM)


def cost(microseconds):
    return pl.CostEstimate(flops=0, bytes_accessed=int(microseconds * 3.0e6), transcendentals=0)


def limit(mebibytes):
    return pltpu.CompilerParams(vmem_limit_bytes=mebibytes << 20)


def body(populations, levels, refine_flags, new_owner):
    columns = lax.axis_size("yz")
    slabs = lax.axis_size("gx")
    total = new_owner.shape[0]
    devices = slabs * columns

    top = jnp.transpose(populations[:, :, 30:32, :], (0, 2, 1, 3))
    bottom = jnp.transpose(populations[:, :, 0:2, :], (0, 2, 1, 3))
    low = lax.ppermute(top, "yz", ring(columns, 1))
    high = lax.ppermute(bottom, "yz", ring(columns, -1))

    rate = pl.pallas_call(
        rate_kernel,
        out_shape=struct((3, ROWS, 128), F32),
        in_specs=[SM],
        out_specs=VM,
        compiler_params=limit(4),
        cost_estimate=cost(1),
        name="rates",
    )(in_hbm(levels))

    c1 = pl.pallas_call(
        collide_kernel,
        out_shape=struct((19, 16, 32, 128), BF16),
        in_specs=[HBM, VM],
        out_specs=VM,
        scratch_shapes=[pltpu.VMEM((19, 16, 32, 128), BF16), pltpu.SemaphoreType.DMA((4,))],
        compiler_params=limit(8),
        cost_estimate=cost(5),
        name="collide",
    )(in_hbm(populations), rate)

    cy, rim, right, left = pl.pallas_call(
        face_kernel,
        out_shape=(
            struct((19, 8, 16, 128), BF16),
            struct((19, 4, FROWS, 128), BF16),
            struct((FACES, FROWS, 128), BF16),
            struct((FACES, FROWS, 128), BF16),
        ),
        in_specs=[ANY, VM, VM, VM],
        out_specs=(VM,) * 4,
        scratch_shapes=[
            pltpu.VMEM((19, 4, 32, 128), BF16),
            pltpu.VMEM((19 * 128 + 128, 128), F32),
            pltpu.SemaphoreType.DMA((2,)),
        ],
        compiler_params=limit(8),
        cost_estimate=cost(2),
        name="faces",
    )(c1, low, high, rate)

    from_left = lax.ppermute(right, "gx", ring(slabs, 1))
    from_right = lax.ppermute(left, "gx", ring(slabs, -1))

    reduce = jnp.asarray(mean_matrix(), BF16)
    flag_rows = refine_flags.reshape(total // 128, 128)
    owner_rows = new_owner.reshape(total // 128, 128)
    rest, inner, middle, target = pl.pallas_call(
        inner_kernel,
        out_shape=(
            struct((19, 4 * ROWS, 128), F32),
            struct((6, 608, 256), BF16),
            struct((BLK, 96, 128), F32),
            struct((8, 128), jnp.int32),
        ),
        in_specs=[VM] * 6,
        out_specs=(ANY, VM, VM, VM),
        scratch_shapes=[
            pltpu.VMEM((19, 16 * ROWS, 128), F32),
            pltpu.VMEM((19, 14 * ROWS, 128), F32),
            pltpu.VMEM((2, 608, 128), F32),
            pltpu.VMEM((2, 2, 192, 128), F32),
            pltpu.SemaphoreType.DMA((2,)),
        ],
        compiler_params=limit(22),
        cost_estimate=cost(6),
        name="inner",
    )(c1, cy, rate, reduce, flag_rows, owner_rows)

    outer, send = pl.pallas_call(
        step_kernel,
        out_shape=(struct((2, 608, 256), BF16), pltpu.HBM((devices, 19, 4, 128), BF16)),
        in_specs=[SM, ANY] + [VM] * 7,
        out_specs=(VM, HBM),
        scratch_shapes=[
            pltpu.VMEM((19, 8 * ROWS, 128), F32),
            pltpu.VMEM((19, 8 * ROWS, 128), F32),
            pltpu.VMEM((2, 608, 128), F32),
            pltpu.VMEM((2, 2, 192, 128), F32),
            pltpu.VMEM((BLK, 96, 128), F32),
            pltpu.VMEM((BLK, 19, 4, 128), BF16),
            pltpu.SemaphoreType.DMA,
            pltpu.SemaphoreType.DMA((BLK,)),
        ],
        compiler_params=limit(18),
        cost_estimate=cost(6),
        name="step",
    )(
        target, rest, rim, from_left, from_right, rate, reduce, inner, middle,
    )

    recv = lax.all_to_all(send, ("gx", "yz"), split_axis=0, concat_axis=0, tiled=True)

    owned, kind = pl.pallas_call(
        plan_kernel,
        out_shape=(struct((8, 128), jnp.int32), struct((32, 128), F32)),
        in_specs=[VM, VM, ANY],
        out_specs=(VM, VM),
        scratch_shapes=[pltpu.VMEM((32, 128), F32), pltpu.VMEM((32, 128), F32)],
        compiler_params=limit(4),
        cost_estimate=cost(2),
        name="plan",
    )(refine_flags.reshape(total // 128, 128), new_owner.reshape(total // 128, 128), outer)

    half = pl.pallas_call(
        keep_kernel,
        out_shape=pltpu.HBM((19, CAP, 4096), BF16),
        in_specs=[SM, VM, VM],
        out_specs=VM,
        scratch_shapes=[
            pltpu.VMEM((4, 192, 128), F32),
            pltpu.VMEM((32, (CAP + 1) * 24, 128), F32),
            pltpu.SMEM((BLK,), jnp.int32),
        ],
        compiler_params=limit(20),
        cost_estimate=cost(10),
        name="keep",
    )(owned, inner, outer)

    migrated = pl.pallas_call(
        refine_kernel,
        out_shape=struct((19, CAP, 4096), BF16),
        in_specs=[SM, VM, VM, VM, HBM],
        out_specs=ANY,
        scratch_shapes=[
            pltpu.VMEM((CAP * 76, 128), F32),
            pltpu.VMEM((4, 456, 256), BF16),
            pltpu.VMEM((4, 456, 512), F32),
            pltpu.VMEM((19, CAP, 4096), BF16),
            pltpu.VMEM((19, CAP, 4096), BF16),
            pltpu.SemaphoreType.DMA((19,)),
            pltpu.SemaphoreType.DMA((19,)),
        ],
        compiler_params=limit(18),
        cost_estimate=cost(5),
        name="refine",
    )(owned, recv, kind, jnp.asarray(expand_matrix(), BF16), in_hbm(half))
    return jnp.transpose(migrated, (1, 0, 2))


def solution(mesh):
    placed = (P(None, "gx", "yz", None), P(), P(), P())
    return jax.shard_map(
        body, mesh=mesh, in_specs=placed, out_specs=P(("gx", "yz"), None, None), check_vma=False
    )
```
